256 devices in a mesh: kern: 4 (over z_lo, core), slab: 64 (over z_hi, y, x).
Axes of the slice: x: 4, y: 4, z: 8 (z_hi: 4, z_lo: 2; z = z_hi * 2 + z_lo), core: 2. Of those that a mesh axis runs over, the one named last changes fastest.
Arguments:
- layout: int32 [4096, 4096], P('slab', 'kern'), may hold values 0 or 1
- band_freqs: int32 [128], replicated, may hold values from -256 to 255, as said below
- kernels: float32 [2, 48, 128, 128], P(None, 'kern'), may hold values from -6 to 6
- eigen_values: float32 [48], P('kern'), may hold values from 0.1 to 1
- bake_rates: float32 [5], replicated, may hold values from 0.1 to 0.25
Outputs:
- aerial_image: float32 [4096, 4096], P('slab', 'kern')
- latent_acid: float32 [4096, 4096], P('slab', 'kern')
The draws below stay inside these ranges and needn't reach their ends.
Inputs may be any that keep to these rules, and one draw needn't show every extreme that they name: `band_freqs`: the 128 numbers are distinct; both ends of the range are among them.
All inputs are finite; a program needn't handle non-finite values. No bound on the sum of `layout` on one device may be relied on, other than what follows from the above.
Results may differ from the reference program's by a relative error of at most 0.0017.
Values sent between devices are 32-bit elements; how exact they have to be, the bound alone decides.
No kernel may reach another device: no remote copies, remote signals or barrier semaphores. Data moves between devices by JAX's collectives and lax.ppermute only.
A program may use at most 64 MiB of HBM per device.

```python
import math
import jax
import jax.numpy as jnp
from jax import lax

N = 4096
W = 128
FIELDS = 48
STEPS = 2


def draw_band_freqs(key, part):
    shuffled = jax.random.permutation(key, 4 * W - 2)[:W - 2].astype(jnp.int32) - 2 * W + 1
    ends = jnp.array([-2 * W, 2 * W - 1], dtype=jnp.int32)
    return jnp.concatenate([ends, shuffled]).astype(jnp.int32)


def set_ends(entries, own_key, smallest, largest):
    dims = entries.shape
    spot = [jax.random.randint(jax.random.fold_in(own_key, axis), (), 0, dims[axis]) for axis in range(len(dims))]
    entries = entries.at[tuple(spot)].set(smallest)
    longest = dims.index(max(dims))
    spot[longest] = (spot[longest] + 1) % dims[longest]
    return entries.at[tuple(spot)].set(largest)


def block_scale(key, dims, shards, least, largest):
    level = 1.0
    for dim, blocks in shards:
        steps = jax.random.uniform(jax.random.fold_in(jax.random.fold_in(key, 6), dim), (blocks,), jnp.float32, least / len(shards), largest / len(shards))
        level = level * jnp.repeat(jnp.exp(steps), dims[dim] // blocks).reshape((-1,) + (1,) * (len(dims) - 1 - dim))
    return level


def normal_values(own_key, dims, spread, bound, cuts=(), kind=jnp.bfloat16):
    values = jax.random.normal(own_key, dims, jnp.float32) * spread
    if len(cuts) > 0:
        values = block_scale(own_key, dims, cuts, -0.22, 0.18) * values
    return jnp.clip(values, min=-bound, max=bound).astype(kind)


def setup_inputs(seed: int = 0) -> dict:
    keys = jax.random.split(jax.random.key(seed), 6)
    return {
        "layout": set_ends((jax.random.randint(keys[0], (N, N), 0, 2) < 1).astype(jnp.int32), jax.random.fold_in(keys[0], 1), 0, 1),
        "band_freqs": draw_band_freqs(jax.random.fold_in(keys[5], 71), 0),
        "kernels": normal_values(keys[2], (2, FIELDS, W, W), 1.0, 6.0, ((1, 4),), jnp.float32),
        "eigen_values": jnp.clip(jnp.exp(math.log(1.0) - 2.3025851 * jax.random.uniform(keys[3], (FIELDS,), jnp.float32) ** block_scale(keys[3], (FIELDS,), ((0, 4),), -0.2, 0.2)), 0.1, 1.0),
        "bake_rates": jnp.clip(jnp.exp(jax.random.uniform(keys[4], (5,), jnp.float32, math.log(0.1), math.log(0.25))), 0.1, 0.25),
    }


highest = lax.Precision.HIGHEST


def tables(frequencies, first_index, length):
    positions = first_index + jnp.arange(length, dtype=jnp.int32)
    angles = jnp.mod(positions[:, None] * frequencies[None, :], N).astype(jnp.float32) * (2.0 * math.pi / N)
    return jnp.cos(angles), jnp.sin(angles)


def laplace(field):
    return (jnp.roll(field, 1, 0) + jnp.roll(field, -1, 0) + jnp.roll(field, 1, 1)
            + jnp.roll(field, -1, 1) - 4.0 * field)


def reference(layout, band_freqs, kernels, eigen_values, bake_rates):
    transmit = (2 * layout - 1).astype(jnp.float32)
    cos_all, sin_all = tables(band_freqs, 0, N)
    along_re = jnp.dot(transmit, cos_all, precision=highest)
    along_im = -jnp.dot(transmit, sin_all, precision=highest)
    spec_re = (jnp.dot(cos_all.T, along_re, precision=highest) + jnp.dot(sin_all.T, along_im, precision=highest)) / N
    spec_im = (jnp.dot(cos_all.T, along_im, precision=highest) - jnp.dot(sin_all.T, along_re, precision=highest)) / N
    row_table = jnp.concatenate([cos_all, sin_all], 1).astype(jnp.bfloat16).astype(jnp.float32)
    col_table = jnp.concatenate([jnp.concatenate([cos_all.T, sin_all.T], 1),
                                 jnp.concatenate([-sin_all.T, cos_all.T], 1)], 0)
    col_table = col_table.astype(jnp.bfloat16).astype(jnp.float32)

    def one_field(total_sum, field_item):
        kern_re, kern_im, eigen_one = field_item
        prod_re = spec_re * kern_re - spec_im * kern_im
        prod_im = spec_re * kern_im + spec_im * kern_re
        spectral_block = jnp.concatenate([jnp.concatenate([prod_re, prod_im], 1),
                                          jnp.concatenate([-prod_im, prod_re], 1)], 0)
        spectral_block = spectral_block.astype(jnp.bfloat16).astype(jnp.float32)
        row_field = (jnp.dot(row_table, spectral_block, preferred_element_type=jnp.float32) / W)
        row_field = row_field.astype(jnp.bfloat16).astype(jnp.float32)
        field_pair = jnp.dot(row_field, col_table, preferred_element_type=jnp.float32)
        power = field_pair[:, :N] * field_pair[:, :N] + field_pair[:, N:] * field_pair[:, N:]
        return total_sum + eigen_one * power, None

    total_sum, unused = lax.scan(one_field, jnp.zeros((N, N), jnp.float32),
                                 (kernels[0], kernels[1], eigen_values))
    aerial_image = total_sum / FIELDS
    dill_rate, acid_rate, quench_rate, react_rate, quench_start = (bake_rates[0], bake_rates[1], bake_rates[2], bake_rates[3], bake_rates[4])
    acid_field = 1.0 - jnp.exp(-4.0 * dill_rate * aerial_image)
    acid_diffusion = acid_rate * (0.5 + 0.5 * acid_field)
    quencher = jnp.zeros_like(acid_field) + quench_start
    for bake_step in range(STEPS):
        reaction = 4.0 * react_rate * acid_field * quencher
        new_acid = acid_field + acid_diffusion * laplace(acid_field) - reaction
        quencher = quencher + quench_rate * laplace(quencher) - reaction
        acid_field = new_acid
    return aerial_image, acid_field
```

```python
import math

import jax
import jax.numpy as jnp
from jax import lax
from jax.experimental import pallas as pl
from jax.experimental.pallas import tpu as pltpu
from jax.sharding import PartitionSpec as P

N = 4096
W = 128
FIELDS = 48
STEPS = 2

ROWS = 64
COLS = 1024
RING_ROWS = 72
MXU_ROWS = 80
RING_COLS = 1152
WIDE = 2304
ALL = ("kern", "slab")
CHIP_Z, CORES, FAR_Z, SIDE = 2, 2, 4, 4


def device(z_lo, core, z_hi, y, x):
    return (z_lo * CORES + core) * 64 + (z_hi * SIDE + y) * SIDE + x


def column_groups():
    return [
        [device(a, b, c, y, x) for a in range(CHIP_Z) for b in range(CORES) for c in range(FAR_Z)]
        for y in range(SIDE)
        for x in range(SIDE)
    ]


def plane_groups():
    return [
        [device(a, b, c, y, x) for y in range(SIDE) for x in range(SIDE)]
        for a in range(CHIP_Z)
        for b in range(CORES)
        for c in range(FAR_Z)
    ]


def cos_sin(turns):
    m = jnp.bitwise_and(turns, N - 1)
    quarter = jnp.right_shift(m + N // 8, 10)
    t = (m - jnp.left_shift(quarter, 10)).astype(jnp.float32) * (2.0 * math.pi / N)
    t2 = t * t
    s = t * (1.0 + t2 * (-1.0 / 6 + t2 * (1.0 / 120 + t2 * (-1.0 / 5040 + t2 * (1.0 / 362880)))))
    c = 1.0 + t2 * (-0.5 + t2 * (1.0 / 24 + t2 * (-1.0 / 720 + t2 * (1.0 / 40320))))
    odd = jnp.bitwise_and(quarter, 1) == 1
    cos = jnp.where(odd, s, c)
    sin = jnp.where(odd, c, s)
    cos = jnp.where(jnp.bitwise_and(quarter + 1, 2) == 2, -cos, cos)
    sin = jnp.where(jnp.bitwise_and(quarter, 2) == 2, -sin, sin)
    return cos, sin


def split(values):
    high = values.astype(jnp.bfloat16)
    return high, (values - high.astype(jnp.float32)).astype(jnp.bfloat16)


def iota(shape, dim):
    return lax.broadcasted_iota(jnp.int32, shape, dim)


def transform_kernel(layout_ref, freqs_ref, out_ref, table):
    row_first = lax.axis_index("slab") * ROWS
    col_first = lax.axis_index("kern") * COLS
    freqs = freqs_ref[...]
    step = 32
    base_cos, base_sin = cos_sin((col_first + iota((step, W), 0)) * freqs)
    turn_cos, turn_sin = cos_sin((step * iota((COLS // step, W), 0)) * freqs)
    for a in range(COLS // step):
        ca, sa = turn_cos[a : a + 1, :], turn_sin[a : a + 1, :]
        cos = ca * base_cos - sa * base_sin
        sin = sa * base_cos + ca * base_sin
        cos_high, cos_low = split(cos)
        sin_high, sin_low = split(sin)
        at = pl.ds(a * step, step)
        table[at, 0:W] = cos_high
        table[at, W : 2 * W] = sin_high
        table[at, 2 * W : 3 * W] = cos_low
        table[at, 3 * W : 4 * W] = sin_low
    transmit = (2 * layout_ref[...] - 1).astype(jnp.float32).astype(jnp.bfloat16)
    along = jnp.dot(transmit, table[...], preferred_element_type=jnp.float32)
    along_re = along[:, 0:W] + along[:, 2 * W : 3 * W]
    along_im = -(along[:, W : 2 * W] + along[:, 3 * W : 4 * W])
    cos_row, sin_row = cos_sin((row_first + iota((ROWS, W), 0)) * freqs)
    left_high, left_low = split(jnp.concatenate([cos_row, sin_row], 0))
    right = jnp.concatenate(
        [
            jnp.concatenate([along_re, along_im], 1),
            jnp.concatenate([along_im, -along_re], 1),
        ],
        0,
    )
    right_high, right_low = split(right)
    both = lax.dot_general(
        jnp.concatenate([left_high, left_high, left_low], 0),
        jnp.concatenate([right_high, right_low, right_high], 0),
        (((0,), (0,)), ((), ())),
        preferred_element_type=jnp.float32,
    ) * (1.0 / N)
    out_ref[0:W, :] = both[:, 0:W]
    out_ref[W : 2 * W, :] = both[:, W : 2 * W]


def image_kernel(
    spec_ref, near_ref, far_ref, near_eigen, far_eigen, freqs_ref, freqs_col_ref,
    send_ref, keep_ref, table_re, table_im, fields, image,
):
    row_first = lax.axis_index("slab") * ROWS
    kern = lax.axis_index("kern")
    core = lax.rem(kern, CORES)
    wide_first = (kern - core) * COLS - 128

    freqs_col = jnp.broadcast_to(freqs_col_ref[...], (W, 128))
    cos, sin = cos_sin((wide_first + iota((W, 128), 1)) * freqs_col)
    turn_cos, turn_sin = cos_sin(128 * freqs_col)
    for tile in range(WIDE // 128):
        at = pl.ds(tile * 128, 128)
        table_re[0:W, at] = cos.astype(jnp.bfloat16)
        table_re[W : 2 * W, at] = (-sin).astype(jnp.bfloat16)
        table_im[0:W, at] = sin.astype(jnp.bfloat16)
        table_im[W : 2 * W, at] = cos.astype(jnp.bfloat16)
        cos, sin = cos * turn_cos - sin * turn_sin, sin * turn_cos + cos * turn_sin

    place = iota((MXU_ROWS, W), 0)
    place = jnp.where(place < ROWS + 4, place, place - RING_ROWS)
    cos_row, sin_row = cos_sin((row_first + place) * freqs_ref[...])
    row_table = jnp.concatenate([cos_row, sin_row], 1).astype(jnp.bfloat16)

    spec_re = spec_ref[0:W, :]
    spec_im = spec_ref[W : 2 * W, :]
    own = near_ref.shape[1]
    for kernels_ref, first in ((near_ref, 0), (far_ref, own)):

        def one_row_field(f, carry, kernels_ref=kernels_ref, first=first):
            kern_re = kernels_ref[0, f]
            kern_im = kernels_ref[1, f]
            prod_re = spec_re * kern_re - spec_im * kern_im
            prod_im = spec_re * kern_im + spec_im * kern_re
            re16 = prod_re.astype(jnp.bfloat16)
            im16 = prod_im.astype(jnp.bfloat16)
            block = jnp.concatenate(
                [
                    jnp.concatenate([re16, im16], 1),
                    jnp.concatenate([-im16, re16], 1),
                ],
                0,
            )
            row_field = jnp.dot(row_table, block, preferred_element_type=jnp.float32) / W
            at = pl.multiple_of((first + f) * MXU_ROWS, MXU_ROWS)
            fields[pl.ds(at, MXU_ROWS), :] = row_field.astype(jnp.bfloat16)
            return carry

        lax.fori_loop(0, own, one_row_field, 0, unroll=2)

    def one_pair(p, carry):
        at = pl.ds(pl.multiple_of(p * 256, 256), 256)
        rows = fields[...]
        real = jnp.dot(rows, table_re[:, at], preferred_element_type=jnp.float32)
        imag = jnp.dot(rows, table_im[:, at], preferred_element_type=jnp.float32)
        total = jnp.zeros((RING_ROWS, 256), jnp.float32)
        for f in range(2 * own):
            eigen = near_eigen[f] if f < own else far_eigen[f - own]
            re = real[f * MXU_ROWS : f * MXU_ROWS + RING_ROWS]
            im = imag[f * MXU_ROWS : f * MXU_ROWS + RING_ROWS]
            total = total + eigen * (re * re + im * im)
        image[:, at] = total
        return carry

    lax.fori_loop(0, WIDE // 256, one_pair, 0)

    for ref, which in ((keep_ref, core), (send_ref, 1 - core)):
        start = which * COLS
        before = image[:, pl.ds(pl.multiple_of(start, 128), 128)]
        after = image[:, pl.ds(pl.multiple_of(start + 128 + COLS, 128), 128)]
        ref[:, 0:COLS] = image[:, pl.ds(pl.multiple_of(start + 128, 128), COLS)]
        ref[:, COLS:RING_COLS] = jnp.where(iota((RING_ROWS, 128), 1) < 64, after, before)


def laplace(field):
    rows, cols = field.shape
    return (
        pltpu.roll(field, 1, 0)
        + pltpu.roll(field, rows - 1, 0)
        + pltpu.roll(field, 1, 1)
        + pltpu.roll(field, cols - 1, 1)
        - 4.0 * field
    )


def bake_kernel(keep_ref, got_ref, rates, image_ref, acid_ref):
    dill_rate, acid_rate, quench_rate, react_rate, quench_start = (rates[i] for i in range(5))
    aerial_image = (keep_ref[...] + got_ref[...]) / FIELDS
    image_ref[...] = aerial_image[0:ROWS, 0:COLS]
    acid_field = 1.0 - jnp.exp((-4.0 * dill_rate) * aerial_image)
    acid_diffusion = acid_rate * (0.5 + 0.5 * acid_field)
    quencher = jnp.zeros_like(acid_field) + quench_start
    for bake_step in range(STEPS):
        reaction = (4.0 * react_rate) * acid_field * quencher
        new_acid = acid_field + acid_diffusion * laplace(acid_field) - reaction
        quencher = quencher + quench_rate * laplace(quencher) - reaction
        acid_field = new_acid
    acid_ref[...] = acid_field[0:ROWS, 0:COLS]


VMEM = pl.BlockSpec(memory_space=pltpu.VMEM)
SMEM = pl.BlockSpec(memory_space=pltpu.SMEM)


def sum_everywhere(part):
    ring, plane = column_groups(), plane_groups()
    count = len(ring[0])
    piece = part.shape[0] // count

    def exchange(blocks, groups):
        return lax.all_to_all(blocks, ALL, 0, 0, tiled=True, axis_index_groups=groups)

    def total(blocks):
        return jnp.sum(blocks.reshape(-1, piece, part.shape[1]), 0)

    def copies(block, many):
        return jnp.broadcast_to(block[None], (many,) + block.shape).reshape(-1, block.shape[1])

    some = total(exchange(part, ring))
    full = total(exchange(copies(some, len(plane[0])), plane))
    return exchange(copies(full, count), ring)


def shards(layout, band_freqs, kernels, eigen_values, bake_rates):
    freqs = band_freqs.reshape(1, W)
    freqs_col = band_freqs.reshape(W, 1)
    f32 = jnp.float32
    across_z = [(i, (i + 128) % 256) for i in range(256)]
    far_kernels = lax.ppermute(kernels, ALL, across_z)
    far_eigen = lax.ppermute(eigen_values, ALL, across_z)
    part = pl.pallas_call(
        transform_kernel,
        out_shape=jax.ShapeDtypeStruct((2 * W, W), f32),
        in_specs=[VMEM, VMEM],
        out_specs=VMEM,
        scratch_shapes=[pltpu.VMEM((COLS, 4 * W), jnp.bfloat16)],
        name="transform",
    )(layout, freqs)
    spectrum = sum_everywhere(part)
    half = jax.ShapeDtypeStruct((RING_ROWS, RING_COLS), f32)
    own = kernels.shape[1]
    send, keep = pl.pallas_call(
        image_kernel,
        out_shape=(half, half),
        in_specs=[VMEM, VMEM, VMEM, SMEM, SMEM, VMEM, VMEM],
        out_specs=(VMEM, VMEM),
        scratch_shapes=[
            pltpu.VMEM((2 * W, WIDE), jnp.bfloat16),
            pltpu.VMEM((2 * W, WIDE), jnp.bfloat16),
            pltpu.VMEM((2 * own * MXU_ROWS, 2 * W), jnp.bfloat16),
            pltpu.VMEM((RING_ROWS, WIDE), f32),
        ],
        name="image",
    )(spectrum, kernels, far_kernels, eigen_values, far_eigen, freqs, freqs_col)
    across_cores = [(i, i + 64 if (i // 64) % 2 == 0 else i - 64) for i in range(256)]
    got = lax.ppermute(send, ALL, across_cores)
    block = jax.ShapeDtypeStruct((ROWS, COLS), f32)
    return pl.pallas_call(
        bake_kernel,
        out_shape=(block, block),
        in_specs=[VMEM, VMEM, SMEM],
        out_specs=(VMEM, VMEM),
        name="bake",
    )(keep, got, bake_rates)


def solution(mesh):
    return jax.shard_map(
        shards,
        mesh=mesh,
        in_specs=(P("slab", "kern"), P(), P(None, "kern", None, None), P("kern"), P()),
        out_specs=(P("slab", "kern"), P("slab", "kern")),
        check_vma=False,
    )
```

```python
import math

import jax
import jax.numpy as jnp
import ml_dtypes
import numpy as np
from jax import lax
from jax.experimental import pallas as pl
from jax.experimental.pallas import tpu as pltpu
from jax.sharding import PartitionSpec as P

N = 4096
W = 128
FIELDS = 48
STEPS = 2

ROWS = 64
COLS = 1024
RING_ROWS = 72
MXU_ROWS = 80
RING_COLS = 1152
SPARSE = 4
COARSE = N // SPARSE
HALF = COARSE // 2
ALL = ("kern", "slab")
CHIP_Z, CORES, FAR_Z, SIDE = 2, 2, 4, 4


def device(z_lo, core, z_hi, y, x):
    return (z_lo * CORES + core) * 64 + (z_hi * SIDE + y) * SIDE + x


def column_groups():
    return [
        [device(a, b, c, y, x) for a in range(CHIP_Z) for b in range(CORES) for c in range(FAR_Z)]
        for y in range(SIDE)
        for x in range(SIDE)
    ]


def plane_groups():
    return [
        [device(a, b, c, y, x) for y in range(SIDE) for x in range(SIDE)]
        for a in range(CHIP_Z)
        for b in range(CORES)
        for c in range(FAR_Z)
    ]


def cos_sin(turns):
    m = jnp.bitwise_and(turns, N - 1)
    quarter = jnp.right_shift(m + N // 8, 10)
    t = (m - jnp.left_shift(quarter, 10)).astype(jnp.float32) * (2.0 * math.pi / N)
    t2 = t * t
    s = t * (1.0 + t2 * (-1.0 / 6 + t2 * (1.0 / 120 + t2 * (-1.0 / 5040 + t2 * (1.0 / 362880)))))
    c = 1.0 + t2 * (-0.5 + t2 * (1.0 / 24 + t2 * (-1.0 / 720 + t2 * (1.0 / 40320))))
    odd = jnp.bitwise_and(quarter, 1) == 1
    cos = jnp.where(odd, s, c)
    sin = jnp.where(odd, c, s)
    cos = jnp.where(jnp.bitwise_and(quarter + 1, 2) == 2, -cos, cos)
    sin = jnp.where(jnp.bitwise_and(quarter, 2) == 2, -sin, sin)
    return cos, sin


def split(values):
    high = values.astype(jnp.bfloat16)
    return high, (values - high.astype(jnp.float32)).astype(jnp.bfloat16)


def iota(shape, dim):
    return lax.broadcasted_iota(jnp.int32, shape, dim)


def transform_kernel(layout_ref, freqs_ref, out_ref, table):
    row_first = lax.axis_index("slab") * ROWS
    col_first = lax.axis_index("kern") * COLS
    freqs = freqs_ref[...]
    step = 32
    base_cos, base_sin = cos_sin((col_first + iota((step, W), 0)) * freqs)
    turn_cos, turn_sin = cos_sin((step * iota((COLS // step, W), 0)) * freqs)
    for a in range(COLS // step):
        ca, sa = turn_cos[a : a + 1, :], turn_sin[a : a + 1, :]
        cos = ca * base_cos - sa * base_sin
        sin = sa * base_cos + ca * base_sin
        cos_high, cos_low = split(cos)
        sin_high, sin_low = split(sin)
        at = pl.ds(a * step, step)
        table[at, 0:W] = cos_high
        table[at, W : 2 * W] = sin_high
        table[at, 2 * W : 3 * W] = cos_low
        table[at, 3 * W : 4 * W] = sin_low
    transmit = (2 * layout_ref[...] - 1).astype(jnp.float32).astype(jnp.bfloat16)
    along = jnp.dot(transmit, table[...], preferred_element_type=jnp.float32)
    along_re = along[:, 0:W] + along[:, 2 * W : 3 * W]
    along_im = -(along[:, W : 2 * W] + along[:, 3 * W : 4 * W])
    cos_row, sin_row = cos_sin((row_first + iota((ROWS, W), 0)) * freqs)
    left_high, left_low = split(jnp.concatenate([cos_row, sin_row], 0))
    right = jnp.concatenate(
        [
            jnp.concatenate([along_re, along_im], 1),
            jnp.concatenate([along_im, -along_re], 1),
        ],
        0,
    )
    right_high, right_low = split(right)
    both = lax.dot_general(
        jnp.concatenate([left_high, left_high, left_low], 0),
        jnp.concatenate([right_high, right_low, right_high], 0),
        (((0,), (0,)), ((), ())),
        preferred_element_type=jnp.float32,
    ) * (1.0 / N)
    out_ref[0:W, :] = both[:, 0:W]
    out_ref[W : 2 * W, :] = both[:, W : 2 * W]


def image_kernel(spec_ref, kernels_ref, eigen, freqs_ref, send_ref, keep_ref, table_re, table_im, fields):
    row_first = lax.axis_index("slab") * ROWS
    core = lax.rem(lax.axis_index("kern"), CORES)
    freqs = freqs_ref[...]

    freqs_col = jnp.broadcast_to(freqs, (W, W)).astype(jnp.float32).T.astype(jnp.int32)
    cos, sin = cos_sin((SPARSE * iota((W, 128), 1)) * freqs_col)
    turn_cos, turn_sin = cos_sin((SPARSE * 128) * freqs_col)
    for tile in range(COARSE // 128):
        at = pl.ds(tile * 128, 128)
        table_re[0:W, at] = cos.astype(jnp.bfloat16)
        table_re[W : 2 * W, at] = (-sin).astype(jnp.bfloat16)
        table_im[0:W, at] = sin.astype(jnp.bfloat16)
        table_im[W : 2 * W, at] = cos.astype(jnp.bfloat16)
        cos, sin = cos * turn_cos - sin * turn_sin, sin * turn_cos + cos * turn_sin

    place = iota((MXU_ROWS, W), 0)
    place = jnp.where(place < ROWS + 4, place, place - RING_ROWS)
    cos_row, sin_row = cos_sin((row_first + place) * freqs)
    row_table = jnp.concatenate([cos_row, sin_row], 1).astype(jnp.bfloat16)

    spec_re = spec_ref[0:W, :]
    spec_im = spec_ref[W : 2 * W, :]
    count = kernels_ref.shape[1]
    for f in range(count):
        kern_re = kernels_ref[0, f]
        kern_im = kernels_ref[1, f]
        re16 = (spec_re * kern_re - spec_im * kern_im).astype(jnp.bfloat16)
        im16 = (spec_re * kern_im + spec_im * kern_re).astype(jnp.bfloat16)
        block = jnp.concatenate(
            [jnp.concatenate([re16, im16], 1), jnp.concatenate([-im16, re16], 1)], 0
        )
        row_field = jnp.dot(row_table, block, preferred_element_type=jnp.float32) / W
        fields[f * MXU_ROWS : (f + 1) * MXU_ROWS, :] = row_field.astype(jnp.bfloat16)

    for ref, which in ((send_ref, 1 - core), (keep_ref, core)):
        for p in range(HALF // 256):
            at = pl.ds(pl.multiple_of(which * HALF + p * 256, 256), 256)
            rows = fields[...]
            real = jnp.dot(rows, table_re[:, at], preferred_element_type=jnp.float32)
            imag = jnp.dot(rows, table_im[:, at], preferred_element_type=jnp.float32)
            total = jnp.zeros((RING_ROWS, 256), jnp.float32)
            for f in range(count):
                re = real[f * MXU_ROWS : f * MXU_ROWS + RING_ROWS]
                im = imag[f * MXU_ROWS : f * MXU_ROWS + RING_ROWS]
                total = total + eigen[f] * (re * re + im * im)
            ref[:, p * 256 : (p + 1) * 256] = total


def dirichlet():
    distance = np.mod(np.arange(N)[None, :] - SPARSE * np.arange(32)[:, None], N)
    turn = np.pi * distance / N
    sine = np.where(distance == 0, 1.0, COARSE * np.sin(turn))
    kernel = np.where(distance % SPARSE == 0, distance == 0, np.sin(COARSE * turn) * np.cos(turn) / sine)
    kernel = kernel.astype(np.float32)
    high = kernel.astype(ml_dtypes.bfloat16)
    low = (kernel - high.astype(np.float32)).astype(ml_dtypes.bfloat16)
    return high, low


def laplace(field):
    rows, cols = field.shape
    return (
        pltpu.roll(field, 1, 0)
        + pltpu.roll(field, rows - 1, 0)
        + pltpu.roll(field, 1, 1)
        + pltpu.roll(field, cols - 1, 1)
        - 4.0 * field
    )


def bake_kernel(own_ref, other_ref, high_ref, low_ref, rates, image_ref, acid_ref, parts, ring):
    kern = lax.axis_index("kern")
    core = lax.rem(kern, CORES)
    for ref, which in ((own_ref, core), (other_ref, 1 - core)):
        for p in range(HALF // 256):
            block = jnp.bitwise_and(which * (HALF // 256) + p - kern, COARSE // 256 - 1)
            at = pl.ds(pl.multiple_of(block * 256, 256), 256)
            high, low = split(ref[:, p * 256 : (p + 1) * 256])
            parts[0:RING_ROWS, at] = high
            parts[MXU_ROWS : MXU_ROWS + RING_ROWS, at] = low

    def weights(ref, tiles):
        rows = [
            jnp.concatenate([ref[:, ((t - m) % 32) * 128 : ((t - m) % 32) * 128 + 128] for t in tiles], 1)
            for m in range(COARSE // 32)
        ]
        return jnp.concatenate(rows, 0)

    for p in range(5):
        tiles = (2 * p, 2 * p + 1) if p < 4 else (8, 31)
        wide = jnp.dot(parts[...], weights(high_ref, tiles), preferred_element_type=jnp.float32)
        fine = jnp.dot(parts[0:MXU_ROWS, :], weights(low_ref, tiles), preferred_element_type=jnp.float32)
        value = wide[0:RING_ROWS] + (wide[MXU_ROWS : MXU_ROWS + RING_ROWS] + fine[0:RING_ROWS])
        if p < 4:
            ring[:, p * 256 : (p + 1) * 256] = value
        else:
            side = iota((RING_ROWS, 128), 1) < 64
            ring[:, COLS:RING_COLS] = jnp.where(side, value[:, 0:128], value[:, 128:256])

    dill_rate, acid_rate, quench_rate, react_rate, quench_start = (rates[i] for i in range(5))
    aerial_image = ring[...] / FIELDS
    image_ref[...] = aerial_image[0:ROWS, 0:COLS]
    acid_field = 1.0 - jnp.exp((-4.0 * dill_rate) * aerial_image)
    acid_diffusion = acid_rate * (0.5 + 0.5 * acid_field)
    quencher = jnp.zeros_like(acid_field) + quench_start
    for bake_step in range(STEPS):
        reaction = (4.0 * react_rate) * acid_field * quencher
        new_acid = acid_field + acid_diffusion * laplace(acid_field) - reaction
        quencher = quencher + quench_rate * laplace(quencher) - reaction
        acid_field = new_acid
    acid_ref[...] = acid_field[0:ROWS, 0:COLS]


VMEM = pl.BlockSpec(memory_space=pltpu.VMEM)
SMEM = pl.BlockSpec(memory_space=pltpu.SMEM)


def sum_everywhere(part):
    ring, plane = column_groups(), plane_groups()
    count = len(ring[0])
    piece = part.shape[0] // count

    def exchange(blocks, groups):
        return lax.all_to_all(blocks, ALL, 0, 0, tiled=True, axis_index_groups=groups)

    def total(blocks):
        return jnp.sum(blocks.reshape(-1, piece, part.shape[1]), 0)

    def copies(block, many):
        return jnp.broadcast_to(block[None], (many,) + block.shape).reshape(-1, block.shape[1])

    some = total(exchange(part, ring))
    full = total(exchange(copies(some, len(plane[0])), plane))
    return exchange(copies(full, count), ring)


def shards(layout, band_freqs, kernels, eigen_values, bake_rates):
    freqs = band_freqs.reshape(1, W)
    f32 = jnp.float32
    params = pltpu.CompilerParams(vmem_limit_bytes=24 * 2**20)
    part = pl.pallas_call(
        transform_kernel,
        out_shape=jax.ShapeDtypeStruct((2 * W, W), f32),
        in_specs=[VMEM, VMEM],
        out_specs=VMEM,
        scratch_shapes=[pltpu.VMEM((COLS, 4 * W), jnp.bfloat16)],
        compiler_params=params,
        name="transform",
    )(layout, freqs)
    spectrum = sum_everywhere(part)
    half = jax.ShapeDtypeStruct((RING_ROWS, HALF), f32)
    send, keep = pl.pallas_call(
        image_kernel,
        out_shape=(half, half),
        in_specs=[VMEM, VMEM, SMEM, VMEM],
        out_specs=(VMEM, VMEM),
        scratch_shapes=[
            pltpu.VMEM((2 * W, COARSE), jnp.bfloat16),
            pltpu.VMEM((2 * W, COARSE), jnp.bfloat16),
            pltpu.VMEM((kernels.shape[1] * MXU_ROWS, 2 * W), jnp.bfloat16),
        ],
        compiler_params=params,
        name="image",
    )(spectrum, kernels, eigen_values, freqs)
    across_z = [(i, (i + 128) % 256) for i in range(256)]
    across_cores = [(i, i + 64 if (i // 64) % 2 == 0 else i - 64) for i in range(256)]
    chip = keep + lax.ppermute(send, ALL, across_cores)
    own = chip + lax.ppermute(chip, ALL, across_z)
    other = lax.ppermute(own, ALL, across_cores)
    block = jax.ShapeDtypeStruct((ROWS, COLS), f32)
    high, low = dirichlet()
    return pl.pallas_call(
        bake_kernel,
        out_shape=(block, block),
        in_specs=[VMEM, VMEM, VMEM, VMEM, SMEM],
        out_specs=(VMEM, VMEM),
        scratch_shapes=[
            pltpu.VMEM((2 * MXU_ROWS, COARSE), jnp.bfloat16),
            pltpu.VMEM((RING_ROWS, RING_COLS), f32),
        ],
        compiler_params=params,
        name="bake",
    )(own, other, jnp.asarray(high), jnp.asarray(low), bake_rates)


def solution(mesh):
    return jax.shard_map(
        shards,
        mesh=mesh,
        in_specs=(P("slab", "kern"), P(), P(None, "kern", None, None), P("kern"), P()),
        out_specs=(P("slab", "kern"), P("slab", "kern")),
        check_vma=False,
    )
```

```python
import math

import jax
import jax.numpy as jnp
import ml_dtypes
import numpy as np
from jax import lax
from jax.experimental import pallas as pl
from jax.experimental.pallas import tpu as pltpu
from jax.sharding import PartitionSpec as P

N = 4096
W = 128
FIELDS = 48
STEPS = 2

ROWS = 64
COLS = 1024
RING_ROWS = 72
MXU_ROWS = 80
RING_COLS = 1152
SPARSE = 4
COARSE = N // SPARSE
ALL = ("kern", "slab")
CHIP_Z, CORES, FAR_Z, SIDE = 2, 2, 4, 4


def device(z_lo, core, z_hi, y, x):
    return (z_lo * CORES + core) * 64 + (z_hi * SIDE + y) * SIDE + x


def place(i):
    kern, slab = divmod(i, 64)
    return kern // CORES, kern % CORES, slab // SIDE**2, slab // SIDE % SIDE, slab % SIDE


def groups_along(kept):
    groups = {}
    for i in range(256):
        groups.setdefault(tuple(place(i)[axis] for axis in kept), []).append(i)
    return list(groups.values())


def plane_groups():
    return groups_along((0, 2))


def z_groups():
    return groups_along((1, 3, 4))


def from_next_z():
    pairs = []
    for i in range(256):
        z_lo, core, z_hi, y, x = place(i)
        z = (z_hi * CHIP_Z + z_lo + (1 if z_lo == core else -1)) % (FAR_Z * CHIP_Z)
        pairs.append((device(z % CHIP_Z, core, z // CHIP_Z, y, x), i))
    return pairs


def cos_sin(turns):
    m = jnp.bitwise_and(turns, N - 1)
    quarter = jnp.right_shift(m + N // 8, 10)
    t = (m - jnp.left_shift(quarter, 10)).astype(jnp.float32) * (2.0 * math.pi / N)
    t2 = t * t
    s = t * (1.0 + t2 * (-1.0 / 6 + t2 * (1.0 / 120 + t2 * (-1.0 / 5040 + t2 * (1.0 / 362880)))))
    c = 1.0 + t2 * (-0.5 + t2 * (1.0 / 24 + t2 * (-1.0 / 720 + t2 * (1.0 / 40320))))
    odd = jnp.bitwise_and(quarter, 1) == 1
    cos = jnp.where(odd, s, c)
    sin = jnp.where(odd, c, s)
    cos = jnp.where(jnp.bitwise_and(quarter + 1, 2) == 2, -cos, cos)
    sin = jnp.where(jnp.bitwise_and(quarter, 2) == 2, -sin, sin)
    return cos, sin


def split(values):
    high = values.astype(jnp.bfloat16)
    return high, (values - high.astype(jnp.float32)).astype(jnp.bfloat16)


def iota(shape, dim):
    return lax.broadcasted_iota(jnp.int32, shape, dim)


def image_tables(freqs, row_first, re_ref, im_ref, row_ref):
    row = iota((MXU_ROWS, W), 0)
    row = jnp.where(row < ROWS + 4, row, row - RING_ROWS)
    cos_row, sin_row = cos_sin((row_first + row) * freqs)
    row_ref[:, 0:W] = cos_row.astype(jnp.bfloat16)
    row_ref[:, W : 2 * W] = sin_row.astype(jnp.bfloat16)

    freqs_col = jnp.broadcast_to(freqs, (W, W)).astype(jnp.float32).T.astype(jnp.int32)
    cos, sin = cos_sin((SPARSE * iota((W, 128), 1)) * freqs_col)
    turn_cos, turn_sin = cos_sin((SPARSE * 128) * freqs_col)
    for tile in range(COARSE // 128):
        at = slice(tile * 128, tile * 128 + 128)
        re_ref[0:W, at] = cos.astype(jnp.bfloat16)
        re_ref[W : 2 * W, at] = (-sin).astype(jnp.bfloat16)
        im_ref[0:W, at] = sin.astype(jnp.bfloat16)
        im_ref[W : 2 * W, at] = cos.astype(jnp.bfloat16)
        cos, sin = cos * turn_cos - sin * turn_sin, sin * turn_cos + cos * turn_sin


def transform_kernel(
    layout_hbm, freqs_hbm, eigen_hbm, out_ref, re_ref, im_ref, row_ref, eigen_ref, table, layout_ref, freqs_ref, sems
):
    freqs_copy = pltpu.make_async_copy(freqs_hbm, freqs_ref, sems.at[0])
    layout_copy = pltpu.make_async_copy(layout_hbm, layout_ref, sems.at[1])
    eigen_copy = pltpu.make_async_copy(eigen_hbm, eigen_ref, sems.at[2])
    freqs_copy.start()
    layout_copy.start()
    eigen_copy.start()
    row_first = lax.axis_index("slab") * ROWS
    col_first = lax.axis_index("kern") * COLS
    freqs_copy.wait()
    freqs = freqs_ref[...]
    step = 32
    base_cos, base_sin = cos_sin((col_first + iota((step, W), 0)) * freqs)
    turn_cos, turn_sin = cos_sin((step * iota((COLS // step, W), 0)) * freqs)
    for a in range(COLS // step):
        ca, sa = turn_cos[a : a + 1, :], turn_sin[a : a + 1, :]
        cos = ca * base_cos - sa * base_sin
        sin = sa * base_cos + ca * base_sin
        cos_high, cos_low = split(cos)
        sin_high, sin_low = split(sin)
        at = pl.ds(a * step, step)
        table[at, 0:W] = cos_high
        table[at, W : 2 * W] = sin_high
        table[at, 2 * W : 3 * W] = cos_low
        table[at, 3 * W : 4 * W] = sin_low
    cos_row, sin_row = cos_sin((row_first + iota((ROWS, W), 0)) * freqs)
    left_high, left_low = split(jnp.concatenate([cos_row, sin_row], 0))
    image_tables(freqs, row_first, re_ref, im_ref, row_ref)
    layout_copy.wait()
    eigen_copy.wait()
    transmit = (2 * layout_ref[...] - 1).astype(jnp.float32).astype(jnp.bfloat16)
    along = jnp.dot(transmit, table[...], preferred_element_type=jnp.float32)
    along_re = along[:, 0:W] + along[:, 2 * W : 3 * W]
    along_im = -(along[:, W : 2 * W] + along[:, 3 * W : 4 * W])
    right = jnp.concatenate(
        [
            jnp.concatenate([along_re, along_im], 1),
            jnp.concatenate([along_im, -along_re], 1),
        ],
        0,
    )
    right_high, right_low = split(right)
    both = lax.dot_general(
        jnp.concatenate([left_high, left_high, left_low], 0),
        jnp.concatenate([right_high, right_low, right_high], 0),
        (((0,), (0,)), ((), ())),
        preferred_element_type=jnp.float32,
    ) * (1.0 / N)
    out_ref[0:W, :] = both[:, 0:W]
    out_ref[W : 2 * W, :] = both[:, W : 2 * W]


def image_kernel(
    spec_ref, near_hbm, far_ref, table_re, table_im, row_ref, near_eigen, far_eigen, image_ref, fields, near_ref, sem
):
    near_copy = pltpu.make_async_copy(near_hbm, near_ref, sem)
    near_copy.start()
    row_table = row_ref[...]
    spec_re = spec_ref[0:W, :]
    spec_im = spec_ref[W : 2 * W, :]
    own = far_ref.shape[1]

    def row_field(kernels_ref, f):
        kern_re = kernels_ref[0, f]
        kern_im = kernels_ref[1, f]
        re16 = (spec_re * kern_re - spec_im * kern_im).astype(jnp.bfloat16)
        im16 = (spec_re * kern_im + spec_im * kern_re).astype(jnp.bfloat16)
        block = jnp.concatenate(
            [jnp.concatenate([re16, im16], 1), jnp.concatenate([-im16, re16], 1)], 0
        )
        return jnp.dot(row_table, block, preferred_element_type=jnp.float32)[0:RING_ROWS] / W

    for kernels_ref, first in ((far_ref, 0), (near_ref, own)):
        if first:
            near_copy.wait()
        for f in range(0, own, 2):
            both = jnp.concatenate([row_field(kernels_ref, f), row_field(kernels_ref, f + 1)], 0)
            at = (first + f) * RING_ROWS
            fields[at : at + 2 * RING_ROWS, :] = both.astype(jnp.bfloat16)

    eigen = [ref[0:1, f : f + 1] for ref in (far_eigen, near_eigen) for f in range(own)]
    for p in range(COARSE // 256):
        at = slice(p * 256, (p + 1) * 256)
        rows = fields[...]
        real = jnp.dot(rows, table_re[:, at], preferred_element_type=jnp.float32)
        imag = jnp.dot(rows, table_im[:, at], preferred_element_type=jnp.float32)
        total = jnp.zeros((RING_ROWS, 256), jnp.float32)
        for f in range(2 * own):
            re = real[f * RING_ROWS : (f + 1) * RING_ROWS]
            im = imag[f * RING_ROWS : (f + 1) * RING_ROWS]
            total = total + eigen[f] * (re * re + im * im)
        image_ref[:, at] = total


def dirichlet():
    distance = np.mod(np.arange(N)[None, :] - SPARSE * np.arange(32)[:, None], N)
    turn = np.pi * distance / N
    sine = np.where(distance == 0, 1.0, COARSE * np.sin(turn))
    kernel = np.where(distance % SPARSE == 0, distance == 0, np.sin(COARSE * turn) * np.cos(turn) / sine)
    kernel = kernel.astype(np.float32)
    high = kernel.astype(ml_dtypes.bfloat16)
    low = (kernel - high.astype(np.float32)).astype(ml_dtypes.bfloat16)
    return high, low


def laplace(field):
    rows, cols = field.shape
    return (
        pltpu.roll(field, 1, 0)
        + pltpu.roll(field, rows - 1, 0)
        + pltpu.roll(field, 1, 1)
        + pltpu.roll(field, cols - 1, 1)
        - 4.0 * field
    )


def bake_kernel(own_ref, other_ref, high_ref, low_ref, rates, image_ref, acid_ref, parts, ring):
    kern = lax.axis_index("kern")
    for p in range(COARSE // 256):
        block = jnp.bitwise_and(p - kern, COARSE // 256 - 1)
        at = pl.ds(pl.multiple_of(block * 256, 256), 256)
        high, low = split(own_ref[:, p * 256 : (p + 1) * 256] + other_ref[:, p * 256 : (p + 1) * 256])
        parts[0:RING_ROWS, at] = high
        parts[MXU_ROWS : MXU_ROWS + RING_ROWS, at] = low

    def weights(ref, tiles):
        rows = [
            jnp.concatenate([ref[:, ((t - m) % 32) * 128 : ((t - m) % 32) * 128 + 128] for t in tiles], 1)
            for m in range(COARSE // 32)
        ]
        return jnp.concatenate(rows, 0)

    for p in range(5):
        tiles = (2 * p, 2 * p + 1) if p < 4 else (8, 31)
        wide = jnp.dot(parts[...], weights(high_ref, tiles), preferred_element_type=jnp.float32)
        fine = jnp.dot(parts[0:MXU_ROWS, :], weights(low_ref, tiles), preferred_element_type=jnp.float32)
        value = wide[0:RING_ROWS] + (wide[MXU_ROWS : MXU_ROWS + RING_ROWS] + fine[0:RING_ROWS])
        if p < 4:
            ring[:, p * 256 : (p + 1) * 256] = value
        else:
            side = iota((RING_ROWS, 128), 1) < 64
            ring[:, COLS:RING_COLS] = jnp.where(side, value[:, 0:128], value[:, 128:256])

    dill_rate, acid_rate, quench_rate, react_rate, quench_start = (rates[i] for i in range(5))
    aerial_image = ring[...] / FIELDS
    image_ref[...] = aerial_image[0:ROWS, 0:COLS]
    acid_field = 1.0 - jnp.exp((-4.0 * dill_rate) * aerial_image)
    acid_diffusion = acid_rate * (0.5 + 0.5 * acid_field)
    quencher = jnp.zeros_like(acid_field) + quench_start
    for bake_step in range(STEPS):
        reaction = (4.0 * react_rate) * acid_field * quencher
        new_acid = acid_field + acid_diffusion * laplace(acid_field) - reaction
        quencher = quencher + quench_rate * laplace(quencher) - reaction
        acid_field = new_acid
    acid_ref[...] = acid_field[0:ROWS, 0:COLS]


VMEM = pl.BlockSpec(memory_space=pltpu.VMEM)
SMEM = pl.BlockSpec(memory_space=pltpu.SMEM)
HBM = pl.BlockSpec(memory_space=pltpu.HBM)


def in_hbm(array):
    return pltpu.with_memory_space_constraint(array, pltpu.HBM)


def sum_everywhere(part):
    plane, along_z = plane_groups(), z_groups()
    count = len(plane[0])
    piece = part.shape[0] // count

    def exchange(blocks, groups):
        return lax.all_to_all(blocks, ALL, 0, 0, tiled=True, axis_index_groups=groups)

    def total(blocks):
        return jnp.sum(blocks.reshape(-1, piece, part.shape[1]), 0)

    def copies(block, many):
        return jnp.broadcast_to(block[None], (many,) + block.shape).reshape(-1, block.shape[1])

    some = total(exchange(part, plane))
    full = total(exchange(copies(some, len(along_z[0])), along_z))
    return exchange(copies(full, count), plane)


def shards(layout, band_freqs, kernels, eigen_values, bake_rates):
    freqs = band_freqs.reshape(1, W)
    f32 = jnp.float32
    params = pltpu.CompilerParams(vmem_limit_bytes=24 * 2**20)
    far_kernels = lax.ppermute(kernels, ALL, from_next_z())
    far_eigen = lax.ppermute(eigen_values, ALL, from_next_z())
    own = kernels.shape[1]
    table = jax.ShapeDtypeStruct((2 * W, COARSE), jnp.bfloat16)
    part, *tables, near_eigen = pl.pallas_call(
        transform_kernel,
        out_shape=(
            jax.ShapeDtypeStruct((2 * W, W), f32),
            table,
            table,
            jax.ShapeDtypeStruct((MXU_ROWS, 2 * W), jnp.bfloat16),
            jax.ShapeDtypeStruct((1, own), f32),
        ),
        in_specs=[HBM, HBM, HBM],
        out_specs=(VMEM,) * 5,
        scratch_shapes=[
            pltpu.VMEM((COLS, 4 * W), jnp.bfloat16),
            pltpu.VMEM((ROWS, COLS), jnp.int32),
            pltpu.VMEM((1, W), jnp.int32),
            pltpu.SemaphoreType.DMA((3,)),
        ],
        compiler_params=params,
        name="transform",
    )(in_hbm(layout), in_hbm(freqs), in_hbm(eigen_values.reshape(1, own)))
    part, far_eigen = lax.optimization_barrier((part, far_eigen))
    spectrum = sum_everywhere(part)
    own_image = pl.pallas_call(
        image_kernel,
        out_shape=jax.ShapeDtypeStruct((RING_ROWS, COARSE), f32),
        in_specs=[VMEM, HBM] + [VMEM] * 6,
        out_specs=VMEM,
        scratch_shapes=[
            pltpu.VMEM((2 * own * RING_ROWS, 2 * W), jnp.bfloat16),
            pltpu.VMEM(kernels.shape, f32),
            pltpu.SemaphoreType.DMA,
        ],
        compiler_params=params,
        name="image",
    )(spectrum, in_hbm(kernels), far_kernels, *tables, near_eigen, far_eigen.reshape(1, own))
    across_cores = [(i, i + 64 if (i // 64) % 2 == 0 else i - 64) for i in range(256)]
    other_image = lax.ppermute(own_image, ALL, across_cores)
    block = jax.ShapeDtypeStruct((ROWS, COLS), f32)
    high, low = dirichlet()
    return pl.pallas_call(
        bake_kernel,
        out_shape=(block, block),
        in_specs=[VMEM, VMEM, VMEM, VMEM, SMEM],
        out_specs=(VMEM, VMEM),
        scratch_shapes=[
            pltpu.VMEM((2 * MXU_ROWS, COARSE), jnp.bfloat16),
            pltpu.VMEM((RING_ROWS, RING_COLS), f32),
        ],
        compiler_params=params,
        name="bake",
    )(own_image, other_image, jnp.asarray(high), jnp.asarray(low), bake_rates)


def solution(mesh):
    return jax.shard_map(
        shards,
        mesh=mesh,
        in_specs=(P("slab", "kern"), P(), P(None, "kern", None, None), P("kern"), P()),
        out_specs=(P("slab", "kern"), P("slab", "kern")),
        check_vma=False,
    )
```

```python
import math

import jax
import jax.numpy as jnp
import ml_dtypes
import numpy as np
from jax import lax
from jax.experimental import pallas as pl
from jax.experimental.pallas import tpu as pltpu
from jax.sharding import PartitionSpec as P

N = 4096
W = 128
FIELDS = 48
STEPS = 2

ROWS = 64
COLS = 1024
RING_ROWS = 72
MXU_ROWS = 80
RING_COLS = 1152
SPARSE = 4
COARSE = N // SPARSE
ALL = ("kern", "slab")
CHIP_Z, CORES, FAR_Z, SIDE = 2, 2, 4, 4


def device(z_lo, core, z_hi, y, x):
    return (z_lo * CORES + core) * 64 + (z_hi * SIDE + y) * SIDE + x


def place(i):
    kern, slab = divmod(i, 64)
    return kern // CORES, kern % CORES, slab // SIDE**2, slab // SIDE % SIDE, slab % SIDE


def groups_along(kept):
    groups = {}
    for i in range(256):
        groups.setdefault(tuple(place(i)[axis] for axis in kept), []).append(i)
    return list(groups.values())


def plane_groups():
    return groups_along((0, 2))


def z_groups():
    return groups_along((1, 3, 4))


def from_next_z(side):
    pairs = []
    for i in range(256):
        z_lo, core, z_hi, y, x = place(i)
        z = (z_hi * CHIP_Z + z_lo + (side if z_lo == core else -side)) % (FAR_Z * CHIP_Z)
        pairs.append((device(z % CHIP_Z, core, z // CHIP_Z, y, x), i))
    return pairs


def cos_sin(turns):
    m = jnp.bitwise_and(turns, N - 1)
    quarter = jnp.right_shift(m + N // 8, 10)
    t = (m - jnp.left_shift(quarter, 10)).astype(jnp.float32) * (2.0 * math.pi / N)
    t2 = t * t
    s = t * (1.0 + t2 * (-1.0 / 6 + t2 * (1.0 / 120 + t2 * (-1.0 / 5040 + t2 * (1.0 / 362880)))))
    c = 1.0 + t2 * (-0.5 + t2 * (1.0 / 24 + t2 * (-1.0 / 720 + t2 * (1.0 / 40320))))
    odd = jnp.bitwise_and(quarter, 1) == 1
    cos = jnp.where(odd, s, c)
    sin = jnp.where(odd, c, s)
    cos = jnp.where(jnp.bitwise_and(quarter + 1, 2) == 2, -cos, cos)
    sin = jnp.where(jnp.bitwise_and(quarter, 2) == 2, -sin, sin)
    return cos, sin


def split(values):
    high = values.astype(jnp.bfloat16)
    return high, (values - high.astype(jnp.float32)).astype(jnp.bfloat16)


def iota(shape, dim):
    return lax.broadcasted_iota(jnp.int32, shape, dim)


def image_tables(freqs, row_first, re_ref, im_ref, row_ref):
    row = iota((MXU_ROWS, W), 0)
    row = jnp.where(row < ROWS + 4, row, row - RING_ROWS)
    cos_row, sin_row = cos_sin((row_first + row) * freqs)
    row_ref[:, 0:W] = cos_row.astype(jnp.bfloat16)
    row_ref[:, W : 2 * W] = sin_row.astype(jnp.bfloat16)

    freqs_col = jnp.broadcast_to(freqs, (W, W)).astype(jnp.float32).T.astype(jnp.int32)
    cos, sin = cos_sin((SPARSE * iota((W, 128), 1)) * freqs_col)
    turn_cos, turn_sin = cos_sin((SPARSE * 128) * freqs_col)
    for tile in range(COARSE // 128):
        at = slice(tile * 128, tile * 128 + 128)
        re_ref[0:W, at] = cos.astype(jnp.bfloat16)
        re_ref[W : 2 * W, at] = (-sin).astype(jnp.bfloat16)
        im_ref[0:W, at] = sin.astype(jnp.bfloat16)
        im_ref[W : 2 * W, at] = cos.astype(jnp.bfloat16)
        cos, sin = cos * turn_cos - sin * turn_sin, sin * turn_cos + cos * turn_sin


def transform_kernel(
    layout_hbm, freqs_hbm, eigen_hbm, out_ref, re_ref, im_ref, row_ref, eigen_ref, table, layout_ref, freqs_ref, sems
):
    freqs_copy = pltpu.make_async_copy(freqs_hbm, freqs_ref, sems.at[0])
    layout_copy = pltpu.make_async_copy(layout_hbm, layout_ref, sems.at[1])
    eigen_copy = pltpu.make_async_copy(eigen_hbm, eigen_ref, sems.at[2])
    freqs_copy.start()
    layout_copy.start()
    eigen_copy.start()
    row_first = lax.axis_index("slab") * ROWS
    col_first = lax.axis_index("kern") * COLS
    freqs_copy.wait()
    freqs = freqs_ref[...]
    step = 32
    base_cos, base_sin = cos_sin((col_first + iota((step, W), 0)) * freqs)
    turn_cos, turn_sin = cos_sin((step * iota((COLS // step, W), 0)) * freqs)
    for a in range(COLS // step):
        ca, sa = turn_cos[a : a + 1, :], turn_sin[a : a + 1, :]
        cos = ca * base_cos - sa * base_sin
        sin = sa * base_cos + ca * base_sin
        cos_high, cos_low = split(cos)
        sin_high, sin_low = split(sin)
        at = pl.ds(a * step, step)
        table[at, 0:W] = cos_high
        table[at, W : 2 * W] = sin_high
        table[at, 2 * W : 3 * W] = cos_low
        table[at, 3 * W : 4 * W] = sin_low
    cos_row, sin_row = cos_sin((row_first + iota((ROWS, W), 0)) * freqs)
    left_high, left_low = split(jnp.concatenate([cos_row, sin_row], 0))
    image_tables(freqs, row_first, re_ref, im_ref, row_ref)
    layout_copy.wait()
    eigen_copy.wait()
    transmit = (2 * layout_ref[...] - 1).astype(jnp.float32).astype(jnp.bfloat16)
    along = jnp.dot(transmit, table[...], preferred_element_type=jnp.float32)
    along_re = along[:, 0:W] + along[:, 2 * W : 3 * W]
    along_im = -(along[:, W : 2 * W] + along[:, 3 * W : 4 * W])
    right = jnp.concatenate(
        [
            jnp.concatenate([along_re, along_im], 1),
            jnp.concatenate([along_im, -along_re], 1),
        ],
        0,
    )
    right_high, right_low = split(right)
    both = lax.dot_general(
        jnp.concatenate([left_high, left_high, left_low], 0),
        jnp.concatenate([right_high, right_low, right_high], 0),
        (((0,), (0,)), ((), ())),
        preferred_element_type=jnp.float32,
    ) * (1.0 / N)
    out_ref[0:W, :] = both[:, 0:W]
    out_ref[W : 2 * W, :] = both[:, W : 2 * W]


def image_kernel(
    spec_ref, near_hbm, far_ref, table_re, table_im, row_ref, near_eigen, far_eigen, image_ref, fields, near_ref, sem
):
    near_copy = pltpu.make_async_copy(near_hbm, near_ref, sem)
    near_copy.start()
    row_table = row_ref[...]
    spec_re = spec_ref[0:W, :]
    spec_im = spec_ref[W : 2 * W, :]
    own = far_ref.shape[1]

    def row_field(kernels_ref, f):
        kern_re = kernels_ref[0, f]
        kern_im = kernels_ref[1, f]
        re16 = (spec_re * kern_re - spec_im * kern_im).astype(jnp.bfloat16)
        im16 = (spec_re * kern_im + spec_im * kern_re).astype(jnp.bfloat16)
        block = jnp.concatenate(
            [jnp.concatenate([re16, im16], 1), jnp.concatenate([-im16, re16], 1)], 0
        )
        return jnp.dot(row_table, block, preferred_element_type=jnp.float32)[0:RING_ROWS] / W

    for kernels_ref, first in ((far_ref, 0), (near_ref, own)):
        if first:
            near_copy.wait()
        for f in range(0, own, 2):
            both = jnp.concatenate([row_field(kernels_ref, f), row_field(kernels_ref, f + 1)], 0)
            at = (first + f) * RING_ROWS
            fields[at : at + 2 * RING_ROWS, :] = both.astype(jnp.bfloat16)

    eigen = [ref[0:1, f : f + 1] for ref in (far_eigen, near_eigen) for f in range(own)]
    for p in range(COARSE // 256):
        at = slice(p * 256, (p + 1) * 256)
        rows = fields[...]
        real = jnp.dot(rows, table_re[:, at], preferred_element_type=jnp.float32)
        imag = jnp.dot(rows, table_im[:, at], preferred_element_type=jnp.float32)
        total = jnp.zeros((RING_ROWS, 256), jnp.float32)
        for f in range(2 * own):
            re = real[f * RING_ROWS : (f + 1) * RING_ROWS]
            im = imag[f * RING_ROWS : (f + 1) * RING_ROWS]
            total = total + eigen[f] * (re * re + im * im)
        image_ref[:, at] = total


def dirichlet():
    distance = np.mod(np.arange(N)[None, :] - SPARSE * np.arange(32)[:, None], N)
    turn = np.pi * distance / N
    sine = np.where(distance == 0, 1.0, COARSE * np.sin(turn))
    kernel = np.where(distance % SPARSE == 0, distance == 0, np.sin(COARSE * turn) * np.cos(turn) / sine)
    kernel = kernel.astype(np.float32)
    high = kernel.astype(ml_dtypes.bfloat16)
    low = (kernel - high.astype(np.float32)).astype(ml_dtypes.bfloat16)
    return high, low


def laplace(field):
    rows, cols = field.shape
    return (
        pltpu.roll(field, 1, 0)
        + pltpu.roll(field, rows - 1, 0)
        + pltpu.roll(field, 1, 1)
        + pltpu.roll(field, cols - 1, 1)
        - 4.0 * field
    )


def bake_kernel(own_ref, other_ref, high_ref, low_ref, rates, image_ref, acid_ref, parts, ring):
    kern = lax.axis_index("kern")
    for p in range(COARSE // 256):
        block = jnp.bitwise_and(p - kern, COARSE // 256 - 1)
        at = pl.ds(pl.multiple_of(block * 256, 256), 256)
        high, low = split(own_ref[:, p * 256 : (p + 1) * 256] + other_ref[:, p * 256 : (p + 1) * 256])
        parts[0:RING_ROWS, at] = high
        parts[MXU_ROWS : MXU_ROWS + RING_ROWS, at] = low

    def weights(ref, tiles):
        rows = [
            jnp.concatenate([ref[:, ((t - m) % 32) * 128 : ((t - m) % 32) * 128 + 128] for t in tiles], 1)
            for m in range(COARSE // 32)
        ]
        return jnp.concatenate(rows, 0)

    for p in range(5):
        tiles = (2 * p, 2 * p + 1) if p < 4 else (8, 31)
        wide = jnp.dot(parts[...], weights(high_ref, tiles), preferred_element_type=jnp.float32)
        fine = jnp.dot(parts[0:MXU_ROWS, :], weights(low_ref, tiles), preferred_element_type=jnp.float32)
        value = wide[0:RING_ROWS] + (wide[MXU_ROWS : MXU_ROWS + RING_ROWS] + fine[0:RING_ROWS])
        if p < 4:
            ring[:, p * 256 : (p + 1) * 256] = value
        else:
            side = iota((RING_ROWS, 128), 1) < 64
            ring[:, COLS:RING_COLS] = jnp.where(side, value[:, 0:128], value[:, 128:256])

    dill_rate, acid_rate, quench_rate, react_rate, quench_start = (rates[i] for i in range(5))
    aerial_image = ring[...] / FIELDS
    image_ref[...] = aerial_image[0:ROWS, 0:COLS]
    acid_field = 1.0 - jnp.exp((-4.0 * dill_rate) * aerial_image)
    acid_diffusion = acid_rate * (0.5 + 0.5 * acid_field)
    quencher = jnp.zeros_like(acid_field) + quench_start
    for bake_step in range(STEPS):
        reaction = (4.0 * react_rate) * acid_field * quencher
        new_acid = acid_field + acid_diffusion * laplace(acid_field) - reaction
        quencher = quencher + quench_rate * laplace(quencher) - reaction
        acid_field = new_acid
    acid_ref[...] = acid_field[0:ROWS, 0:COLS]


VMEM = pl.BlockSpec(memory_space=pltpu.VMEM)
SMEM = pl.BlockSpec(memory_space=pltpu.SMEM)
HBM = pl.BlockSpec(memory_space=pltpu.HBM)


def in_hbm(array):
    return pltpu.with_memory_space_constraint(array, pltpu.HBM)


def sum_everywhere(part):
    plane, along_z = plane_groups(), z_groups()
    count = len(plane[0])
    piece = part.shape[0] // count

    def exchange(blocks, groups):
        return lax.all_to_all(blocks, ALL, 0, 0, tiled=True, axis_index_groups=groups)

    def total(blocks):
        return jnp.sum(blocks.reshape(-1, piece, part.shape[1]), 0)

    def copies(block, many):
        return jnp.broadcast_to(block[None], (many,) + block.shape).reshape(-1, block.shape[1])

    some = total(exchange(part, plane))
    full = total(exchange(copies(some, len(along_z[0])), along_z))
    return exchange(copies(full, count), plane)


def shards(layout, band_freqs, kernels, eigen_values, bake_rates):
    freqs = band_freqs.reshape(1, W)
    f32 = jnp.float32
    params = pltpu.CompilerParams(vmem_limit_bytes=24 * 2**20)
    far_kernels = lax.ppermute(kernels, ALL, from_next_z(1))
    far_eigen = lax.ppermute(eigen_values, ALL, from_next_z(-1))
    own = kernels.shape[1]
    table = jax.ShapeDtypeStruct((2 * W, COARSE), jnp.bfloat16)
    part, *tables, near_eigen = pl.pallas_call(
        transform_kernel,
        out_shape=(
            jax.ShapeDtypeStruct((2 * W, W), f32),
            table,
            table,
            jax.ShapeDtypeStruct((MXU_ROWS, 2 * W), jnp.bfloat16),
            jax.ShapeDtypeStruct((1, own), f32),
        ),
        in_specs=[HBM, HBM, HBM],
        out_specs=(VMEM,) * 5,
        scratch_shapes=[
            pltpu.VMEM((COLS, 4 * W), jnp.bfloat16),
            pltpu.VMEM((ROWS, COLS), jnp.int32),
            pltpu.VMEM((1, W), jnp.int32),
            pltpu.SemaphoreType.DMA((3,)),
        ],
        compiler_params=params,
        name="transform",
    )(in_hbm(layout), in_hbm(freqs), in_hbm(eigen_values.reshape(1, own)))
    part, far_eigen = lax.optimization_barrier((part, far_eigen))
    spectrum = sum_everywhere(part)
    own_image = pl.pallas_call(
        image_kernel,
        out_shape=jax.ShapeDtypeStruct((RING_ROWS, COARSE), f32),
        in_specs=[VMEM, HBM] + [VMEM] * 6,
        out_specs=VMEM,
        scratch_shapes=[
            pltpu.VMEM((2 * own * RING_ROWS, 2 * W), jnp.bfloat16),
            pltpu.VMEM(kernels.shape, f32),
            pltpu.SemaphoreType.DMA,
        ],
        compiler_params=params,
        name="image",
    )(spectrum, in_hbm(kernels), far_kernels, *tables, near_eigen, far_eigen.reshape(1, own))
    across_cores = [(i, i + 64 if (i // 64) % 2 == 0 else i - 64) for i in range(256)]
    other_image = lax.ppermute(own_image, ALL, across_cores)
    block = jax.ShapeDtypeStruct((ROWS, COLS), f32)
    high, low = dirichlet()
    return pl.pallas_call(
        bake_kernel,
        out_shape=(block, block),
        in_specs=[VMEM, VMEM, VMEM, VMEM, SMEM],
        out_specs=(VMEM, VMEM),
        scratch_shapes=[
            pltpu.VMEM((2 * MXU_ROWS, COARSE), jnp.bfloat16),
            pltpu.VMEM((RING_ROWS, RING_COLS), f32),
        ],
        compiler_params=params,
        name="bake",
    )(own_image, other_image, jnp.asarray(high), jnp.asarray(low), bake_rates)


def solution(mesh):
    return jax.shard_map(
        shards,
        mesh=mesh,
        in_specs=(P("slab", "kern"), P(), P(None, "kern", None, None), P("kern"), P()),
        out_specs=(P("slab", "kern"), P("slab", "kern")),
        check_vma=False,
    )
```

```python
import math

import jax
import jax.numpy as jnp
import ml_dtypes
import numpy as np
from jax import lax
from jax.experimental import pallas as pl
from jax.experimental.pallas import tpu as pltpu
from jax.sharding import PartitionSpec as P

N = 4096
W = 128
FIELDS = 48
STEPS = 2

ROWS = 64
COLS = 1024
RING_ROWS = 72
MXU_ROWS = 80
RING_COLS = 1152
SPARSE = 4
COARSE = N // SPARSE
ALL = ("kern", "slab")
CHIP_Z, CORES, FAR_Z, SIDE = 2, 2, 4, 4


def device(z_lo, core, z_hi, y, x):
    return (z_lo * CORES + core) * 64 + (z_hi * SIDE + y) * SIDE + x


def place(i):
    kern, slab = divmod(i, 64)
    return kern // CORES, kern % CORES, slab // SIDE**2, slab // SIDE % SIDE, slab % SIDE


def groups_along(kept):
    groups = {}
    for i in range(256):
        groups.setdefault(tuple(place(i)[axis] for axis in kept), []).append(i)
    return list(groups.values())


def plane_groups():
    return groups_along((0, 2))


def z_groups():
    return groups_along((1, 3, 4))


def from_next_z(side):
    pairs = []
    for i in range(256):
        z_lo, core, z_hi, y, x = place(i)
        z = (z_hi * CHIP_Z + z_lo + (side if z_lo == core else -side)) % (FAR_Z * CHIP_Z)
        pairs.append((device(z % CHIP_Z, core, z // CHIP_Z, y, x), i))
    return pairs


def cos_sin(turns):
    m = jnp.bitwise_and(turns, N - 1)
    quarter = jnp.right_shift(m + N // 8, 10)
    t = (m - jnp.left_shift(quarter, 10)).astype(jnp.float32) * (2.0 * math.pi / N)
    t2 = t * t
    s = t * (1.0 + t2 * (-1.0 / 6 + t2 * (1.0 / 120 + t2 * (-1.0 / 5040 + t2 * (1.0 / 362880)))))
    c = 1.0 + t2 * (-0.5 + t2 * (1.0 / 24 + t2 * (-1.0 / 720 + t2 * (1.0 / 40320))))
    odd = jnp.bitwise_and(quarter, 1) == 1
    cos = jnp.where(odd, s, c)
    sin = jnp.where(odd, c, s)
    cos = jnp.where(jnp.bitwise_and(quarter + 1, 2) == 2, -cos, cos)
    sin = jnp.where(jnp.bitwise_and(quarter, 2) == 2, -sin, sin)
    return cos, sin


def split(values):
    high = values.astype(jnp.bfloat16)
    return high, (values - high.astype(jnp.float32)).astype(jnp.bfloat16)


def iota(shape, dim):
    return lax.broadcasted_iota(jnp.int32, shape, dim)


def image_tables(freqs, weights_ref):
    low_cos, low_sin = cos_sin(SPARSE * iota((8, W), 0) * freqs)
    high_cos, high_sin = cos_sin(SPARSE * 8 * iota((16, W), 0) * freqs)
    turn_cos, turn_sin = cos_sin(jnp.broadcast_to(SPARSE * 128 * freqs, (8, W)))
    cos_parts, sin_parts = [], []
    for a in range(16):
        ca, sa = high_cos[a : a + 1, :], high_sin[a : a + 1, :]
        cos_parts.append(ca * low_cos - sa * low_sin)
        sin_parts.append(sa * low_cos + ca * low_sin)
    cos = jnp.concatenate(cos_parts, 0).T
    sin = jnp.concatenate(sin_parts, 0).T
    turn_cos = jnp.broadcast_to(turn_cos[0:1], (W, W)).T
    turn_sin = jnp.broadcast_to(turn_sin[0:1], (W, W)).T
    for tile in range(COARSE // 128):
        at = slice(tile * 128, tile * 128 + 128)
        weights_ref[0:W, at] = cos.astype(jnp.bfloat16)
        weights_ref[W : 2 * W, at] = sin.astype(jnp.bfloat16)
        cos, sin = cos * turn_cos - sin * turn_sin, sin * turn_cos + cos * turn_sin


def transform_kernel(
    layout_hbm, freqs_hbm, eigen_hbm, out_ref, weights_ref, row_ref, eigen_ref, table, layout_ref, freqs_ref, sems
):
    freqs_copy = pltpu.make_async_copy(freqs_hbm, freqs_ref, sems.at[0])
    layout_copy = pltpu.make_async_copy(layout_hbm, layout_ref, sems.at[1])
    eigen_copy = pltpu.make_async_copy(eigen_hbm, eigen_ref, sems.at[2])
    freqs_copy.start()
    layout_copy.start()
    eigen_copy.start()
    row_first = lax.axis_index("slab") * ROWS
    col_first = lax.axis_index("kern") * COLS
    freqs_copy.wait()
    freqs = freqs_ref[...]
    step = 32
    base_cos, base_sin = cos_sin((col_first + iota((step, W), 0)) * freqs)
    turn_cos, turn_sin = cos_sin((step * iota((COLS // step, W), 0)) * freqs)
    for a in range(COLS // step):
        ca, sa = turn_cos[a : a + 1, :], turn_sin[a : a + 1, :]
        cos = ca * base_cos - sa * base_sin
        sin = sa * base_cos + ca * base_sin
        cos_high, cos_low = split(cos)
        sin_high, sin_low = split(sin)
        at = pl.ds(a * step, step)
        table[at, 0:W] = cos_high
        table[at, W : 2 * W] = sin_high
        table[at, 2 * W : 3 * W] = cos_low
        table[at, 3 * W : 4 * W] = sin_low
    row = iota((MXU_ROWS, W), 0)
    row = jnp.where(row < ROWS + 4, row, row - RING_ROWS)
    cos_row, sin_row = cos_sin((row_first + row) * freqs)
    row_ref[...] = (jnp.concatenate([cos_row, sin_row], 1) / W).astype(jnp.bfloat16)
    left_high, left_low = split(jnp.concatenate([cos_row[0:ROWS], sin_row[0:ROWS]], 0))
    layout_copy.wait()
    transmit = (2 * layout_ref[...] - 1).astype(jnp.float32).astype(jnp.bfloat16)
    along = jnp.dot(transmit, table[...], preferred_element_type=jnp.float32)
    along_re = along[:, 0:W] + along[:, 2 * W : 3 * W]
    along_im = -(along[:, W : 2 * W] + along[:, 3 * W : 4 * W])
    right = jnp.concatenate(
        [
            jnp.concatenate([along_re, along_im], 1),
            jnp.concatenate([along_im, -along_re], 1),
        ],
        0,
    )
    right_high, right_low = split(right)
    both = lax.dot_general(
        jnp.concatenate([left_high, left_high, left_low], 0),
        jnp.concatenate([right_high, right_low, right_high], 0),
        (((0,), (0,)), ((), ())),
        preferred_element_type=jnp.float32,
    ) * (1.0 / N)
    out_ref[0:W, :] = both[:, 0:W]
    out_ref[W : 2 * W, :] = both[:, W : 2 * W]
    image_tables(freqs, weights_ref)
    eigen_copy.wait()


def image_kernel(
    spec_ref, near_hbm, far_ref, weights_ref, row_ref, near_eigen, far_eigen, image_ref,
    fields_re, fields_im, near_ref, sem,
):
    near_copy = pltpu.make_async_copy(near_hbm, near_ref, sem)
    near_copy.start()
    row_table = row_ref[...]
    spec_re = spec_ref[0:W, :]
    spec_im = spec_ref[W : 2 * W, :]
    own = far_ref.shape[1]

    def row_field(kernels_ref, f):
        kern_re = kernels_ref[0, f]
        kern_im = kernels_ref[1, f]
        re16 = (spec_re * kern_re - spec_im * kern_im).astype(jnp.bfloat16)
        im16 = (spec_re * kern_im + spec_im * kern_re).astype(jnp.bfloat16)
        block = jnp.concatenate(
            [jnp.concatenate([re16, im16], 1), jnp.concatenate([-im16, re16], 1)], 0
        )
        part = jnp.dot(row_table, block, preferred_element_type=jnp.float32)
        real = part[0:RING_ROWS, 0:W]
        imag = part[0:RING_ROWS, W : 2 * W]
        return real, imag

    def pair_of_fields(kernels_ref, f, first):
        pair = [row_field(kernels_ref, f), row_field(kernels_ref, f + 1)]
        real = jnp.concatenate([pair[0][0], pair[1][0]], 0).astype(jnp.bfloat16)
        imag = jnp.concatenate([pair[0][1], pair[1][1]], 0).astype(jnp.bfloat16)
        at = slice((first + f) * RING_ROWS, (first + f + 2) * RING_ROWS)
        fields_re[at, 0:W] = real
        fields_re[at, W : 2 * W] = -imag
        fields_im[at, 0:W] = imag
        fields_im[at, W : 2 * W] = real

    def power(first, count, eigen_ref, f0, p, start):
        rows = slice(first * RING_ROWS, (first + count) * RING_ROWS)
        weights = weights_ref[:, p * 256 : (p + 1) * 256]
        real = jnp.dot(fields_re[rows, :], weights, preferred_element_type=jnp.float32)
        imag = jnp.dot(fields_im[rows, :], weights, preferred_element_type=jnp.float32)
        for f in range(count):
            re = real[f * RING_ROWS : (f + 1) * RING_ROWS]
            im = imag[f * RING_ROWS : (f + 1) * RING_ROWS]
            term = eigen_ref[0:1, f0 + f : f0 + f + 1] * (re * re + im * im)
            start = term if start is None else start + term
        return start

    parts = COARSE // 256
    for f in range(0, own, 2):
        pair_of_fields(far_ref, f, 0)
    near_copy.wait()
    for p in range(parts):
        for f in range(0, own, 2):
            if p == min(f * parts // own + (f > 0), parts - 1):
                pair_of_fields(near_ref, f, own)
        image_ref[:, p * 256 : (p + 1) * 256] = power(0, own, far_eigen, 0, p, None)
    for p in range(parts):
        at = slice(p * 256, (p + 1) * 256)
        image_ref[:, at] = power(own, own, near_eigen, 0, p, image_ref[:, at])


def dirichlet():
    distance = np.mod(np.arange(N)[None, :] - SPARSE * np.arange(32)[:, None], N)
    turn = np.pi * distance / N
    sine = np.where(distance == 0, 1.0, COARSE * np.sin(turn))
    kernel = np.where(distance % SPARSE == 0, distance == 0, np.sin(COARSE * turn) * np.cos(turn) / sine)
    kernel = kernel.astype(np.float32)
    high = kernel.astype(ml_dtypes.bfloat16)
    low = (kernel - high.astype(np.float32)).astype(ml_dtypes.bfloat16)
    return high, low


def laplace(field):
    rows, cols = field.shape
    return (
        pltpu.roll(field, 1, 0)
        + pltpu.roll(field, rows - 1, 0)
        + pltpu.roll(field, 1, 1)
        + pltpu.roll(field, cols - 1, 1)
        - 4.0 * field
    )


def bake_kernel(
    own_ref, other_ref, high_ref, low_ref, rates, image_hbm, acid_hbm, parts, ring, image_ref, acid_ref, sems
):
    kern = lax.axis_index("kern")
    for p in range(COARSE // 256):
        block = jnp.bitwise_and(p - kern, COARSE // 256 - 1)
        at = pl.ds(pl.multiple_of(block * 256, 256), 256)
        value = own_ref[:, p * 256 : (p + 1) * 256] + other_ref[:, p * 256 : (p + 1) * 256]
        high = value.astype(jnp.bfloat16).astype(jnp.float32)
        parts[0 : 2 * RING_ROWS, at] = jnp.concatenate([high, value - high], 0).astype(jnp.bfloat16)

    def weights(ref, tiles):
        rows = [
            jnp.concatenate([ref[:, ((t - m) % 32) * 128 : ((t - m) % 32) * 128 + 128] for t in tiles], 1)
            for m in range(COARSE // 32)
        ]
        return jnp.concatenate(rows, 0)

    for p in range(5):
        tiles = (2 * p, 2 * p + 1) if p < 4 else (8, 31)
        wide = jnp.dot(parts[0 : 2 * RING_ROWS, :], weights(high_ref, tiles), preferred_element_type=jnp.float32)
        fine = jnp.dot(parts[0:MXU_ROWS, :], weights(low_ref, tiles), preferred_element_type=jnp.float32)
        value = wide[0:RING_ROWS] + (wide[RING_ROWS : 2 * RING_ROWS] + fine[0:RING_ROWS])
        if p < 4:
            ring[:, p * 256 : (p + 1) * 256] = value
        else:
            side = iota((RING_ROWS, 128), 1) < 64
            ring[:, COLS:RING_COLS] = jnp.where(side, value[:, 0:128], value[:, 128:256])

    dill_rate, acid_rate, quench_rate, react_rate, quench_start = (rates[i] for i in range(5))
    aerial_image = ring[...] / FIELDS
    image_ref[...] = aerial_image[0:ROWS, 0:COLS]
    image_copy = pltpu.make_async_copy(image_ref, image_hbm, sems.at[0])
    image_copy.start()
    acid_field = 1.0 - jnp.exp((-4.0 * dill_rate) * aerial_image)
    acid_diffusion = acid_rate * (0.5 + 0.5 * acid_field)
    quencher = jnp.zeros_like(acid_field) + quench_start
    for bake_step in range(STEPS):
        reaction = (4.0 * react_rate) * acid_field * quencher
        new_acid = acid_field + acid_diffusion * laplace(acid_field) - reaction
        quencher = quencher + quench_rate * laplace(quencher) - reaction
        acid_field = new_acid
    acid_ref[...] = acid_field[0:ROWS, 0:COLS]
    acid_copy = pltpu.make_async_copy(acid_ref, acid_hbm, sems.at[1])
    acid_copy.start()
    image_copy.wait()
    acid_copy.wait()


VMEM = pl.BlockSpec(memory_space=pltpu.VMEM)
SMEM = pl.BlockSpec(memory_space=pltpu.SMEM)
HBM = pl.BlockSpec(memory_space=pltpu.HBM)


def in_hbm(array):
    return pltpu.with_memory_space_constraint(array, pltpu.HBM)


def sum_everywhere(part):
    plane, along_z = plane_groups(), z_groups()
    count = len(plane[0])
    piece = part.shape[0] // count

    def exchange(blocks, groups):
        return lax.all_to_all(blocks, ALL, 0, 0, tiled=True, axis_index_groups=groups)

    def total(blocks):
        return jnp.sum(blocks.reshape(-1, piece, part.shape[1]), 0)

    def copies(block, many):
        return jnp.broadcast_to(block[None], (many,) + block.shape).reshape(-1, block.shape[1])

    some = total(exchange(part, plane))
    full = total(exchange(copies(some, len(along_z[0])), along_z))
    return exchange(copies(full, count), plane)


def shards(layout, band_freqs, kernels, eigen_values, bake_rates):
    freqs = band_freqs.reshape(1, W)
    f32 = jnp.float32
    params = pltpu.CompilerParams(vmem_limit_bytes=24 * 2**20)
    far_kernels = lax.ppermute(kernels, ALL, from_next_z(1))
    far_eigen = lax.ppermute(eigen_values, ALL, from_next_z(-1))
    own = kernels.shape[1]
    part, *tables, near_eigen = pl.pallas_call(
        transform_kernel,
        out_shape=(
            jax.ShapeDtypeStruct((2 * W, W), f32),
            jax.ShapeDtypeStruct((2 * W, COARSE), jnp.bfloat16),
            jax.ShapeDtypeStruct((MXU_ROWS, 2 * W), jnp.bfloat16),
            jax.ShapeDtypeStruct((1, own), f32),
        ),
        in_specs=[HBM] * 3,
        out_specs=(VMEM,) * 4,
        scratch_shapes=[
            pltpu.VMEM((COLS, 4 * W), jnp.bfloat16),
            pltpu.VMEM((ROWS, COLS), jnp.int32),
            pltpu.VMEM((1, W), jnp.int32),
            pltpu.SemaphoreType.DMA((3,)),
        ],
        compiler_params=params,
        name="transform",
    )(in_hbm(layout), in_hbm(freqs), in_hbm(eigen_values.reshape(1, own)))
    part, far_eigen = lax.optimization_barrier((part, far_eigen))
    spectrum = sum_everywhere(part)
    own_image = pl.pallas_call(
        image_kernel,
        out_shape=jax.ShapeDtypeStruct((RING_ROWS, COARSE), f32),
        in_specs=[VMEM, HBM] + [VMEM] * 5,
        out_specs=VMEM,
        scratch_shapes=[
            pltpu.VMEM((2 * own * RING_ROWS, 2 * W), jnp.bfloat16),
            pltpu.VMEM((2 * own * RING_ROWS, 2 * W), jnp.bfloat16),
            pltpu.VMEM(kernels.shape, f32),
            pltpu.SemaphoreType.DMA,
        ],
        compiler_params=params,
        name="image",
    )(spectrum, in_hbm(kernels), far_kernels, *tables, near_eigen, far_eigen.reshape(1, own))
    across_cores = [(i, i + 64 if (i // 64) % 2 == 0 else i - 64) for i in range(256)]
    other_image = lax.ppermute(own_image, ALL, across_cores)
    block = jax.ShapeDtypeStruct((ROWS, COLS), f32)
    high, low = dirichlet()
    return pl.pallas_call(
        bake_kernel,
        out_shape=(block, block),
        in_specs=[VMEM, VMEM, VMEM, VMEM, SMEM],
        out_specs=(HBM, HBM),
        scratch_shapes=[
            pltpu.VMEM((2 * MXU_ROWS, COARSE), jnp.bfloat16),
            pltpu.VMEM((RING_ROWS, RING_COLS), f32),
            pltpu.VMEM((ROWS, COLS), f32),
            pltpu.VMEM((ROWS, COLS), f32),
            pltpu.SemaphoreType.DMA((2,)),
        ],
        compiler_params=params,
        name="bake",
    )(own_image, other_image, jnp.asarray(high), jnp.asarray(low), bake_rates)


def solution(mesh):
    return jax.shard_map(
        shards,
        mesh=mesh,
        in_specs=(P("slab", "kern"), P(), P(None, "kern", None, None), P("kern"), P()),
        out_specs=(P("slab", "kern"), P("slab", "kern")),
        check_vma=False,
    )
```

```python
import math

import jax
import jax.numpy as jnp
import ml_dtypes
import numpy as np
from jax import lax
from jax.experimental import pallas as pl
from jax.experimental.pallas import tpu as pltpu
from jax.sharding import PartitionSpec as P

N = 4096
W = 128
FIELDS = 48
STEPS = 2

ROWS = 64
COLS = 1024
RING_ROWS = 72
MXU_ROWS = 80
RING_COLS = 1152
SPARSE = 4
COARSE = N // SPARSE
ALL = ("kern", "slab")
CHIP_Z, CORES, FAR_Z, SIDE = 2, 2, 4, 4


def device(z_lo, core, z_hi, y, x):
    return (z_lo * CORES + core) * 64 + (z_hi * SIDE + y) * SIDE + x


def place(i):
    kern, slab = divmod(i, 64)
    return kern // CORES, kern % CORES, slab // SIDE**2, slab // SIDE % SIDE, slab % SIDE


def groups_along(kept):
    groups = {}
    for i in range(256):
        groups.setdefault(tuple(place(i)[axis] for axis in kept), []).append(i)
    return list(groups.values())


def plane_groups():
    return groups_along((0, 2))


def z_groups():
    return groups_along((1, 3, 4))


def from_next_z(side):
    pairs = []
    for i in range(256):
        z_lo, core, z_hi, y, x = place(i)
        z = (z_hi * CHIP_Z + z_lo + (side if z_lo == core else -side)) % (FAR_Z * CHIP_Z)
        pairs.append((device(z % CHIP_Z, core, z // CHIP_Z, y, x), i))
    return pairs


def cos_sin(turns):
    m = jnp.bitwise_and(turns, N - 1)
    quarter = jnp.right_shift(m + N // 8, 10)
    t = (m - jnp.left_shift(quarter, 10)).astype(jnp.float32) * (2.0 * math.pi / N)
    t2 = t * t
    s = t * (1.0 + t2 * (-1.0 / 6 + t2 * (1.0 / 120 + t2 * (-1.0 / 5040 + t2 * (1.0 / 362880)))))
    c = 1.0 + t2 * (-0.5 + t2 * (1.0 / 24 + t2 * (-1.0 / 720 + t2 * (1.0 / 40320))))
    odd = jnp.bitwise_and(quarter, 1) == 1
    cos = jnp.where(odd, s, c)
    sin = jnp.where(odd, c, s)
    cos = jnp.where(jnp.bitwise_and(quarter + 1, 2) == 2, -cos, cos)
    sin = jnp.where(jnp.bitwise_and(quarter, 2) == 2, -sin, sin)
    return cos, sin


def split(values):
    high = values.astype(jnp.bfloat16)
    return high, (values - high.astype(jnp.float32)).astype(jnp.bfloat16)


def iota(shape, dim):
    return lax.broadcasted_iota(jnp.int32, shape, dim)


def tables_kernel(freqs_ref, weights_ref, row_ref):
    freqs = freqs_ref[...]
    row = iota((MXU_ROWS, W), 0)
    row = jnp.where(row < ROWS + 4, row, row - RING_ROWS)
    cos_row, sin_row = cos_sin((lax.axis_index("slab") * ROWS + row) * freqs)
    row_ref[...] = (jnp.concatenate([cos_row, sin_row], 1) / W).astype(jnp.bfloat16)

    low_cos, low_sin = cos_sin(SPARSE * iota((8, W), 0) * freqs)
    high_cos, high_sin = cos_sin(SPARSE * 8 * iota((16, W), 0) * freqs)
    turn_cos, turn_sin = cos_sin(jnp.broadcast_to(SPARSE * 128 * freqs, (8, W)))
    cos_parts, sin_parts = [], []
    for a in range(16):
        ca, sa = high_cos[a : a + 1, :], high_sin[a : a + 1, :]
        cos_parts.append(ca * low_cos - sa * low_sin)
        sin_parts.append(sa * low_cos + ca * low_sin)
    cos = jnp.concatenate(cos_parts, 0).T
    sin = jnp.concatenate(sin_parts, 0).T
    turn_cos = jnp.broadcast_to(turn_cos[0:1], (W, W)).T
    turn_sin = jnp.broadcast_to(turn_sin[0:1], (W, W)).T
    for tile in range(COARSE // 128):
        at = slice(tile * 128, tile * 128 + 128)
        weights_ref[0:W, at] = cos.astype(jnp.bfloat16)
        weights_ref[W : 2 * W, at] = sin.astype(jnp.bfloat16)
        cos, sin = cos * turn_cos - sin * turn_sin, sin * turn_cos + cos * turn_sin


def transform_kernel(
    layout_hbm, freqs_hbm, eigen_hbm, out_ref, freqs_ref, eigen_ref, table, layout_ref, sems
):
    freqs_copy = pltpu.make_async_copy(freqs_hbm, freqs_ref, sems.at[0])
    layout_copy = pltpu.make_async_copy(layout_hbm, layout_ref, sems.at[1])
    eigen_copy = pltpu.make_async_copy(eigen_hbm, eigen_ref, sems.at[2])
    freqs_copy.start()
    layout_copy.start()
    eigen_copy.start()
    row_first = lax.axis_index("slab") * ROWS
    col_first = lax.axis_index("kern") * COLS
    freqs_copy.wait()
    freqs = freqs_ref[...]
    step = 32
    base_cos, base_sin = cos_sin((col_first + iota((step, W), 0)) * freqs)
    turn_cos, turn_sin = cos_sin((step * iota((COLS // step, W), 0)) * freqs)
    for a in range(COLS // step):
        ca, sa = turn_cos[a : a + 1, :], turn_sin[a : a + 1, :]
        cos = ca * base_cos - sa * base_sin
        sin = sa * base_cos + ca * base_sin
        cos_high, cos_low = split(cos)
        sin_high, sin_low = split(sin)
        at = pl.ds(a * step, step)
        table[at, 0:W] = cos_high
        table[at, W : 2 * W] = sin_high
        table[at, 2 * W : 3 * W] = cos_low
        table[at, 3 * W : 4 * W] = sin_low
    cos_row, sin_row = cos_sin((row_first + iota((ROWS, W), 0)) * freqs)
    left_high, left_low = split(jnp.concatenate([cos_row, sin_row], 0))
    layout_copy.wait()
    transmit = (2 * layout_ref[...] - 1).astype(jnp.float32).astype(jnp.bfloat16)
    along = jnp.dot(transmit, table[...], preferred_element_type=jnp.float32)
    along_re = along[:, 0:W] + along[:, 2 * W : 3 * W]
    along_im = -(along[:, W : 2 * W] + along[:, 3 * W : 4 * W])
    right = jnp.concatenate(
        [
            jnp.concatenate([along_re, along_im], 1),
            jnp.concatenate([along_im, -along_re], 1),
        ],
        0,
    )
    right_high, right_low = split(right)
    both = lax.dot_general(
        jnp.concatenate([left_high, left_high, left_low], 0),
        jnp.concatenate([right_high, right_low, right_high], 0),
        (((0,), (0,)), ((), ())),
        preferred_element_type=jnp.float32,
    ) * (1.0 / N)
    out_ref[0:W, :] = both[:, 0:W]
    out_ref[W : 2 * W, :] = both[:, W : 2 * W]
    eigen_copy.wait()


def image_kernel(
    spec_ref, near_hbm, far_ref, weights_ref, row_ref, near_eigen, far_eigen, image_ref,
    fields_re, fields_im, near_ref, sem,
):
    near_copy = pltpu.make_async_copy(near_hbm, near_ref, sem)
    near_copy.start()
    row_table = row_ref[...]
    spec_re = spec_ref[0:W, :]
    spec_im = spec_ref[W : 2 * W, :]
    own = far_ref.shape[1]

    def row_field(kernels_ref, f):
        kern_re = kernels_ref[0, f]
        kern_im = kernels_ref[1, f]
        re16 = (spec_re * kern_re - spec_im * kern_im).astype(jnp.bfloat16)
        im16 = (spec_re * kern_im + spec_im * kern_re).astype(jnp.bfloat16)
        block = jnp.concatenate(
            [jnp.concatenate([re16, im16], 1), jnp.concatenate([-im16, re16], 1)], 0
        )
        part = jnp.dot(row_table, block, preferred_element_type=jnp.float32)
        real = part[0:RING_ROWS, 0:W]
        imag = part[0:RING_ROWS, W : 2 * W]
        return real, imag

    def pair_of_fields(kernels_ref, f, first):
        pair = [row_field(kernels_ref, f), row_field(kernels_ref, f + 1)]
        real = jnp.concatenate([pair[0][0], pair[1][0]], 0).astype(jnp.bfloat16)
        imag = jnp.concatenate([pair[0][1], pair[1][1]], 0).astype(jnp.bfloat16)
        at = slice((first + f) * RING_ROWS, (first + f + 2) * RING_ROWS)
        fields_re[at, 0:W] = real
        fields_re[at, W : 2 * W] = -imag
        fields_im[at, 0:W] = imag
        fields_im[at, W : 2 * W] = real

    def power(first, count, eigen_ref, f0, p, start):
        rows = slice(first * RING_ROWS, (first + count) * RING_ROWS)
        weights = weights_ref[:, p * 256 : (p + 1) * 256]
        real = jnp.dot(fields_re[rows, :], weights, preferred_element_type=jnp.float32)
        imag = jnp.dot(fields_im[rows, :], weights, preferred_element_type=jnp.float32)
        for f in range(count):
            re = real[f * RING_ROWS : (f + 1) * RING_ROWS]
            im = imag[f * RING_ROWS : (f + 1) * RING_ROWS]
            term = eigen_ref[0:1, f0 + f : f0 + f + 1] * (re * re + im * im)
            start = term if start is None else start + term
        return start

    parts = COARSE // 256
    for f in range(0, own, 2):
        pair_of_fields(far_ref, f, 0)
    near_copy.wait()
    for p in range(parts):
        for f in range(0, own, 2):
            if p == min(f * parts // own + (f > 0), parts - 1):
                pair_of_fields(near_ref, f, own)
        image_ref[:, p * 256 : (p + 1) * 256] = power(0, own, far_eigen, 0, p, None)
    for p in range(parts):
        at = slice(p * 256, (p + 1) * 256)
        image_ref[:, at] = power(own, own, near_eigen, 0, p, image_ref[:, at])


def dirichlet():
    distance = np.mod(np.arange(N)[None, :] - SPARSE * np.arange(32)[:, None], N)
    turn = np.pi * distance / N
    sine = np.where(distance == 0, 1.0, COARSE * np.sin(turn))
    kernel = np.where(distance % SPARSE == 0, distance == 0, np.sin(COARSE * turn) * np.cos(turn) / sine)
    kernel = kernel.astype(np.float32)
    high = kernel.astype(ml_dtypes.bfloat16)
    low = (kernel - high.astype(np.float32)).astype(ml_dtypes.bfloat16)
    return high, low


def laplace(field):
    rows, cols = field.shape
    return (
        pltpu.roll(field, 1, 0)
        + pltpu.roll(field, rows - 1, 0)
        + pltpu.roll(field, 1, 1)
        + pltpu.roll(field, cols - 1, 1)
        - 4.0 * field
    )


def bake_kernel(
    own_ref, other_ref, high_ref, low_ref, rates, image_hbm, acid_hbm, parts, ring, image_ref, acid_ref, sems
):
    kern = lax.axis_index("kern")
    for p in range(COARSE // 256):
        block = jnp.bitwise_and(p - kern, COARSE // 256 - 1)
        at = pl.ds(pl.multiple_of(block * 256, 256), 256)
        value = own_ref[:, p * 256 : (p + 1) * 256] + other_ref[:, p * 256 : (p + 1) * 256]
        high = value.astype(jnp.bfloat16).astype(jnp.float32)
        parts[0 : 2 * RING_ROWS, at] = jnp.concatenate([high, value - high], 0).astype(jnp.bfloat16)

    def weights(ref, tiles):
        rows = [
            jnp.concatenate([ref[:, ((t - m) % 32) * 128 : ((t - m) % 32) * 128 + 128] for t in tiles], 1)
            for m in range(COARSE // 32)
        ]
        return jnp.concatenate(rows, 0)

    for p in range(5):
        tiles = (2 * p, 2 * p + 1) if p < 4 else (8, 31)
        wide = jnp.dot(parts[0 : 2 * RING_ROWS, :], weights(high_ref, tiles), preferred_element_type=jnp.float32)
        fine = jnp.dot(parts[0:MXU_ROWS, :], weights(low_ref, tiles), preferred_element_type=jnp.float32)
        value = wide[0:RING_ROWS] + (wide[RING_ROWS : 2 * RING_ROWS] + fine[0:RING_ROWS])
        if p < 4:
            ring[:, p * 256 : (p + 1) * 256] = value
        else:
            side = iota((RING_ROWS, 128), 1) < 64
            ring[:, COLS:RING_COLS] = jnp.where(side, value[:, 0:128], value[:, 128:256])

    dill_rate, acid_rate, quench_rate, react_rate, quench_start = (rates[i] for i in range(5))
    aerial_image = ring[...] / FIELDS
    image_ref[...] = aerial_image[0:ROWS, 0:COLS]
    image_copy = pltpu.make_async_copy(image_ref, image_hbm, sems.at[0])
    image_copy.start()
    acid_field = 1.0 - jnp.exp((-4.0 * dill_rate) * aerial_image)
    acid_diffusion = acid_rate * (0.5 + 0.5 * acid_field)
    quencher = jnp.zeros_like(acid_field) + quench_start
    for bake_step in range(STEPS):
        reaction = (4.0 * react_rate) * acid_field * quencher
        new_acid = acid_field + acid_diffusion * laplace(acid_field) - reaction
        quencher = quencher + quench_rate * laplace(quencher) - reaction
        acid_field = new_acid
    acid_ref[...] = acid_field[0:ROWS, 0:COLS]
    acid_copy = pltpu.make_async_copy(acid_ref, acid_hbm, sems.at[1])
    acid_copy.start()
    image_copy.wait()
    acid_copy.wait()


VMEM = pl.BlockSpec(memory_space=pltpu.VMEM)
SMEM = pl.BlockSpec(memory_space=pltpu.SMEM)
HBM = pl.BlockSpec(memory_space=pltpu.HBM)


def in_hbm(array):
    return pltpu.with_memory_space_constraint(array, pltpu.HBM)


def sum_everywhere(part, beside):
    plane, along_z = plane_groups(), z_groups()
    count = len(plane[0])
    piece = part.shape[0] // count

    def exchange(blocks, groups):
        return lax.all_to_all(blocks, ALL, 0, 0, tiled=True, axis_index_groups=groups)

    def total(blocks):
        return jnp.sum(blocks.reshape(-1, piece, part.shape[1]), 0)

    def copies(block, many):
        return jnp.broadcast_to(block[None], (many,) + block.shape).reshape(-1, block.shape[1])

    blocks, beside = lax.optimization_barrier((exchange(part, plane), beside))
    some = total(blocks)
    full = total(exchange(copies(some, len(along_z[0])), along_z))
    return exchange(copies(full, count), plane), beside


def shards(layout, band_freqs, kernels, eigen_values, bake_rates):
    freqs = band_freqs.reshape(1, W)
    f32 = jnp.float32
    params = pltpu.CompilerParams(vmem_limit_bytes=24 * 2**20)
    far_kernels = lax.ppermute(kernels, ALL, from_next_z(1))
    far_eigen = lax.ppermute(eigen_values, ALL, from_next_z(-1))
    own = kernels.shape[1]
    part, freqs_here, near_eigen = pl.pallas_call(
        transform_kernel,
        out_shape=(
            jax.ShapeDtypeStruct((2 * W, W), f32),
            jax.ShapeDtypeStruct((1, W), jnp.int32),
            jax.ShapeDtypeStruct((1, own), f32),
        ),
        in_specs=[HBM] * 3,
        out_specs=(VMEM,) * 3,
        scratch_shapes=[
            pltpu.VMEM((COLS, 4 * W), jnp.bfloat16),
            pltpu.VMEM((ROWS, COLS), jnp.int32),
            pltpu.SemaphoreType.DMA((3,)),
        ],
        compiler_params=params,
        name="transform",
    )(in_hbm(layout), in_hbm(freqs), in_hbm(eigen_values.reshape(1, own)))
    tables = pl.pallas_call(
        tables_kernel,
        out_shape=(
            jax.ShapeDtypeStruct((2 * W, COARSE), jnp.bfloat16),
            jax.ShapeDtypeStruct((MXU_ROWS, 2 * W), jnp.bfloat16),
        ),
        in_specs=[VMEM],
        out_specs=(VMEM, VMEM),
        compiler_params=params,
        cost_estimate=pl.CostEstimate(flops=2_000_000, transcendentals=0, bytes_accessed=1_000_000),
        name="tables",
    )(freqs_here)
    spectrum, (far_eigen, tables) = sum_everywhere(part, (far_eigen, tables))
    own_image = pl.pallas_call(
        image_kernel,
        out_shape=jax.ShapeDtypeStruct((RING_ROWS, COARSE), f32),
        in_specs=[VMEM, HBM] + [VMEM] * 5,
        out_specs=VMEM,
        scratch_shapes=[
            pltpu.VMEM((2 * own * RING_ROWS, 2 * W), jnp.bfloat16),
            pltpu.VMEM((2 * own * RING_ROWS, 2 * W), jnp.bfloat16),
            pltpu.VMEM(kernels.shape, f32),
            pltpu.SemaphoreType.DMA,
        ],
        compiler_params=params,
        name="image",
    )(spectrum, in_hbm(kernels), far_kernels, *tables, near_eigen, far_eigen.reshape(1, own))
    across_cores = [(i, i + 64 if (i // 64) % 2 == 0 else i - 64) for i in range(256)]
    other_image = lax.ppermute(own_image, ALL, across_cores)
    block = jax.ShapeDtypeStruct((ROWS, COLS), f32)
    high, low = dirichlet()
    return pl.pallas_call(
        bake_kernel,
        out_shape=(block, block),
        in_specs=[VMEM, VMEM, VMEM, VMEM, SMEM],
        out_specs=(HBM, HBM),
        scratch_shapes=[
            pltpu.VMEM((2 * MXU_ROWS, COARSE), jnp.bfloat16),
            pltpu.VMEM((RING_ROWS, RING_COLS), f32),
            pltpu.VMEM((ROWS, COLS), f32),
            pltpu.VMEM((ROWS, COLS), f32),
            pltpu.SemaphoreType.DMA((2,)),
        ],
        compiler_params=params,
        name="bake",
    )(own_image, other_image, jnp.asarray(high), jnp.asarray(low), bake_rates)


def solution(mesh):
    return jax.shard_map(
        shards,
        mesh=mesh,
        in_specs=(P("slab", "kern"), P(), P(None, "kern", None, None), P("kern"), P()),
        out_specs=(P("slab", "kern"), P("slab", "kern")),
        check_vma=False,
    )
```

```python
import math

import jax
import jax.numpy as jnp
import ml_dtypes
import numpy as np
from jax import lax
from jax.experimental import pallas as pl
from jax.experimental.pallas import tpu as pltpu
from jax.sharding import PartitionSpec as P

N = 4096
W = 128
FIELDS = 48
STEPS = 2

ROWS = 64
COLS = 1024
RING_ROWS = 72
MXU_ROWS = 80
RING_COLS = 1152
SPARSE = 4
COARSE = N // SPARSE
ALL = ("kern", "slab")
CHIP_Z, CORES, FAR_Z, SIDE = 2, 2, 4, 4


def device(z_lo, core, z_hi, y, x):
    return (z_lo * CORES + core) * 64 + (z_hi * SIDE + y) * SIDE + x


def place(i):
    kern, slab = divmod(i, 64)
    return kern // CORES, kern % CORES, slab // SIDE**2, slab // SIDE % SIDE, slab % SIDE


def groups_along(kept):
    groups = {}
    for i in range(256):
        groups.setdefault(tuple(place(i)[axis] for axis in kept), []).append(i)
    return list(groups.values())


def plane_groups():
    return groups_along((0, 2))


def z_groups():
    return groups_along((1, 3, 4))


def from_next_z(side):
    pairs = []
    for i in range(256):
        z_lo, core, z_hi, y, x = place(i)
        z = (z_hi * CHIP_Z + z_lo + (side if z_lo == core else -side)) % (FAR_Z * CHIP_Z)
        pairs.append((device(z % CHIP_Z, core, z // CHIP_Z, y, x), i))
    return pairs


def cos_sin(turns):
    m = jnp.bitwise_and(turns, N - 1)
    quarter = jnp.right_shift(m + N // 8, 10)
    t = (m - jnp.left_shift(quarter, 10)).astype(jnp.float32) * (2.0 * math.pi / N)
    t2 = t * t
    s = t * (1.0 + t2 * (-1.0 / 6 + t2 * (1.0 / 120 + t2 * (-1.0 / 5040 + t2 * (1.0 / 362880)))))
    c = 1.0 + t2 * (-0.5 + t2 * (1.0 / 24 + t2 * (-1.0 / 720 + t2 * (1.0 / 40320))))
    odd = jnp.bitwise_and(quarter, 1) == 1
    cos = jnp.where(odd, s, c)
    sin = jnp.where(odd, c, s)
    cos = jnp.where(jnp.bitwise_and(quarter + 1, 2) == 2, -cos, cos)
    sin = jnp.where(jnp.bitwise_and(quarter, 2) == 2, -sin, sin)
    return cos, sin


def split(values):
    high = values.astype(jnp.bfloat16)
    return high, (values - high.astype(jnp.float32)).astype(jnp.bfloat16)


def iota(shape, dim):
    return lax.broadcasted_iota(jnp.int32, shape, dim)


def image_tables(freqs, weights_ref):
    low_cos, low_sin = cos_sin(SPARSE * iota((8, W), 0) * freqs)
    high_cos, high_sin = cos_sin(SPARSE * 8 * iota((16, W), 0) * freqs)
    turn_cos, turn_sin = cos_sin(jnp.broadcast_to(SPARSE * 128 * freqs, (8, W)))
    cos_parts, sin_parts = [], []
    for a in range(16):
        ca, sa = high_cos[a : a + 1, :], high_sin[a : a + 1, :]
        cos_parts.append(ca * low_cos - sa * low_sin)
        sin_parts.append(sa * low_cos + ca * low_sin)
    cos = jnp.concatenate(cos_parts, 0).T
    sin = jnp.concatenate(sin_parts, 0).T
    turn_cos = jnp.broadcast_to(turn_cos[0:1], (W, W)).T
    turn_sin = jnp.broadcast_to(turn_sin[0:1], (W, W)).T
    for tile in range(COARSE // 128):
        at = slice(tile * 128, tile * 128 + 128)
        weights_ref[0:W, at] = cos.astype(jnp.bfloat16)
        weights_ref[W : 2 * W, at] = sin.astype(jnp.bfloat16)
        cos, sin = cos * turn_cos - sin * turn_sin, sin * turn_cos + cos * turn_sin


def transform_kernel(
    layout_hbm, freqs_hbm, eigen_hbm, out_ref, weights_ref, row_ref, eigen_ref, table, layout_ref, freqs_ref, sems
):
    freqs_copy = pltpu.make_async_copy(freqs_hbm, freqs_ref, sems.at[0])
    layout_copy = pltpu.make_async_copy(layout_hbm, layout_ref, sems.at[1])
    eigen_copy = pltpu.make_async_copy(eigen_hbm, eigen_ref, sems.at[2])
    freqs_copy.start()
    layout_copy.start()
    eigen_copy.start()
    row_first = lax.axis_index("slab") * ROWS
    col_first = lax.axis_index("kern") * COLS
    freqs_copy.wait()
    freqs = freqs_ref[...]
    step = 32
    base_cos, base_sin = cos_sin((col_first + iota((step, W), 0)) * freqs)
    turn_cos, turn_sin = cos_sin((step * iota((COLS // step, W), 0)) * freqs)
    for a in range(COLS // step):
        ca, sa = turn_cos[a : a + 1, :], turn_sin[a : a + 1, :]
        cos = ca * base_cos - sa * base_sin
        sin = sa * base_cos + ca * base_sin
        cos_high, cos_low = split(cos)
        sin_high, sin_low = split(sin)
        at = pl.ds(a * step, step)
        table[at, 0:W] = cos_high
        table[at, W : 2 * W] = sin_high
        table[at, 2 * W : 3 * W] = cos_low
        table[at, 3 * W : 4 * W] = sin_low
    row = iota((MXU_ROWS, W), 0)
    row = jnp.where(row < ROWS + 4, row, row - RING_ROWS)
    cos_row, sin_row = cos_sin((row_first + row) * freqs)
    row_ref[...] = (jnp.concatenate([cos_row, sin_row], 1) / W).astype(jnp.bfloat16)
    left_high, left_low = split(jnp.concatenate([cos_row[0:ROWS], sin_row[0:ROWS]], 0))
    layout_copy.wait()
    transmit = (2 * layout_ref[...] - 1).astype(jnp.float32).astype(jnp.bfloat16)
    along = jnp.dot(transmit, table[...], preferred_element_type=jnp.float32)
    along_re = along[:, 0:W] + along[:, 2 * W : 3 * W]
    along_im = -(along[:, W : 2 * W] + along[:, 3 * W : 4 * W])
    right = jnp.concatenate(
        [
            jnp.concatenate([along_re, along_im], 1),
            jnp.concatenate([along_im, -along_re], 1),
        ],
        0,
    )
    right_high, right_low = split(right)
    both = lax.dot_general(
        jnp.concatenate([left_high, left_high, left_low], 0),
        jnp.concatenate([right_high, right_low, right_high], 0),
        (((0,), (0,)), ((), ())),
        preferred_element_type=jnp.float32,
    ) * (1.0 / N)
    out_ref[0:W, :] = both[:, 0:W]
    out_ref[W : 2 * W, :] = both[:, W : 2 * W]
    image_tables(freqs, weights_ref)
    eigen_copy.wait()


def image_kernel(
    spec_ref, near_hbm, far_ref, weights_ref, row_ref, near_eigen, far_eigen, image_ref,
    fields_re, fields_im, near_ref, sem,
):
    near_copy = pltpu.make_async_copy(near_hbm, near_ref, sem)
    near_copy.start()
    row_table = row_ref[...]
    spec_re = spec_ref[0:W, :]
    spec_im = spec_ref[W : 2 * W, :]
    own = far_ref.shape[1]

    def row_field(kernels_ref, f):
        kern_re = kernels_ref[0, f]
        kern_im = kernels_ref[1, f]
        re16 = (spec_re * kern_re - spec_im * kern_im).astype(jnp.bfloat16)
        im16 = (spec_re * kern_im + spec_im * kern_re).astype(jnp.bfloat16)
        block = jnp.concatenate(
            [jnp.concatenate([re16, im16], 1), jnp.concatenate([-im16, re16], 1)], 0
        )
        part = jnp.dot(row_table, block, preferred_element_type=jnp.float32)
        real = part[0:RING_ROWS, 0:W]
        imag = part[0:RING_ROWS, W : 2 * W]
        return real, imag

    def pair_of_fields(kernels_ref, f, first):
        pair = [row_field(kernels_ref, f), row_field(kernels_ref, f + 1)]
        real = jnp.concatenate([pair[0][0], pair[1][0]], 0).astype(jnp.bfloat16)
        imag = jnp.concatenate([pair[0][1], pair[1][1]], 0).astype(jnp.bfloat16)
        at = slice((first + f) * RING_ROWS, (first + f + 2) * RING_ROWS)
        fields_re[at, 0:W] = real
        fields_re[at, W : 2 * W] = -imag
        fields_im[at, 0:W] = imag
        fields_im[at, W : 2 * W] = real

    def power(first, count, eigen_ref, f0, p, start):
        rows = slice(first * RING_ROWS, (first + count) * RING_ROWS)
        weights = weights_ref[:, p * 256 : (p + 1) * 256]
        real = jnp.dot(fields_re[rows, :], weights, preferred_element_type=jnp.float32)
        imag = jnp.dot(fields_im[rows, :], weights, preferred_element_type=jnp.float32)
        for f in range(count):
            re = real[f * RING_ROWS : (f + 1) * RING_ROWS]
            im = imag[f * RING_ROWS : (f + 1) * RING_ROWS]
            term = eigen_ref[0:1, f0 + f : f0 + f + 1] * (re * re + im * im)
            start = term if start is None else start + term
        return start

    parts = COARSE // 256
    for f in range(0, own, 2):
        pair_of_fields(far_ref, f, 0)
    near_copy.wait()
    for p in range(parts):
        for f in range(0, own, 2):
            if p == min(f * parts // own + (f > 0), parts - 1):
                pair_of_fields(near_ref, f, own)
        image_ref[:, p * 256 : (p + 1) * 256] = power(0, own, far_eigen, 0, p, None)
    for p in range(parts):
        at = slice(p * 256, (p + 1) * 256)
        image_ref[:, at] = power(own, own, near_eigen, 0, p, image_ref[:, at])


def dirichlet():
    distance = np.mod(np.arange(N)[None, :] - SPARSE * np.arange(32)[:, None], N)
    turn = np.pi * distance / N
    sine = np.where(distance == 0, 1.0, COARSE * np.sin(turn))
    kernel = np.where(distance % SPARSE == 0, distance == 0, np.sin(COARSE * turn) * np.cos(turn) / sine)
    kernel = kernel.astype(np.float32)
    high = kernel.astype(ml_dtypes.bfloat16)
    low = (kernel - high.astype(np.float32)).astype(ml_dtypes.bfloat16)
    return high, low


def laplace(field):
    rows, cols = field.shape
    return (
        pltpu.roll(field, 1, 0)
        + pltpu.roll(field, rows - 1, 0)
        + pltpu.roll(field, 1, 1)
        + pltpu.roll(field, cols - 1, 1)
        - 4.0 * field
    )


def bake_kernel(
    own_ref, other_ref, high_ref, low_ref, rates, image_hbm, acid_hbm, parts, ring, image_ref, acid_ref, sems
):
    kern = lax.axis_index("kern")
    for p in range(COARSE // 256):
        block = jnp.bitwise_and(p - kern, COARSE // 256 - 1)
        at = pl.ds(pl.multiple_of(block * 256, 256), 256)
        value = own_ref[:, p * 256 : (p + 1) * 256] + other_ref[:, p * 256 : (p + 1) * 256]
        high = value.astype(jnp.bfloat16).astype(jnp.float32)
        parts[0 : 2 * RING_ROWS, at] = jnp.concatenate([high, value - high], 0).astype(jnp.bfloat16)

    def weights(ref, tiles):
        rows = [
            jnp.concatenate([ref[:, ((t - m) % 32) * 128 : ((t - m) % 32) * 128 + 128] for t in tiles], 1)
            for m in range(COARSE // 32)
        ]
        return jnp.concatenate(rows, 0)

    for p in range(5):
        tiles = (2 * p, 2 * p + 1) if p < 4 else (8, 31)
        wide = jnp.dot(parts[0 : 2 * RING_ROWS, :], weights(high_ref, tiles), preferred_element_type=jnp.float32)
        fine = jnp.dot(parts[0:MXU_ROWS, :], weights(low_ref, tiles), preferred_element_type=jnp.float32)
        value = wide[0:RING_ROWS] + (wide[RING_ROWS : 2 * RING_ROWS] + fine[0:RING_ROWS])
        if p < 4:
            ring[:, p * 256 : (p + 1) * 256] = value
        else:
            side = iota((RING_ROWS, 128), 1) < 64
            ring[:, COLS:RING_COLS] = jnp.where(side, value[:, 0:128], value[:, 128:256])

    dill_rate, acid_rate, quench_rate, react_rate, quench_start = (rates[i] for i in range(5))
    aerial_image = ring[...] / FIELDS
    image_ref[...] = aerial_image[0:ROWS, 0:COLS]
    image_copy = pltpu.make_async_copy(image_ref, image_hbm, sems.at[0])
    image_copy.start()
    acid_field = 1.0 - jnp.exp((-4.0 * dill_rate) * aerial_image)
    acid_diffusion = acid_rate * (0.5 + 0.5 * acid_field)
    quencher = jnp.zeros_like(acid_field) + quench_start
    for _ in range(STEPS):
        reaction = (4.0 * react_rate) * acid_field * quencher
        new_acid = acid_field + acid_diffusion * laplace(acid_field) - reaction
        quencher = quencher + quench_rate * laplace(quencher) - reaction
        acid_field = new_acid
    acid_ref[...] = acid_field[0:ROWS, 0:COLS]
    acid_copy = pltpu.make_async_copy(acid_ref, acid_hbm, sems.at[1])
    acid_copy.start()
    image_copy.wait()
    acid_copy.wait()


VMEM = pl.BlockSpec(memory_space=pltpu.VMEM)
SMEM = pl.BlockSpec(memory_space=pltpu.SMEM)
HBM = pl.BlockSpec(memory_space=pltpu.HBM)


def in_hbm(array):
    return pltpu.with_memory_space_constraint(array, pltpu.HBM)


def sum_everywhere(part, beside):
    plane, along_z = plane_groups(), z_groups()
    count = len(plane[0])
    piece = part.shape[0] // count

    def exchange(blocks, groups):
        return lax.all_to_all(blocks, ALL, 0, 0, tiled=True, axis_index_groups=groups)

    def total(blocks):
        return jnp.sum(blocks.reshape(-1, piece, part.shape[1]), 0)

    def copies(block, many):
        return jnp.broadcast_to(block[None], (many,) + block.shape).reshape(-1, block.shape[1])

    blocks = exchange(part, plane)
    some = total(blocks)
    some, beside = lax.optimization_barrier((some, beside))
    full = total(exchange(copies(some, len(along_z[0])), along_z))
    return exchange(copies(full, count), plane), beside


def shards(layout, band_freqs, kernels, eigen_values, bake_rates):
    freqs = band_freqs.reshape(1, W)
    f32 = jnp.float32
    params = pltpu.CompilerParams(vmem_limit_bytes=24 * 2**20)
    far_kernels = lax.ppermute(kernels, ALL, from_next_z(1))
    own = kernels.shape[1]
    part, *tables, near_eigen = pl.pallas_call(
        transform_kernel,
        out_shape=(
            jax.ShapeDtypeStruct((2 * W, W), f32),
            jax.ShapeDtypeStruct((2 * W, COARSE), jnp.bfloat16),
            jax.ShapeDtypeStruct((MXU_ROWS, 2 * W), jnp.bfloat16),
            jax.ShapeDtypeStruct((1, own), f32),
        ),
        in_specs=[HBM] * 3,
        out_specs=(VMEM,) * 4,
        scratch_shapes=[
            pltpu.VMEM((COLS, 4 * W), jnp.bfloat16),
            pltpu.VMEM((ROWS, COLS), jnp.int32),
            pltpu.VMEM((1, W), jnp.int32),
            pltpu.SemaphoreType.DMA((3,)),
        ],
        compiler_params=params,
        name="transform",
    )(in_hbm(layout), in_hbm(freqs), in_hbm(eigen_values.reshape(1, own)))
    far_eigen = lax.ppermute(near_eigen, ALL, from_next_z(-1))
    spectrum, far_eigen = sum_everywhere(part, far_eigen)
    own_image = pl.pallas_call(
        image_kernel,
        out_shape=jax.ShapeDtypeStruct((RING_ROWS, COARSE), f32),
        in_specs=[VMEM, HBM] + [VMEM] * 5,
        out_specs=VMEM,
        scratch_shapes=[
            pltpu.VMEM((2 * own * RING_ROWS, 2 * W), jnp.bfloat16),
            pltpu.VMEM((2 * own * RING_ROWS, 2 * W), jnp.bfloat16),
            pltpu.VMEM(kernels.shape, f32),
            pltpu.SemaphoreType.DMA,
        ],
        compiler_params=params,
        name="image",
    )(spectrum, in_hbm(kernels), far_kernels, *tables, near_eigen, far_eigen)
    across_cores = [(i, i + 64 if (i // 64) % 2 == 0 else i - 64) for i in range(256)]
    other_image = lax.ppermute(own_image, ALL, across_cores)
    block = jax.ShapeDtypeStruct((ROWS, COLS), f32)
    high, low = dirichlet()
    return pl.pallas_call(
        bake_kernel,
        out_shape=(block, block),
        in_specs=[VMEM, VMEM, VMEM, VMEM, SMEM],
        out_specs=(HBM, HBM),
        scratch_shapes=[
            pltpu.VMEM((2 * MXU_ROWS, COARSE), jnp.bfloat16),
            pltpu.VMEM((RING_ROWS, RING_COLS), f32),
            pltpu.VMEM((ROWS, COLS), f32),
            pltpu.VMEM((ROWS, COLS), f32),
            pltpu.SemaphoreType.DMA((2,)),
        ],
        compiler_params=params,
        name="bake",
    )(own_image, other_image, jnp.asarray(high), jnp.asarray(low), bake_rates)


def solution(mesh):
    return jax.shard_map(
        shards,
        mesh=mesh,
        in_specs=(P("slab", "kern"), P(), P(None, "kern", None, None), P("kern"), P()),
        out_specs=(P("slab", "kern"), P("slab", "kern")),
        check_vma=False,
    )
```

```python
import math

import jax
import jax.numpy as jnp
import ml_dtypes
import numpy as np
from jax import lax
from jax.experimental import pallas as pl
from jax.experimental.pallas import tpu as pltpu
from jax.sharding import PartitionSpec as P

N = 4096
W = 128
FIELDS = 48
STEPS = 2

ROWS = 64
COLS = 1024
RING_ROWS = 72
MXU_ROWS = 80
RING_COLS = 1152
SPARSE = 4
COARSE = N // SPARSE
ALL = ("kern", "slab")
CHIP_Z, CORES, FAR_Z, SIDE = 2, 2, 4, 4


def device(z_lo, core, z_hi, y, x):
    return (z_lo * CORES + core) * 64 + (z_hi * SIDE + y) * SIDE + x


def place(i):
    kern, slab = divmod(i, 64)
    return kern // CORES, kern % CORES, slab // SIDE**2, slab // SIDE % SIDE, slab % SIDE


def groups_along(kept):
    groups = {}
    for i in range(256):
        groups.setdefault(tuple(place(i)[axis] for axis in kept), []).append(i)
    return list(groups.values())


def plane_groups():
    return groups_along((0, 2))


def z_groups():
    return groups_along((1, 3, 4))


def from_next_z(side):
    pairs = []
    for i in range(256):
        z_lo, core, z_hi, y, x = place(i)
        z = (z_hi * CHIP_Z + z_lo + (side if z_lo == core else -side)) % (FAR_Z * CHIP_Z)
        pairs.append((device(z % CHIP_Z, core, z // CHIP_Z, y, x), i))
    return pairs


def cos_sin(turns):
    m = jnp.bitwise_and(turns, N - 1)
    quarter = jnp.right_shift(m + N // 8, 10)
    t = (m - jnp.left_shift(quarter, 10)).astype(jnp.float32) * (2.0 * math.pi / N)
    t2 = t * t
    s = t * (1.0 + t2 * (-1.0 / 6 + t2 * (1.0 / 120 + t2 * (-1.0 / 5040 + t2 * (1.0 / 362880)))))
    c = 1.0 + t2 * (-0.5 + t2 * (1.0 / 24 + t2 * (-1.0 / 720 + t2 * (1.0 / 40320))))
    odd = jnp.bitwise_and(quarter, 1) == 1
    cos = jnp.where(odd, s, c)
    sin = jnp.where(odd, c, s)
    cos = jnp.where(jnp.bitwise_and(quarter + 1, 2) == 2, -cos, cos)
    sin = jnp.where(jnp.bitwise_and(quarter, 2) == 2, -sin, sin)
    return cos, sin


def split(values):
    high = values.astype(jnp.bfloat16)
    return high, (values - high.astype(jnp.float32)).astype(jnp.bfloat16)


def iota(shape, dim):
    return lax.broadcasted_iota(jnp.int32, shape, dim)


def image_tables(freqs, weights_ref):
    low_cos, low_sin = cos_sin(SPARSE * iota((8, W), 0) * freqs)
    high_cos, high_sin = cos_sin(SPARSE * 8 * iota((16, W), 0) * freqs)
    turn_cos, turn_sin = cos_sin(jnp.broadcast_to(SPARSE * 128 * freqs, (8, W)))
    cos_parts, sin_parts = [], []
    for a in range(16):
        ca, sa = high_cos[a : a + 1, :], high_sin[a : a + 1, :]
        cos_parts.append(ca * low_cos - sa * low_sin)
        sin_parts.append(sa * low_cos + ca * low_sin)
    cos = jnp.concatenate(cos_parts, 0).T
    sin = jnp.concatenate(sin_parts, 0).T
    turn_cos = jnp.broadcast_to(turn_cos[0:1], (W, W)).T
    turn_sin = jnp.broadcast_to(turn_sin[0:1], (W, W)).T
    for tile in range(COARSE // 128):
        at = slice(tile * 128, tile * 128 + 128)
        weights_ref[0:W, at] = cos.astype(jnp.bfloat16)
        weights_ref[W : 2 * W, at] = sin.astype(jnp.bfloat16)
        cos, sin = cos * turn_cos - sin * turn_sin, sin * turn_cos + cos * turn_sin


def transform_kernel(
    layout_hbm, freqs_hbm, eigen_hbm, out_ref, weights_ref, row_ref, eigen_ref, table, layout_ref, freqs_ref, sems
):
    freqs_copy = pltpu.make_async_copy(freqs_hbm, freqs_ref, sems.at[0])
    layout_copy = pltpu.make_async_copy(layout_hbm, layout_ref, sems.at[1])
    eigen_copy = pltpu.make_async_copy(eigen_hbm, eigen_ref, sems.at[2])
    freqs_copy.start()
    layout_copy.start()
    eigen_copy.start()
    row_first = lax.axis_index("slab") * ROWS
    col_first = lax.axis_index("kern") * COLS
    freqs_copy.wait()
    freqs = freqs_ref[...]
    step = 32
    base_cos, base_sin = cos_sin((col_first + iota((step, W), 0)) * freqs)
    turn_cos, turn_sin = cos_sin((step * iota((COLS // step, W), 0)) * freqs)
    for a in range(COLS // step):
        ca, sa = turn_cos[a : a + 1, :], turn_sin[a : a + 1, :]
        cos = ca * base_cos - sa * base_sin
        sin = sa * base_cos + ca * base_sin
        cos_high, cos_low = split(cos)
        sin_high, sin_low = split(sin)
        at = pl.ds(a * step, step)
        table[at, 0:W] = cos_high
        table[at, W : 2 * W] = sin_high
        table[at, 2 * W : 3 * W] = cos_low
        table[at, 3 * W : 4 * W] = sin_low
    row = iota((MXU_ROWS, W), 0)
    row = jnp.where(row < ROWS + 4, row, row - RING_ROWS)
    cos_row, sin_row = cos_sin((row_first + row) * freqs)
    row_ref[...] = (jnp.concatenate([cos_row, sin_row], 1) / W).astype(jnp.bfloat16)
    left_high, left_low = split(jnp.concatenate([cos_row[0:ROWS], sin_row[0:ROWS]], 0))
    layout_copy.wait()
    transmit = (2 * layout_ref[...] - 1).astype(jnp.float32).astype(jnp.bfloat16)
    along = jnp.dot(transmit, table[...], preferred_element_type=jnp.float32)
    along_re = along[:, 0:W] + along[:, 2 * W : 3 * W]
    along_im = -(along[:, W : 2 * W] + along[:, 3 * W : 4 * W])
    right = jnp.concatenate(
        [
            jnp.concatenate([along_re, along_im], 1),
            jnp.concatenate([along_im, -along_re], 1),
        ],
        0,
    )
    right_high, right_low = split(right)
    both = lax.dot_general(
        jnp.concatenate([left_high, left_high, left_low], 0),
        jnp.concatenate([right_high, right_low, right_high], 0),
        (((0,), (0,)), ((), ())),
        preferred_element_type=jnp.float32,
    ) * (1.0 / N)
    out_ref[0:W, :] = both[:, 0:W]
    out_ref[W : 2 * W, :] = both[:, W : 2 * W]
    image_tables(freqs, weights_ref)
    eigen_copy.wait()


def image_kernel(
    spec_ref, near_hbm, far_ref, weights_ref, row_ref, near_eigen, far_eigen, image_ref,
    fields_re, fields_im, near_ref, sem,
):
    near_copy = pltpu.make_async_copy(near_hbm, near_ref, sem)
    near_copy.start()
    row_table = row_ref[...]
    spec_re = spec_ref[0:W, :]
    spec_im = spec_ref[W : 2 * W, :]
    own = far_ref.shape[1]

    def row_field(kernels_ref, f):
        kern_re = kernels_ref[0, f]
        kern_im = kernels_ref[1, f]
        re16 = (spec_re * kern_re - spec_im * kern_im).astype(jnp.bfloat16)
        im16 = (spec_re * kern_im + spec_im * kern_re).astype(jnp.bfloat16)
        block = jnp.concatenate(
            [jnp.concatenate([re16, im16], 1), jnp.concatenate([-im16, re16], 1)], 0
        )
        part = jnp.dot(row_table, block, preferred_element_type=jnp.float32)
        real = part[0:RING_ROWS, 0:W]
        imag = part[0:RING_ROWS, W : 2 * W]
        return real, imag

    def pair_of_fields(kernels_ref, f, first):
        pair = [row_field(kernels_ref, f), row_field(kernels_ref, f + 1)]
        real = jnp.concatenate([pair[0][0], pair[1][0]], 0).astype(jnp.bfloat16)
        imag = jnp.concatenate([pair[0][1], pair[1][1]], 0).astype(jnp.bfloat16)
        at = slice((first + f) * RING_ROWS, (first + f + 2) * RING_ROWS)
        fields_re[at, 0:W] = real
        fields_re[at, W : 2 * W] = -imag
        fields_im[at, 0:W] = imag
        fields_im[at, W : 2 * W] = real

    def power(first, count, eigen_ref, f0, p, start):
        rows = slice(first * RING_ROWS, (first + count) * RING_ROWS)
        weights = weights_ref[:, p * 256 : (p + 1) * 256]
        real = jnp.dot(fields_re[rows, :], weights, preferred_element_type=jnp.float32)
        imag = jnp.dot(fields_im[rows, :], weights, preferred_element_type=jnp.float32)
        for f in range(count):
            re = real[f * RING_ROWS : (f + 1) * RING_ROWS]
            im = imag[f * RING_ROWS : (f + 1) * RING_ROWS]
            term = eigen_ref[0:1, f0 + f : f0 + f + 1] * (re * re + im * im)
            start = term if start is None else start + term
        return start

    parts = COARSE // 256
    for f in range(0, own, 2):
        pair_of_fields(far_ref, f, 0)
    near_copy.wait()
    for p in range(parts):
        for f in range(0, own, 2):
            if p == min(f * parts // own + (f > 0), parts - 1):
                pair_of_fields(near_ref, f, own)
        image_ref[:, p * 256 : (p + 1) * 256] = power(0, own, far_eigen, 0, p, None)
    for p in range(parts):
        at = slice(p * 256, (p + 1) * 256)
        image_ref[:, at] = power(own, own, near_eigen, 0, p, image_ref[:, at])


def dirichlet():
    distance = np.mod(np.arange(N)[None, :] - SPARSE * np.arange(32)[:, None], N)
    turn = np.pi * distance / N
    sine = np.where(distance == 0, 1.0, COARSE * np.sin(turn))
    kernel = np.where(distance % SPARSE == 0, distance == 0, np.sin(COARSE * turn) * np.cos(turn) / sine)
    kernel = kernel.astype(np.float32)
    high = kernel.astype(ml_dtypes.bfloat16)
    low = (kernel - high.astype(np.float32)).astype(ml_dtypes.bfloat16)
    return high, low


def laplace(field):
    rows, cols = field.shape
    return (
        pltpu.roll(field, 1, 0)
        + pltpu.roll(field, rows - 1, 0)
        + pltpu.roll(field, 1, 1)
        + pltpu.roll(field, cols - 1, 1)
        - 4.0 * field
    )


def bake_kernel(
    own_ref, other_ref, high_ref, low_ref, rates, image_hbm, acid_hbm, parts, ring, image_ref, acid_ref, sems
):
    kern = lax.axis_index("kern")
    for p in range(COARSE // 256):
        block = jnp.bitwise_and(p - kern, COARSE // 256 - 1)
        at = pl.ds(pl.multiple_of(block * 256, 256), 256)
        value = own_ref[:, p * 256 : (p + 1) * 256] + other_ref[:, p * 256 : (p + 1) * 256]
        high = value.astype(jnp.bfloat16).astype(jnp.float32)
        parts[0 : 2 * RING_ROWS, at] = jnp.concatenate([high, value - high], 0).astype(jnp.bfloat16)

    def weights(ref, tiles):
        rows = [
            jnp.concatenate([ref[:, ((t - m) % 32) * 128 : ((t - m) % 32) * 128 + 128] for t in tiles], 1)
            for m in range(COARSE // 32)
        ]
        return jnp.concatenate(rows, 0)

    for p in range(5):
        tiles = (2 * p, 2 * p + 1) if p < 4 else (8, 31)
        wide = jnp.dot(parts[0 : 2 * RING_ROWS, :], weights(high_ref, tiles), preferred_element_type=jnp.float32)
        fine = jnp.dot(parts[0:MXU_ROWS, :], weights(low_ref, tiles), preferred_element_type=jnp.float32)
        value = wide[0:RING_ROWS] + (wide[RING_ROWS : 2 * RING_ROWS] + fine[0:RING_ROWS])
        if p < 4:
            ring[:, p * 256 : (p + 1) * 256] = value
        else:
            side = iota((RING_ROWS, 128), 1) < 64
            ring[:, COLS:RING_COLS] = jnp.where(side, value[:, 0:128], value[:, 128:256])

    dill_rate, acid_rate, quench_rate, react_rate, quench_start = (rates[i] for i in range(5))
    aerial_image = ring[...] / FIELDS
    image_ref[...] = aerial_image[0:ROWS, 0:COLS]
    image_copy = pltpu.make_async_copy(image_ref, image_hbm, sems.at[0])
    image_copy.start()
    acid_field = 1.0 - jnp.exp((-4.0 * dill_rate) * aerial_image)
    acid_diffusion = acid_rate * (0.5 + 0.5 * acid_field)
    quencher = jnp.zeros_like(acid_field) + quench_start
    for _ in range(STEPS):
        reaction = (4.0 * react_rate) * acid_field * quencher
        new_acid = acid_field + acid_diffusion * laplace(acid_field) - reaction
        quencher = quencher + quench_rate * laplace(quencher) - reaction
        acid_field = new_acid
    acid_ref[...] = acid_field[0:ROWS, 0:COLS]
    acid_copy = pltpu.make_async_copy(acid_ref, acid_hbm, sems.at[1])
    acid_copy.start()
    image_copy.wait()
    acid_copy.wait()


VMEM = pl.BlockSpec(memory_space=pltpu.VMEM)
SMEM = pl.BlockSpec(memory_space=pltpu.SMEM)
HBM = pl.BlockSpec(memory_space=pltpu.HBM)


def in_hbm(array):
    return pltpu.with_memory_space_constraint(array, pltpu.HBM)


def sum_everywhere(part, eigen):
    plane, along_z = plane_groups(), z_groups()
    count = len(plane[0])
    piece = part.shape[0] // count

    def exchange(blocks, groups):
        return lax.all_to_all(blocks, ALL, 0, 0, tiled=True, axis_index_groups=groups)

    def total(blocks):
        return jnp.sum(blocks.reshape(-1, piece, part.shape[1]), 0)

    def copies(block, many):
        return jnp.broadcast_to(block[None], (many,) + block.shape).reshape(-1, block.shape[1])

    some, eigen = lax.optimization_barrier((total(exchange(part, plane)), eigen))
    far_eigen = lax.ppermute(eigen, ALL, from_next_z(-1))
    blocks = exchange(copies(some, len(along_z[0])), along_z)
    full = total(blocks)
    full, far_eigen = lax.optimization_barrier((full, far_eigen))
    return exchange(copies(full, count), plane), far_eigen


def shards(layout, band_freqs, kernels, eigen_values, bake_rates):
    freqs = band_freqs.reshape(1, W)
    f32 = jnp.float32
    params = pltpu.CompilerParams(vmem_limit_bytes=24 * 2**20)
    far_kernels = lax.ppermute(kernels, ALL, from_next_z(1))
    own = kernels.shape[1]
    part, *tables, near_eigen = pl.pallas_call(
        transform_kernel,
        out_shape=(
            jax.ShapeDtypeStruct((2 * W, W), f32),
            jax.ShapeDtypeStruct((2 * W, COARSE), jnp.bfloat16),
            jax.ShapeDtypeStruct((MXU_ROWS, 2 * W), jnp.bfloat16),
            jax.ShapeDtypeStruct((1, own), f32),
        ),
        in_specs=[HBM] * 3,
        out_specs=(VMEM,) * 4,
        scratch_shapes=[
            pltpu.VMEM((COLS, 4 * W), jnp.bfloat16),
            pltpu.VMEM((ROWS, COLS), jnp.int32),
            pltpu.VMEM((1, W), jnp.int32),
            pltpu.SemaphoreType.DMA((3,)),
        ],
        compiler_params=params,
        name="transform",
    )(in_hbm(layout), in_hbm(freqs), in_hbm(eigen_values.reshape(1, own)))
    spectrum, far_eigen = sum_everywhere(part, near_eigen)
    own_image = pl.pallas_call(
        image_kernel,
        out_shape=jax.ShapeDtypeStruct((RING_ROWS, COARSE), f32),
        in_specs=[VMEM, HBM] + [VMEM] * 5,
        out_specs=VMEM,
        scratch_shapes=[
            pltpu.VMEM((2 * own * RING_ROWS, 2 * W), jnp.bfloat16),
            pltpu.VMEM((2 * own * RING_ROWS, 2 * W), jnp.bfloat16),
            pltpu.VMEM(kernels.shape, f32),
            pltpu.SemaphoreType.DMA,
        ],
        compiler_params=params,
        name="image",
    )(spectrum, in_hbm(kernels), far_kernels, *tables, near_eigen, far_eigen)
    across_cores = [(i, i + 64 if (i // 64) % 2 == 0 else i - 64) for i in range(256)]
    other_image = lax.ppermute(own_image, ALL, across_cores)
    block = jax.ShapeDtypeStruct((ROWS, COLS), f32)
    high, low = dirichlet()
    return pl.pallas_call(
        bake_kernel,
        out_shape=(block, block),
        in_specs=[VMEM, VMEM, VMEM, VMEM, SMEM],
        out_specs=(HBM, HBM),
        scratch_shapes=[
            pltpu.VMEM((2 * MXU_ROWS, COARSE), jnp.bfloat16),
            pltpu.VMEM((RING_ROWS, RING_COLS), f32),
            pltpu.VMEM((ROWS, COLS), f32),
            pltpu.VMEM((ROWS, COLS), f32),
            pltpu.SemaphoreType.DMA((2,)),
        ],
        compiler_params=params,
        name="bake",
    )(own_image, other_image, jnp.asarray(high), jnp.asarray(low), bake_rates)


def solution(mesh):
    return jax.shard_map(
        shards,
        mesh=mesh,
        in_specs=(P("slab", "kern"), P(), P(None, "kern", None, None), P("kern"), P()),
        out_specs=(P("slab", "kern"), P("slab", "kern")),
        check_vma=False,
    )
```

```python
import math

import jax
import jax.numpy as jnp
import ml_dtypes
import numpy as np
from jax import lax
from jax.experimental import pallas as pl
from jax.experimental.pallas import tpu as pltpu
from jax.sharding import PartitionSpec as P

N = 4096
W = 128
FIELDS = 48
STEPS = 2

ROWS = 64
COLS = 1024
RING_ROWS = 72
MXU_ROWS = 80
RING_COLS = 1152
SPARSE = 4
COARSE = N // SPARSE
NEAR_BLOCKS = ((0, 3), (0,), (0,), (0, 1), (0, 1, 3))
ALL = ("kern", "slab")
CHIP_Z, CORES, FAR_Z, SIDE = 2, 2, 4, 4


def device(z_lo, core, z_hi, y, x):
    return (z_lo * CORES + core) * 64 + (z_hi * SIDE + y) * SIDE + x


def place(i):
    kern, slab = divmod(i, 64)
    return kern // CORES, kern % CORES, slab // SIDE**2, slab // SIDE % SIDE, slab % SIDE


def groups_along(kept):
    groups = {}
    for i in range(256):
        groups.setdefault(tuple(place(i)[axis] for axis in kept), []).append(i)
    return list(groups.values())


def plane_groups():
    return groups_along((0, 2))


def z_groups():
    return groups_along((1, 3, 4))


def from_next_z(side):
    pairs = []
    for i in range(256):
        z_lo, core, z_hi, y, x = place(i)
        z = (z_hi * CHIP_Z + z_lo + (side if z_lo == core else -side)) % (FAR_Z * CHIP_Z)
        pairs.append((device(z % CHIP_Z, core, z // CHIP_Z, y, x), i))
    return pairs


def cos_sin(turns):
    m = jnp.bitwise_and(turns, N - 1)
    quarter = jnp.right_shift(m + N // 8, 10)
    t = (m - jnp.left_shift(quarter, 10)).astype(jnp.float32) * (2.0 * math.pi / N)
    t2 = t * t
    s = t * (1.0 + t2 * (-1.0 / 6 + t2 * (1.0 / 120 + t2 * (-1.0 / 5040 + t2 * (1.0 / 362880)))))
    c = 1.0 + t2 * (-0.5 + t2 * (1.0 / 24 + t2 * (-1.0 / 720 + t2 * (1.0 / 40320))))
    odd = jnp.bitwise_and(quarter, 1) == 1
    cos = jnp.where(odd, s, c)
    sin = jnp.where(odd, c, s)
    cos = jnp.where(jnp.bitwise_and(quarter + 1, 2) == 2, -cos, cos)
    sin = jnp.where(jnp.bitwise_and(quarter, 2) == 2, -sin, sin)
    return cos, sin


def split(values):
    high = values.astype(jnp.bfloat16)
    return high, (values - high.astype(jnp.float32)).astype(jnp.bfloat16)


def iota(shape, dim):
    return lax.broadcasted_iota(jnp.int32, shape, dim)


def image_tables(freqs, weights_ref):
    low_cos, low_sin = cos_sin(SPARSE * iota((8, W), 0) * freqs)
    high_cos, high_sin = cos_sin(SPARSE * 8 * iota((16, W), 0) * freqs)
    turn_cos, turn_sin = cos_sin(jnp.broadcast_to(SPARSE * 128 * freqs, (8, W)))
    cos_parts, sin_parts = [], []
    for a in range(16):
        ca, sa = high_cos[a : a + 1, :], high_sin[a : a + 1, :]
        cos_parts.append(ca * low_cos - sa * low_sin)
        sin_parts.append(sa * low_cos + ca * low_sin)
    cos = jnp.concatenate(cos_parts, 0).T
    sin = jnp.concatenate(sin_parts, 0).T
    turn_cos = jnp.broadcast_to(turn_cos[0:1], (W, W)).T
    turn_sin = jnp.broadcast_to(turn_sin[0:1], (W, W)).T
    for start in range(0, W, 32):
        rows = slice(start, start + 32)
        c, s, tc, ts = cos[rows], sin[rows], turn_cos[rows], turn_sin[rows]
        for tile in range(COARSE // 128):
            at = slice(tile * 128, tile * 128 + 128)
            weights_ref[rows, at] = c.astype(jnp.bfloat16)
            weights_ref[W + start : W + start + 32, at] = s.astype(jnp.bfloat16)
            c, s = c * tc - s * ts, s * tc + c * ts


def transform_kernel(
    layout_hbm, freqs_hbm, eigen_hbm, out_ref, weights_ref, row_ref, eigen_ref, table, layout_ref, freqs_ref, eigen_row,
    sems,
):
    freqs_copy = pltpu.make_async_copy(freqs_hbm, freqs_ref, sems.at[0])
    layout_copy = pltpu.make_async_copy(layout_hbm, layout_ref, sems.at[1])
    eigen_copy = pltpu.make_async_copy(eigen_hbm, eigen_row, sems.at[2])
    freqs_copy.start()
    layout_copy.start()
    eigen_copy.start()
    eigen_ref[...] = jnp.zeros_like(eigen_ref)
    row_first = lax.axis_index("slab") * ROWS
    col_first = lax.axis_index("kern") * COLS
    freqs_copy.wait()
    freqs = freqs_ref[...]
    step = 32
    base_cos, base_sin = cos_sin((col_first + iota((step, W), 0)) * freqs)
    turn_cos, turn_sin = cos_sin((step * iota((COLS // step, W), 0)) * freqs)
    for a in range(COLS // step):
        ca, sa = turn_cos[a : a + 1, :], turn_sin[a : a + 1, :]
        cos = ca * base_cos - sa * base_sin
        sin = sa * base_cos + ca * base_sin
        cos_high, cos_low = split(cos)
        sin_high, sin_low = split(sin)
        at = pl.ds(a * step, step)
        table[at, 0:W] = cos_high
        table[at, W : 2 * W] = sin_high
        table[at, 2 * W : 3 * W] = cos_low
        table[at, 3 * W : 4 * W] = sin_low
    row = iota((MXU_ROWS, W), 0)
    row = jnp.where(row < ROWS + 4, row, row - RING_ROWS)
    cos_row, sin_row = cos_sin((row_first + row) * freqs)
    row_ref[...] = (jnp.concatenate([cos_row, sin_row], 1) / W).astype(jnp.bfloat16)
    left_high, left_low = split(jnp.concatenate([cos_row[0:ROWS], sin_row[0:ROWS]], 0))
    layout_copy.wait()
    transmit = (2 * layout_ref[...] - 1).astype(jnp.float32).astype(jnp.bfloat16)
    along = jnp.dot(transmit, table[...], preferred_element_type=jnp.float32)
    along_re = along[:, 0:W] + along[:, 2 * W : 3 * W]
    along_im = -(along[:, W : 2 * W] + along[:, 3 * W : 4 * W])
    right = jnp.concatenate(
        [
            jnp.concatenate([along_re, along_im], 1),
            jnp.concatenate([along_im, -along_re], 1),
        ],
        0,
    )
    right_high, right_low = split(right)
    both = lax.dot_general(
        jnp.concatenate([left_high, left_high, left_low], 0),
        jnp.concatenate([right_high, right_low, right_high], 0),
        (((0,), (0,)), ((), ())),
        preferred_element_type=jnp.float32,
    ) * (1.0 / N)
    out_ref[0:W, :] = both[:, 0:W]
    out_ref[W : 2 * W, :] = both[:, W : 2 * W]
    image_tables(freqs, weights_ref)
    eigen_copy.wait()
    eigen_ref[0:1, 0 : eigen_row.shape[1]] = eigen_row[...]


def image_kernel(
    spec_ref, near_hbm, far_ref, weights_ref, row_ref, along_z_ref, image_ref,
    fields_re, fields_im, near_ref, sem,
):
    near_copy = pltpu.make_async_copy(near_hbm, near_ref, sem)
    near_copy.start()
    even_eigen = along_z_ref[8:9, :]
    odd_eigen = along_z_ref[FAR_Z * 16 + 8 : FAR_Z * 16 + 9, :]
    odd = lax.axis_index("kern") // CORES == 1
    near_eigen = jnp.where(odd, odd_eigen, even_eigen)
    far_eigen = jnp.where(odd, even_eigen, odd_eigen)
    row_table = row_ref[...]
    spec_re = spec_ref[0:W, :]
    spec_im = spec_ref[W : 2 * W, :]
    own = far_ref.shape[1]

    def row_field(kernels_ref, f):
        kern_re = kernels_ref[0, f]
        kern_im = kernels_ref[1, f]
        re16 = (spec_re * kern_re - spec_im * kern_im).astype(jnp.bfloat16)
        im16 = (spec_re * kern_im + spec_im * kern_re).astype(jnp.bfloat16)
        block = jnp.concatenate(
            [jnp.concatenate([re16, im16], 1), jnp.concatenate([-im16, re16], 1)], 0
        )
        part = jnp.dot(row_table, block, preferred_element_type=jnp.float32)
        real = part[0:RING_ROWS, 0:W]
        imag = part[0:RING_ROWS, W : 2 * W]
        return real, imag

    def pair_of_fields(kernels_ref, f, first):
        pair = [row_field(kernels_ref, f), row_field(kernels_ref, f + 1)]
        real = jnp.concatenate([pair[0][0], pair[1][0]], 0).astype(jnp.bfloat16)
        imag = jnp.concatenate([pair[0][1], pair[1][1]], 0).astype(jnp.bfloat16)
        at = slice((first + f) * RING_ROWS, (first + f + 2) * RING_ROWS)
        fields_re[at, 0:W] = real
        fields_re[at, W : 2 * W] = -imag
        fields_im[at, 0:W] = imag
        fields_im[at, W : 2 * W] = real

    def power(first, count, eigen_row, f0, p, start):
        rows = slice(first * RING_ROWS, (first + count) * RING_ROWS)
        weights = weights_ref[:, p * 256 : (p + 1) * 256]
        real = jnp.dot(fields_re[rows, :], weights, preferred_element_type=jnp.float32)
        imag = jnp.dot(fields_im[rows, :], weights, preferred_element_type=jnp.float32)
        for f in range(count):
            re = real[f * RING_ROWS : (f + 1) * RING_ROWS]
            im = imag[f * RING_ROWS : (f + 1) * RING_ROWS]
            term = eigen_row[0:1, f0 + f : f0 + f + 1] * (re * re + im * im)
            start = term if start is None else start + term
        return start

    parts = COARSE // 256
    for f in range(0, own, 2):
        pair_of_fields(far_ref, f, 0)
    near_copy.wait()
    for p in range(parts):
        for f in range(0, own, 2):
            if p == min(f * parts // own + (f > 0), parts - 1):
                pair_of_fields(near_ref, f, own)
        image_ref[:, p * 256 : (p + 1) * 256] = power(0, own, far_eigen, 0, p, None)
    for p in range(parts):
        at = slice(p * 256, (p + 1) * 256)
        image_ref[:, at] = power(own, own, near_eigen, 0, p, image_ref[:, at])


def dirichlet():
    distance = np.mod(np.arange(N)[None, :] - SPARSE * np.arange(32)[:, None], N)
    turn = np.pi * distance / N
    sine = np.where(distance == 0, 1.0, COARSE * np.sin(turn))
    kernel = np.where(distance % SPARSE == 0, distance == 0, np.sin(COARSE * turn) * np.cos(turn) / sine)
    kernel = kernel.astype(np.float32)
    high = kernel.astype(ml_dtypes.bfloat16)
    low = (kernel - high.astype(np.float32)).astype(ml_dtypes.bfloat16)
    return high, low


def laplace(field):
    rows, cols = field.shape
    return (
        pltpu.roll(field, 1, 0)
        + pltpu.roll(field, rows - 1, 0)
        + pltpu.roll(field, 1, 1)
        + pltpu.roll(field, cols - 1, 1)
        - 4.0 * field
    )


def bake_kernel(
    own_ref, other_ref, high_ref, low_ref, rates, image_hbm, acid_hbm, parts, ring, image_ref, acid_ref, sems
):
    kern = lax.axis_index("kern")
    for p in range(COARSE // 256):
        block = jnp.bitwise_and(p - kern, COARSE // 256 - 1)
        at = pl.ds(pl.multiple_of(block * 256, 256), 256)
        value = own_ref[:, p * 256 : (p + 1) * 256] + other_ref[:, p * 256 : (p + 1) * 256]
        high = value.astype(jnp.bfloat16).astype(jnp.float32)
        parts[0 : 2 * RING_ROWS, at] = jnp.concatenate([high, value - high], 0).astype(jnp.bfloat16)

    def weights(ref, tiles, blocks):
        rows = [
            jnp.concatenate([ref[:, ((t - m) % 32) * 128 : ((t - m) % 32) * 128 + 128] for t in tiles], 1)
            for block in blocks
            for m in range(8 * block, 8 * block + 8)
        ]
        return jnp.concatenate(rows, 0)

    everywhere = range(COARSE // 256)
    for p in range(5):
        tiles = (2 * p, 2 * p + 1) if p < 4 else (8, 31)
        wide = jnp.dot(
            parts[0 : 2 * RING_ROWS, :], weights(high_ref, tiles, everywhere), preferred_element_type=jnp.float32
        )
        fine = sum(
            jnp.dot(
                parts[0:MXU_ROWS, block * 256 : (block + 1) * 256],
                weights(low_ref, tiles, (block,)),
                preferred_element_type=jnp.float32,
            )
            for block in NEAR_BLOCKS[p]
        )
        value = wide[0:RING_ROWS] + (wide[RING_ROWS : 2 * RING_ROWS] + fine[0:RING_ROWS])
        if p < 4:
            ring[:, p * 256 : (p + 1) * 256] = value
        else:
            side = iota((RING_ROWS, 128), 1) < 64
            ring[:, COLS:RING_COLS] = jnp.where(side, value[:, 0:128], value[:, 128:256])

    dill_rate, acid_rate, quench_rate, react_rate, quench_start = (rates[i] for i in range(5))
    aerial_image = ring[...] / FIELDS
    image_ref[...] = aerial_image[0:ROWS, 0:COLS]
    image_copy = pltpu.make_async_copy(image_ref, image_hbm, sems.at[0])
    image_copy.start()
    acid_field = 1.0 - jnp.exp((-4.0 * dill_rate) * aerial_image)
    acid_diffusion = acid_rate * (0.5 + 0.5 * acid_field)
    quencher = jnp.zeros_like(acid_field) + quench_start
    for bake_step in range(STEPS):
        reaction = (4.0 * react_rate) * acid_field * quencher
        new_acid = acid_field + acid_diffusion * laplace(acid_field) - reaction
        quencher = quencher + quench_rate * laplace(quencher) - reaction
        acid_field = new_acid
    acid_ref[...] = acid_field[0:ROWS, 0:COLS]
    acid_copy = pltpu.make_async_copy(acid_ref, acid_hbm, sems.at[1])
    acid_copy.start()
    image_copy.wait()
    acid_copy.wait()


VMEM = pl.BlockSpec(memory_space=pltpu.VMEM)
SMEM = pl.BlockSpec(memory_space=pltpu.SMEM)
HBM = pl.BlockSpec(memory_space=pltpu.HBM)


def in_hbm(array):
    return pltpu.with_memory_space_constraint(array, pltpu.HBM)


def sum_everywhere(part, beside):
    plane, along_z = plane_groups(), z_groups()
    count, piece = len(plane[0]), part.shape[0] // len(plane[0])

    def exchange(blocks, groups):
        return lax.all_to_all(blocks, ALL, 0, 0, tiled=True, axis_index_groups=groups)

    def copies(block, many):
        return jnp.broadcast_to(block[None], (many,) + block.shape).reshape(-1, block.shape[1])

    some = jnp.sum(exchange(part, plane).reshape(count, piece, -1), 0)
    brought = exchange(copies(jnp.concatenate([some, beside], 0), len(along_z[0])), along_z)
    full = jnp.sum(brought.reshape(len(along_z[0]), 2 * piece, -1)[:, :piece], 0)
    return exchange(copies(full, count), plane), brought


def shards(layout, band_freqs, kernels, eigen_values, bake_rates):
    freqs = band_freqs.reshape(1, W)
    f32 = jnp.float32
    params = pltpu.CompilerParams(vmem_limit_bytes=24 * 2**20)
    far_kernels = lax.ppermute(kernels, ALL, from_next_z(1))
    own = kernels.shape[1]
    part, *tables, eigen_tile = pl.pallas_call(
        transform_kernel,
        out_shape=(
            jax.ShapeDtypeStruct((2 * W, W), f32),
            jax.ShapeDtypeStruct((2 * W, COARSE), jnp.bfloat16),
            jax.ShapeDtypeStruct((MXU_ROWS, 2 * W), jnp.bfloat16),
            jax.ShapeDtypeStruct((8, W), f32),
        ),
        in_specs=[HBM] * 3,
        out_specs=(VMEM,) * 4,
        scratch_shapes=[
            pltpu.VMEM((COLS, 4 * W), jnp.bfloat16),
            pltpu.VMEM((ROWS, COLS), jnp.int32),
            pltpu.VMEM((1, W), jnp.int32),
            pltpu.VMEM((1, own), f32),
            pltpu.SemaphoreType.DMA((3,)),
        ],
        compiler_params=params,
        name="transform",
    )(in_hbm(layout), in_hbm(freqs), in_hbm(eigen_values.reshape(1, own)))
    spectrum, along_z = sum_everywhere(part, eigen_tile)
    own_image = pl.pallas_call(
        image_kernel,
        out_shape=jax.ShapeDtypeStruct((RING_ROWS, COARSE), f32),
        in_specs=[VMEM, HBM] + [VMEM] * 4,
        out_specs=VMEM,
        scratch_shapes=[
            pltpu.VMEM((2 * own * RING_ROWS, 2 * W), jnp.bfloat16),
            pltpu.VMEM((2 * own * RING_ROWS, 2 * W), jnp.bfloat16),
            pltpu.VMEM(kernels.shape, f32),
            pltpu.SemaphoreType.DMA,
        ],
        compiler_params=params,
        name="image",
    )(spectrum, in_hbm(kernels), far_kernels, *tables, along_z)
    across_cores = [(i, i + 64 if (i // 64) % 2 == 0 else i - 64) for i in range(256)]
    other_image = lax.ppermute(own_image, ALL, across_cores)
    block = jax.ShapeDtypeStruct((ROWS, COLS), f32)
    high, low = dirichlet()
    return pl.pallas_call(
        bake_kernel,
        out_shape=(block, block),
        in_specs=[VMEM, VMEM, VMEM, VMEM, SMEM],
        out_specs=(HBM, HBM),
        scratch_shapes=[
            pltpu.VMEM((2 * MXU_ROWS, COARSE), jnp.bfloat16),
            pltpu.VMEM((RING_ROWS, RING_COLS), f32),
            pltpu.VMEM((ROWS, COLS), f32),
            pltpu.VMEM((ROWS, COLS), f32),
            pltpu.SemaphoreType.DMA((2,)),
        ],
        compiler_params=params,
        name="bake",
    )(own_image, other_image, jnp.asarray(high), jnp.asarray(low), bake_rates)


def solution(mesh):
    return jax.shard_map(
        shards,
        mesh=mesh,
        in_specs=(P("slab", "kern"), P(), P(None, "kern", None, None), P("kern"), P()),
        out_specs=(P("slab", "kern"), P("slab", "kern")),
        check_vma=False,
    )
```

```python
import math

import jax
import jax.numpy as jnp
import ml_dtypes
import numpy as np
from jax import lax
from jax.experimental import pallas as pl
from jax.experimental.pallas import tpu as pltpu
from jax.sharding import PartitionSpec as P

N = 4096
W = 128
FIELDS = 48
STEPS = 2

ROWS = 64
COLS = 1024
RING_ROWS = 72
MXU_ROWS = 80
RING_COLS = 1152
SPARSE = 4
COARSE = N // SPARSE
NEAR_BLOCKS = ((0, 3), (0,), (0,), (0, 1), (0, 1, 3))
ALL = ("kern", "slab")
CHIP_Z, CORES, FAR_Z, SIDE = 2, 2, 4, 4


def device(z_lo, core, z_hi, y, x):
    return (z_lo * CORES + core) * 64 + (z_hi * SIDE + y) * SIDE + x


def place(i):
    kern, slab = divmod(i, 64)
    return kern // CORES, kern % CORES, slab // SIDE**2, slab // SIDE % SIDE, slab % SIDE


def groups_along(kept):
    groups = {}
    for i in range(256):
        groups.setdefault(tuple(place(i)[axis] for axis in kept), []).append(i)
    return list(groups.values())


def plane_groups():
    return groups_along((0, 2))


def z_groups():
    return groups_along((1, 3, 4))


def from_next_z(side):
    pairs = []
    for i in range(256):
        z_lo, core, z_hi, y, x = place(i)
        z = (z_hi * CHIP_Z + z_lo + (side if z_lo == core else -side)) % (FAR_Z * CHIP_Z)
        pairs.append((device(z % CHIP_Z, core, z // CHIP_Z, y, x), i))
    return pairs


def cos_sin(turns):
    m = jnp.bitwise_and(turns, N - 1)
    quarter = jnp.right_shift(m + N // 8, 10)
    t = (m - jnp.left_shift(quarter, 10)).astype(jnp.float32) * (2.0 * math.pi / N)
    t2 = t * t
    s = t * (1.0 + t2 * (-1.0 / 6 + t2 * (1.0 / 120 + t2 * (-1.0 / 5040 + t2 * (1.0 / 362880)))))
    c = 1.0 + t2 * (-0.5 + t2 * (1.0 / 24 + t2 * (-1.0 / 720 + t2 * (1.0 / 40320))))
    odd = jnp.bitwise_and(quarter, 1) == 1
    cos = jnp.where(odd, s, c)
    sin = jnp.where(odd, c, s)
    cos = jnp.where(jnp.bitwise_and(quarter + 1, 2) == 2, -cos, cos)
    sin = jnp.where(jnp.bitwise_and(quarter, 2) == 2, -sin, sin)
    return cos, sin


def split(values):
    high = values.astype(jnp.bfloat16)
    return high, (values - high.astype(jnp.float32)).astype(jnp.bfloat16)


def iota(shape, dim):
    return lax.broadcasted_iota(jnp.int32, shape, dim)


def image_tables(freqs, weights_ref):
    low_cos, low_sin = cos_sin(SPARSE * iota((8, W), 0) * freqs)
    high_cos, high_sin = cos_sin(SPARSE * 8 * iota((16, W), 0) * freqs)
    turn_cos, turn_sin = cos_sin(jnp.broadcast_to(SPARSE * 128 * freqs, (8, W)))
    cos_parts, sin_parts = [], []
    for a in range(16):
        ca, sa = high_cos[a : a + 1, :], high_sin[a : a + 1, :]
        cos_parts.append(ca * low_cos - sa * low_sin)
        sin_parts.append(sa * low_cos + ca * low_sin)
    cos = jnp.concatenate(cos_parts, 0).T
    sin = jnp.concatenate(sin_parts, 0).T
    turn_cos = jnp.broadcast_to(turn_cos[0:1], (W, W)).T
    turn_sin = jnp.broadcast_to(turn_sin[0:1], (W, W)).T
    for start in range(0, W, 32):
        rows = slice(start, start + 32)
        c, s, tc, ts = cos[rows], sin[rows], turn_cos[rows], turn_sin[rows]
        for tile in range(COARSE // 128):
            at = slice(tile * 128, tile * 128 + 128)
            weights_ref[rows, at] = c.astype(jnp.bfloat16)
            weights_ref[W + start : W + start + 32, at] = s.astype(jnp.bfloat16)
            c, s = c * tc - s * ts, s * tc + c * ts


def transform_kernel(
    layout_hbm, freqs_hbm, eigen_hbm, out_ref, weights_ref, row_ref, eigen_ref, table, layout_ref, freqs_ref, eigen_row,
    sems,
):
    freqs_copy = pltpu.make_async_copy(freqs_hbm, freqs_ref, sems.at[0])
    layout_copy = pltpu.make_async_copy(layout_hbm, layout_ref, sems.at[1])
    eigen_copy = pltpu.make_async_copy(eigen_hbm, eigen_row, sems.at[2])
    freqs_copy.start()
    layout_copy.start()
    eigen_copy.start()
    eigen_ref[...] = jnp.zeros_like(eigen_ref)
    row_first = lax.axis_index("slab") * ROWS
    col_first = lax.axis_index("kern") * COLS
    freqs_copy.wait()
    freqs = freqs_ref[...]
    step, quarter = 32, COLS // 4
    base_cos, base_sin = cos_sin((col_first + iota((step, W), 0)) * freqs)
    turn_cos, turn_sin = cos_sin((step * iota((quarter // step, W), 0)) * freqs)
    join_cos, join_sin = cos_sin((quarter * iota((8, W), 0)) * freqs)
    for a in range(quarter // step):
        ca, sa = turn_cos[a : a + 1, :], turn_sin[a : a + 1, :]
        cos = ca * base_cos - sa * base_sin
        sin = sa * base_cos + ca * base_sin
        cos_high, cos_low = split(cos)
        sin_high, sin_low = split(sin)
        at = pl.ds(a * step, step)
        table[at, 0:W] = cos_high
        table[at, W : 2 * W] = sin_high
        table[at, 2 * W : 3 * W] = cos_low
        table[at, 3 * W : 4 * W] = sin_low
    row = iota((MXU_ROWS, W), 0)
    row = jnp.where(row < ROWS + 4, row, row - RING_ROWS)
    cos_row, sin_row = cos_sin((row_first + row) * freqs)
    row_ref[...] = (jnp.concatenate([cos_row, sin_row], 1) / W).astype(jnp.bfloat16)
    left_high, left_low = split(jnp.concatenate([cos_row[0:ROWS], sin_row[0:ROWS]], 0).T)
    left = jnp.concatenate([left_high, left_high, left_low], 1)
    image_tables(freqs, weights_ref)
    layout_copy.wait()
    transmit = (2 * layout_ref[...] - 1).astype(jnp.float32).astype(jnp.bfloat16)
    stacked = jnp.concatenate([transmit[:, h * quarter : (h + 1) * quarter] for h in range(4)], 0)
    along = jnp.dot(stacked, table[...], preferred_element_type=jnp.float32)
    along_cos = along[:, 0:W] + along[:, 2 * W : 3 * W]
    along_sin = along[:, W : 2 * W] + along[:, 3 * W : 4 * W]
    along_re, along_im = along_cos[0:ROWS], -along_sin[0:ROWS]
    for h in range(1, 4):
        c, s = along_cos[h * ROWS : (h + 1) * ROWS], along_sin[h * ROWS : (h + 1) * ROWS]
        jc, js = join_cos[h : h + 1, :], join_sin[h : h + 1, :]
        along_re = along_re + (jc * c - js * s)
        along_im = along_im - (jc * s + js * c)
    right = jnp.concatenate(
        [
            jnp.concatenate([along_re, along_im], 1),
            jnp.concatenate([along_im, -along_re], 1),
        ],
        0,
    )
    right_high, right_low = split(right)
    both = jnp.dot(
        left,
        jnp.concatenate([right_high, right_low, right_high], 0),
        preferred_element_type=jnp.float32,
    ) * (1.0 / N)
    out_ref[0:W, :] = both[:, 0:W]
    out_ref[W : 2 * W, :] = both[:, W : 2 * W]
    eigen_copy.wait()
    eigen_ref[0:1, 0 : eigen_row.shape[1]] = eigen_row[...]


def image_kernel(
    spec_ref, near_hbm, far_ref, weights_ref, row_ref, along_z_ref, image_ref,
    fields_re, fields_im, near_ref, sem,
):
    near_copy = pltpu.make_async_copy(near_hbm, near_ref, sem)
    near_copy.start()
    even_eigen = along_z_ref[8:9, :]
    odd_eigen = along_z_ref[FAR_Z * 16 + 8 : FAR_Z * 16 + 9, :]
    odd = lax.axis_index("kern") // CORES == 1
    near_eigen = jnp.where(odd, odd_eigen, even_eigen)
    far_eigen = jnp.where(odd, even_eigen, odd_eigen)
    row_table = row_ref[...]
    spec_re = spec_ref[0:W, :]
    spec_im = spec_ref[W : 2 * W, :]
    own = far_ref.shape[1]

    def row_field(kernels_ref, f):
        kern_re = kernels_ref[0, f]
        kern_im = kernels_ref[1, f]
        re16 = (spec_re * kern_re - spec_im * kern_im).astype(jnp.bfloat16)
        im16 = (spec_re * kern_im + spec_im * kern_re).astype(jnp.bfloat16)
        block = jnp.concatenate(
            [jnp.concatenate([re16, im16], 1), jnp.concatenate([-im16, re16], 1)], 0
        )
        part = jnp.dot(row_table, block, preferred_element_type=jnp.float32)
        real = part[0:RING_ROWS, 0:W]
        imag = part[0:RING_ROWS, W : 2 * W]
        return real, imag

    def pair_of_fields(kernels_ref, f, first):
        pair = [row_field(kernels_ref, f), row_field(kernels_ref, f + 1)]
        real = jnp.concatenate([pair[0][0], pair[1][0]], 0).astype(jnp.bfloat16)
        imag = jnp.concatenate([pair[0][1], pair[1][1]], 0).astype(jnp.bfloat16)
        at = slice((first + f) * RING_ROWS, (first + f + 2) * RING_ROWS)
        fields_re[at, 0:W] = real
        fields_re[at, W : 2 * W] = -imag
        fields_im[at, 0:W] = imag
        fields_im[at, W : 2 * W] = real

    def power(first, count, eigen_row, f0, p, start):
        rows = slice(first * RING_ROWS, (first + count) * RING_ROWS)
        weights = weights_ref[:, p * 256 : (p + 1) * 256]
        real = jnp.dot(fields_re[rows, :], weights, preferred_element_type=jnp.float32)
        imag = jnp.dot(fields_im[rows, :], weights, preferred_element_type=jnp.float32)
        for f in range(count):
            re = real[f * RING_ROWS : (f + 1) * RING_ROWS]
            im = imag[f * RING_ROWS : (f + 1) * RING_ROWS]
            term = eigen_row[0:1, f0 + f : f0 + f + 1] * (re * re + im * im)
            start = term if start is None else start + term
        return start

    parts = COARSE // 256
    for f in range(0, own, 2):
        pair_of_fields(far_ref, f, 0)
    near_copy.wait()
    for p in range(parts):
        for f in range(0, own, 2):
            if p == min(f * parts // own + (f > 0), parts - 1):
                pair_of_fields(near_ref, f, own)
        image_ref[:, p * 256 : (p + 1) * 256] = power(0, own, far_eigen, 0, p, None)
    for p in range(parts):
        at = slice(p * 256, (p + 1) * 256)
        image_ref[:, at] = power(own, own, near_eigen, 0, p, image_ref[:, at])


def dirichlet():
    distance = np.mod(np.arange(N)[None, :] - SPARSE * np.arange(32)[:, None], N)
    turn = np.pi * distance / N
    sine = np.where(distance == 0, 1.0, COARSE * np.sin(turn))
    kernel = np.where(distance % SPARSE == 0, distance == 0, np.sin(COARSE * turn) * np.cos(turn) / sine)
    kernel = kernel.astype(np.float32)
    high = kernel.astype(ml_dtypes.bfloat16)
    low = (kernel - high.astype(np.float32)).astype(ml_dtypes.bfloat16)
    return high, low


def laplace(field):
    rows, cols = field.shape
    return (
        pltpu.roll(field, 1, 0)
        + pltpu.roll(field, rows - 1, 0)
        + pltpu.roll(field, 1, 1)
        + pltpu.roll(field, cols - 1, 1)
        - 4.0 * field
    )


def bake_kernel(
    own_ref, other_ref, high_ref, low_ref, rates, image_hbm, acid_hbm, parts, ring, image_ref, acid_ref, sems
):
    kern = lax.axis_index("kern")
    for p in range(COARSE // 256):
        block = jnp.bitwise_and(p - kern, COARSE // 256 - 1)
        at = pl.ds(pl.multiple_of(block * 256, 256), 256)
        value = own_ref[:, p * 256 : (p + 1) * 256] + other_ref[:, p * 256 : (p + 1) * 256]
        high = value.astype(jnp.bfloat16).astype(jnp.float32)
        parts[0 : 2 * RING_ROWS, at] = jnp.concatenate([high, value - high], 0).astype(jnp.bfloat16)

    def weights(ref, tiles, blocks):
        rows = [
            jnp.concatenate([ref[:, ((t - m) % 32) * 128 : ((t - m) % 32) * 128 + 128] for t in tiles], 1)
            for block in blocks
            for m in range(8 * block, 8 * block + 8)
        ]
        return jnp.concatenate(rows, 0)

    everywhere = range(COARSE // 256)
    for p in range(5):
        tiles = (2 * p, 2 * p + 1) if p < 4 else (8, 31)
        wide = jnp.dot(
            parts[0 : 2 * RING_ROWS, :], weights(high_ref, tiles, everywhere), preferred_element_type=jnp.float32
        )
        fine = sum(
            jnp.dot(
                parts[0:MXU_ROWS, block * 256 : (block + 1) * 256],
                weights(low_ref, tiles, (block,)),
                preferred_element_type=jnp.float32,
            )
            for block in NEAR_BLOCKS[p]
        )
        value = wide[0:RING_ROWS] + (wide[RING_ROWS : 2 * RING_ROWS] + fine[0:RING_ROWS])
        if p < 4:
            ring[:, p * 256 : (p + 1) * 256] = value
        else:
            side = iota((RING_ROWS, 128), 1) < 64
            ring[:, COLS:RING_COLS] = jnp.where(side, value[:, 0:128], value[:, 128:256])

    dill_rate, acid_rate, quench_rate, react_rate, quench_start = (rates[i] for i in range(5))
    aerial_image = ring[...] / FIELDS
    image_ref[...] = aerial_image[0:ROWS, 0:COLS]
    image_copy = pltpu.make_async_copy(image_ref, image_hbm, sems.at[0])
    image_copy.start()
    acid_field = 1.0 - jnp.exp((-4.0 * dill_rate) * aerial_image)
    acid_diffusion = acid_rate * (0.5 + 0.5 * acid_field)
    quencher = jnp.zeros_like(acid_field) + quench_start
    for bake_step in range(STEPS):
        reaction = (4.0 * react_rate) * acid_field * quencher
        new_acid = acid_field + acid_diffusion * laplace(acid_field) - reaction
        quencher = quencher + quench_rate * laplace(quencher) - reaction
        acid_field = new_acid
    acid_ref[...] = acid_field[0:ROWS, 0:COLS]
    acid_copy = pltpu.make_async_copy(acid_ref, acid_hbm, sems.at[1])
    acid_copy.start()
    image_copy.wait()
    acid_copy.wait()


VMEM = pl.BlockSpec(memory_space=pltpu.VMEM)
SMEM = pl.BlockSpec(memory_space=pltpu.SMEM)
HBM = pl.BlockSpec(memory_space=pltpu.HBM)


def in_hbm(array):
    return pltpu.with_memory_space_constraint(array, pltpu.HBM)


def sum_everywhere(part, beside):
    plane, along_z = plane_groups(), z_groups()
    count, piece = len(plane[0]), part.shape[0] // len(plane[0])

    def exchange(blocks, groups):
        return lax.all_to_all(blocks, ALL, 0, 0, tiled=True, axis_index_groups=groups)

    def copies(block, many):
        return jnp.broadcast_to(block[None], (many,) + block.shape).reshape(-1, block.shape[1])

    some = jnp.sum(exchange(part, plane).reshape(count, piece, -1), 0)
    brought = exchange(copies(jnp.concatenate([some, beside], 0), len(along_z[0])), along_z)
    full = jnp.sum(brought.reshape(len(along_z[0]), 2 * piece, -1)[:, :piece], 0)
    return exchange(copies(full, count), plane), brought


def shards(layout, band_freqs, kernels, eigen_values, bake_rates):
    freqs = band_freqs.reshape(1, W)
    f32 = jnp.float32
    params = pltpu.CompilerParams(vmem_limit_bytes=24 * 2**20)
    far_kernels = lax.ppermute(kernels, ALL, from_next_z(1))
    own = kernels.shape[1]
    part, *tables, eigen_tile = pl.pallas_call(
        transform_kernel,
        out_shape=(
            jax.ShapeDtypeStruct((2 * W, W), f32),
            jax.ShapeDtypeStruct((2 * W, COARSE), jnp.bfloat16),
            jax.ShapeDtypeStruct((MXU_ROWS, 2 * W), jnp.bfloat16),
            jax.ShapeDtypeStruct((8, W), f32),
        ),
        in_specs=[HBM] * 3,
        out_specs=(VMEM,) * 4,
        scratch_shapes=[
            pltpu.VMEM((COLS // 4, 4 * W), jnp.bfloat16),
            pltpu.VMEM((ROWS, COLS), jnp.int32),
            pltpu.VMEM((1, W), jnp.int32),
            pltpu.VMEM((1, own), f32),
            pltpu.SemaphoreType.DMA((3,)),
        ],
        compiler_params=params,
        name="transform",
    )(in_hbm(layout), in_hbm(freqs), in_hbm(eigen_values.reshape(1, own)))
    spectrum, along_z = sum_everywhere(part, eigen_tile)
    own_image = pl.pallas_call(
        image_kernel,
        out_shape=jax.ShapeDtypeStruct((RING_ROWS, COARSE), f32),
        in_specs=[VMEM, HBM] + [VMEM] * 4,
        out_specs=VMEM,
        scratch_shapes=[
            pltpu.VMEM((2 * own * RING_ROWS, 2 * W), jnp.bfloat16),
            pltpu.VMEM((2 * own * RING_ROWS, 2 * W), jnp.bfloat16),
            pltpu.VMEM(kernels.shape, f32),
            pltpu.SemaphoreType.DMA,
        ],
        compiler_params=params,
        name="image",
    )(spectrum, in_hbm(kernels), far_kernels, *tables, along_z)
    across_cores = [(i, i + 64 if (i // 64) % 2 == 0 else i - 64) for i in range(256)]
    other_image = lax.ppermute(own_image, ALL, across_cores)
    block = jax.ShapeDtypeStruct((ROWS, COLS), f32)
    high, low = dirichlet()
    return pl.pallas_call(
        bake_kernel,
        out_shape=(block, block),
        in_specs=[VMEM, VMEM, VMEM, VMEM, SMEM],
        out_specs=(HBM, HBM),
        scratch_shapes=[
            pltpu.VMEM((2 * MXU_ROWS, COARSE), jnp.bfloat16),
            pltpu.VMEM((RING_ROWS, RING_COLS), f32),
            pltpu.VMEM((ROWS, COLS), f32),
            pltpu.VMEM((ROWS, COLS), f32),
            pltpu.SemaphoreType.DMA((2,)),
        ],
        compiler_params=params,
        name="bake",
    )(own_image, other_image, jnp.asarray(high), jnp.asarray(low), bake_rates)


def solution(mesh):
    return jax.shard_map(
        shards,
        mesh=mesh,
        in_specs=(P("slab", "kern"), P(), P(None, "kern", None, None), P("kern"), P()),
        out_specs=(P("slab", "kern"), P("slab", "kern")),
        check_vma=False,
    )
```

```python
import math

import jax
import jax.numpy as jnp
import ml_dtypes
import numpy as np
from jax import lax
from jax.experimental import pallas as pl
from jax.experimental.pallas import tpu as pltpu
from jax.sharding import PartitionSpec as P

N = 4096
W = 128
FIELDS = 48
STEPS = 2

ROWS = 64
COLS = 1024
RING_ROWS = 72
MXU_ROWS = 80
RING_COLS = 1152
SPARSE = 4
COARSE = N // SPARSE
NEAR_BLOCKS = ((0, 3), (0,), (0,), (0, 1), (0, 1, 3))
ALL = ("kern", "slab")
CHIP_Z, CORES, FAR_Z, SIDE = 2, 2, 4, 4


def device(z_lo, core, z_hi, y, x):
    return (z_lo * CORES + core) * 64 + (z_hi * SIDE + y) * SIDE + x


def place(i):
    kern, slab = divmod(i, 64)
    return kern // CORES, kern % CORES, slab // SIDE**2, slab // SIDE % SIDE, slab % SIDE


def groups_along(kept):
    groups = {}
    for i in range(256):
        groups.setdefault(tuple(place(i)[axis] for axis in kept), []).append(i)
    return list(groups.values())


def plane_groups():
    return groups_along((0, 2))


def z_groups():
    return groups_along((1, 3, 4))


def from_next_z(side):
    pairs = []
    for i in range(256):
        z_lo, core, z_hi, y, x = place(i)
        z = (z_hi * CHIP_Z + z_lo + (side if z_lo == core else -side)) % (FAR_Z * CHIP_Z)
        pairs.append((device(z % CHIP_Z, core, z // CHIP_Z, y, x), i))
    return pairs


def cos_sin(turns):
    m = jnp.bitwise_and(turns, N - 1)
    quarter = jnp.right_shift(m + N // 8, 10)
    t = (m - jnp.left_shift(quarter, 10)).astype(jnp.float32) * (2.0 * math.pi / N)
    t2 = t * t
    s = t * (1.0 + t2 * (-1.0 / 6 + t2 * (1.0 / 120 + t2 * (-1.0 / 5040 + t2 * (1.0 / 362880)))))
    c = 1.0 + t2 * (-0.5 + t2 * (1.0 / 24 + t2 * (-1.0 / 720 + t2 * (1.0 / 40320))))
    odd = jnp.bitwise_and(quarter, 1) == 1
    cos = jnp.where(odd, s, c)
    sin = jnp.where(odd, c, s)
    cos = jnp.where(jnp.bitwise_and(quarter + 1, 2) == 2, -cos, cos)
    sin = jnp.where(jnp.bitwise_and(quarter, 2) == 2, -sin, sin)
    return cos, sin


def split(values):
    high = values.astype(jnp.bfloat16)
    return high, (values - high.astype(jnp.float32)).astype(jnp.bfloat16)


def iota(shape, dim):
    return lax.broadcasted_iota(jnp.int32, shape, dim)


def image_tables(freqs, weights_ref):
    low_cos, low_sin = cos_sin(SPARSE * iota((8, W), 0) * freqs)
    high_cos, high_sin = cos_sin(SPARSE * 8 * iota((16, W), 0) * freqs)
    turn_cos, turn_sin = cos_sin(jnp.broadcast_to(SPARSE * 128 * freqs, (8, W)))
    cos_parts, sin_parts = [], []
    for a in range(16):
        ca, sa = high_cos[a : a + 1, :], high_sin[a : a + 1, :]
        cos_parts.append(ca * low_cos - sa * low_sin)
        sin_parts.append(sa * low_cos + ca * low_sin)
    cos = jnp.concatenate(cos_parts, 0).T
    sin = jnp.concatenate(sin_parts, 0).T
    turn_cos = jnp.broadcast_to(turn_cos[0:1], (W, W)).T
    turn_sin = jnp.broadcast_to(turn_sin[0:1], (W, W)).T
    for start in range(0, W, 32):
        rows = slice(start, start + 32)
        c, s, tc, ts = cos[rows], sin[rows], turn_cos[rows], turn_sin[rows]
        for tile in range(COARSE // 128):
            at = slice(tile * 128, tile * 128 + 128)
            weights_ref[rows, at] = c.astype(jnp.bfloat16)
            weights_ref[W + start : W + start + 32, at] = s.astype(jnp.bfloat16)
            c, s = c * tc - s * ts, s * tc + c * ts


def transform_kernel(
    layout_hbm, freqs_hbm, eigen_hbm, out_ref, weights_ref, row_ref, eigen_ref, table, layout_ref, freqs_ref, eigen_row,
    sems,
):
    freqs_copy = pltpu.make_async_copy(freqs_hbm, freqs_ref, sems.at[0])
    layout_copies = [
        pltpu.make_async_copy(layout_hbm.at[pl.ds(i * 16, 16), :], layout_ref.at[pl.ds(i * 16, 16), :], sems.at[2 + i])
        for i in range(ROWS // 16)
    ]
    eigen_copy = pltpu.make_async_copy(eigen_hbm, eigen_row, sems.at[1])
    freqs_copy.start()
    for copy in layout_copies:
        copy.start()
    eigen_copy.start()
    eigen_ref[...] = jnp.zeros_like(eigen_ref)
    row_first = lax.axis_index("slab") * ROWS
    col_first = lax.axis_index("kern") * COLS
    freqs_copy.wait()
    freqs = freqs_ref[...]
    step, quarter = 32, COLS // 4
    base_cos, base_sin = cos_sin((col_first + iota((step, W), 0)) * freqs)
    turn_cos, turn_sin = cos_sin((step * iota((quarter // step, W), 0)) * freqs)
    join_cos, join_sin = cos_sin((quarter * iota((8, W), 0)) * freqs)
    for a in range(quarter // step):
        ca, sa = turn_cos[a : a + 1, :], turn_sin[a : a + 1, :]
        cos = ca * base_cos - sa * base_sin
        sin = sa * base_cos + ca * base_sin
        cos_high, cos_low = split(cos)
        sin_high, sin_low = split(sin)
        at = pl.ds(a * step, step)
        table[at, 0:W] = cos_high
        table[at, W : 2 * W] = sin_high
        table[at, 2 * W : 3 * W] = cos_low
        table[at, 3 * W : 4 * W] = sin_low
    row = iota((MXU_ROWS, W), 0)
    row = jnp.where(row < ROWS + 4, row, row - RING_ROWS)
    cos_row, sin_row = cos_sin((row_first + row) * freqs)
    row_ref[...] = (jnp.concatenate([cos_row, sin_row], 1) / W).astype(jnp.bfloat16)
    left_high, left_low = split(jnp.concatenate([cos_row[0:ROWS], sin_row[0:ROWS]], 0).T)
    left = jnp.concatenate([left_high, left_high, left_low], 1)
    image_tables(freqs, weights_ref)
    for copy in layout_copies:
        copy.wait()
    transmit = (2 * layout_ref[...] - 1).astype(jnp.float32).astype(jnp.bfloat16)
    stacked = jnp.concatenate([transmit[:, h * quarter : (h + 1) * quarter] for h in range(4)], 0)
    along = jnp.dot(stacked, table[...], preferred_element_type=jnp.float32)
    along_cos = along[:, 0:W] + along[:, 2 * W : 3 * W]
    along_sin = along[:, W : 2 * W] + along[:, 3 * W : 4 * W]
    along_re, along_im = along_cos[0:ROWS], -along_sin[0:ROWS]
    for h in range(1, 4):
        c, s = along_cos[h * ROWS : (h + 1) * ROWS], along_sin[h * ROWS : (h + 1) * ROWS]
        jc, js = join_cos[h : h + 1, :], join_sin[h : h + 1, :]
        along_re = along_re + (jc * c - js * s)
        along_im = along_im - (jc * s + js * c)
    right = jnp.concatenate(
        [
            jnp.concatenate([along_re, along_im], 1),
            jnp.concatenate([along_im, -along_re], 1),
        ],
        0,
    )
    right_high, right_low = split(right)
    both = jnp.dot(
        left,
        jnp.concatenate([right_high, right_low, right_high], 0),
        preferred_element_type=jnp.float32,
    ) * (1.0 / N)
    out_ref[0:W, :] = both[:, 0:W]
    out_ref[W : 2 * W, :] = both[:, W : 2 * W]
    eigen_copy.wait()
    eigen_ref[0:1, 0 : eigen_row.shape[1]] = eigen_row[...]


def image_kernel(
    spec_ref, near_hbm, far_ref, weights_ref, row_ref, along_z_ref, image_ref,
    fields_re, fields_im, near_ref, sem,
):
    near_copy = pltpu.make_async_copy(near_hbm, near_ref, sem)
    near_copy.start()
    even_eigen = along_z_ref[8:9, :]
    odd_eigen = along_z_ref[FAR_Z * 16 + 8 : FAR_Z * 16 + 9, :]
    odd = lax.axis_index("kern") // CORES == 1
    near_eigen = jnp.where(odd, odd_eigen, even_eigen)
    far_eigen = jnp.where(odd, even_eigen, odd_eigen)
    row_table = row_ref[...]
    spec_re = spec_ref[0:W, :]
    spec_im = spec_ref[W : 2 * W, :]
    own = far_ref.shape[1]

    def row_field(kernels_ref, f):
        kern_re = kernels_ref[0, f]
        kern_im = kernels_ref[1, f]
        re16 = (spec_re * kern_re - spec_im * kern_im).astype(jnp.bfloat16)
        im16 = (spec_re * kern_im + spec_im * kern_re).astype(jnp.bfloat16)
        block = jnp.concatenate(
            [jnp.concatenate([re16, im16], 1), jnp.concatenate([-im16, re16], 1)], 0
        )
        part = jnp.dot(row_table, block, preferred_element_type=jnp.float32)
        real = part[0:RING_ROWS, 0:W]
        imag = part[0:RING_ROWS, W : 2 * W]
        return real, imag

    def pair_of_fields(kernels_ref, f, first):
        pair = [row_field(kernels_ref, f), row_field(kernels_ref, f + 1)]
        real = jnp.concatenate([pair[0][0], pair[1][0]], 0).astype(jnp.bfloat16)
        imag = jnp.concatenate([pair[0][1], pair[1][1]], 0).astype(jnp.bfloat16)
        at = slice((first + f) * RING_ROWS, (first + f + 2) * RING_ROWS)
        fields_re[at, 0:W] = real
        fields_re[at, W : 2 * W] = -imag
        fields_im[at, 0:W] = imag
        fields_im[at, W : 2 * W] = real

    def power(first, count, eigen_row, f0, p, start):
        rows = slice(first * RING_ROWS, (first + count) * RING_ROWS)
        weights = weights_ref[:, p * 256 : (p + 1) * 256]
        real = jnp.dot(fields_re[rows, :], weights, preferred_element_type=jnp.float32)
        imag = jnp.dot(fields_im[rows, :], weights, preferred_element_type=jnp.float32)
        for f in range(count):
            re = real[f * RING_ROWS : (f + 1) * RING_ROWS]
            im = imag[f * RING_ROWS : (f + 1) * RING_ROWS]
            term = eigen_row[0:1, f0 + f : f0 + f + 1] * (re * re + im * im)
            start = term if start is None else start + term
        return start

    parts = COARSE // 256
    for f in range(0, own, 2):
        pair_of_fields(far_ref, f, 0)
    near_copy.wait()
    for p in range(parts):
        for f in range(0, own, 2):
            if p == min(f * parts // own + (f > 0), parts - 1):
                pair_of_fields(near_ref, f, own)
        image_ref[:, p * 256 : (p + 1) * 256] = power(0, own, far_eigen, 0, p, None)
    for p in range(parts):
        at = slice(p * 256, (p + 1) * 256)
        image_ref[:, at] = power(own, own, near_eigen, 0, p, image_ref[:, at])


def dirichlet():
    distance = np.mod(np.arange(N)[None, :] - SPARSE * np.arange(32)[:, None], N)
    turn = np.pi * distance / N
    sine = np.where(distance == 0, 1.0, COARSE * np.sin(turn))
    kernel = np.where(distance % SPARSE == 0, distance == 0, np.sin(COARSE * turn) * np.cos(turn) / sine)
    kernel = kernel.astype(np.float32)
    high = kernel.astype(ml_dtypes.bfloat16)
    low = (kernel - high.astype(np.float32)).astype(ml_dtypes.bfloat16)
    return high, low


def laplace(field):
    rows, cols = field.shape
    return (
        pltpu.roll(field, 1, 0)
        + pltpu.roll(field, rows - 1, 0)
        + pltpu.roll(field, 1, 1)
        + pltpu.roll(field, cols - 1, 1)
        - 4.0 * field
    )


def bake_kernel(
    own_ref, other_ref, high_ref, low_ref, rates, image_hbm, acid_hbm, parts, ring, image_ref, acid_ref, sems
):
    kern = lax.axis_index("kern")
    for p in range(COARSE // 256):
        block = jnp.bitwise_and(p - kern, COARSE // 256 - 1)
        at = pl.ds(pl.multiple_of(block * 256, 256), 256)
        value = own_ref[:, p * 256 : (p + 1) * 256] + other_ref[:, p * 256 : (p + 1) * 256]
        high = value.astype(jnp.bfloat16).astype(jnp.float32)
        parts[0 : 2 * RING_ROWS, at] = jnp.concatenate([high, value - high], 0).astype(jnp.bfloat16)

    def weights(ref, tiles, blocks):
        rows = [
            jnp.concatenate([ref[:, ((t - m) % 32) * 128 : ((t - m) % 32) * 128 + 128] for t in tiles], 1)
            for block in blocks
            for m in range(8 * block, 8 * block + 8)
        ]
        return jnp.concatenate(rows, 0)

    everywhere = range(COARSE // 256)
    for p in range(5):
        tiles = (2 * p, 2 * p + 1) if p < 4 else (8, 31)
        wide = jnp.dot(
            parts[0 : 2 * RING_ROWS, :], weights(high_ref, tiles, everywhere), preferred_element_type=jnp.float32
        )
        fine = sum(
            jnp.dot(
                parts[0:MXU_ROWS, block * 256 : (block + 1) * 256],
                weights(low_ref, tiles, (block,)),
                preferred_element_type=jnp.float32,
            )
            for block in NEAR_BLOCKS[p]
        )
        value = wide[0:RING_ROWS] + (wide[RING_ROWS : 2 * RING_ROWS] + fine[0:RING_ROWS])
        if p < 4:
            ring[:, p * 256 : (p + 1) * 256] = value
        else:
            side = iota((RING_ROWS, 128), 1) < 64
            ring[:, COLS:RING_COLS] = jnp.where(side, value[:, 0:128], value[:, 128:256])

    dill_rate, acid_rate, quench_rate, react_rate, quench_start = (rates[0:1, i : i + 1] for i in range(5))
    aerial_image = ring[...] / FIELDS
    image_ref[...] = aerial_image[0:ROWS, 0:COLS]
    image_copy = pltpu.make_async_copy(image_ref, image_hbm, sems.at[0])
    image_copy.start()
    acid_field = 1.0 - jnp.exp((-4.0 * dill_rate) * aerial_image)
    acid_diffusion = acid_rate * (0.5 + 0.5 * acid_field)
    quencher = jnp.zeros_like(acid_field) + quench_start
    for bake_step in range(STEPS):
        reaction = (4.0 * react_rate) * acid_field * quencher
        new_acid = acid_field + acid_diffusion * laplace(acid_field) - reaction
        quencher = quencher + quench_rate * laplace(quencher) - reaction
        acid_field = new_acid
    acid_copies = []
    for p in range(2):
        at = slice(p * COLS // 2, (p + 1) * COLS // 2)
        acid_ref[:, at] = acid_field[0:ROWS, at]
        acid_copies.append(pltpu.make_async_copy(acid_ref.at[:, at], acid_hbm.at[:, at], sems.at[1 + p]))
        acid_copies[p].start()
    image_copy.wait()
    for copy in acid_copies:
        copy.wait()


VMEM = pl.BlockSpec(memory_space=pltpu.VMEM)
HBM = pl.BlockSpec(memory_space=pltpu.HBM)


def in_hbm(array):
    return pltpu.with_memory_space_constraint(array, pltpu.HBM)


def sum_everywhere(part, beside):
    plane, along_z = plane_groups(), z_groups()
    count, piece = len(plane[0]), part.shape[0] // len(plane[0])

    def exchange(blocks, groups):
        return lax.all_to_all(blocks, ALL, 0, 0, tiled=True, axis_index_groups=groups)

    def copies(block, many):
        return jnp.broadcast_to(block[None], (many,) + block.shape).reshape(-1, block.shape[1])

    some = jnp.sum(exchange(part, plane).reshape(count, piece, -1), 0)
    brought = exchange(copies(jnp.concatenate([some, beside], 0), len(along_z[0])), along_z)
    full = jnp.sum(brought.reshape(len(along_z[0]), 2 * piece, -1)[:, :piece], 0)
    return exchange(copies(full, count), plane), brought


def shards(layout, band_freqs, kernels, eigen_values, bake_rates):
    freqs = band_freqs.reshape(1, W)
    f32 = jnp.float32
    params = pltpu.CompilerParams(vmem_limit_bytes=24 * 2**20)
    far_kernels = lax.ppermute(kernels, ALL, from_next_z(1))
    own = kernels.shape[1]
    part, *tables, eigen_tile = pl.pallas_call(
        transform_kernel,
        out_shape=(
            jax.ShapeDtypeStruct((2 * W, W), f32),
            jax.ShapeDtypeStruct((2 * W, COARSE), jnp.bfloat16),
            jax.ShapeDtypeStruct((MXU_ROWS, 2 * W), jnp.bfloat16),
            jax.ShapeDtypeStruct((8, W), f32),
        ),
        in_specs=[HBM] * 3,
        out_specs=(VMEM,) * 4,
        scratch_shapes=[
            pltpu.VMEM((COLS // 4, 4 * W), jnp.bfloat16),
            pltpu.VMEM((ROWS, COLS), jnp.int32),
            pltpu.VMEM((1, W), jnp.int32),
            pltpu.VMEM((1, own), f32),
            pltpu.SemaphoreType.DMA((6,)),
        ],
        compiler_params=params,
        name="transform",
    )(in_hbm(layout), in_hbm(freqs), in_hbm(eigen_values.reshape(1, own)))
    spectrum, along_z = sum_everywhere(part, eigen_tile)
    own_image = pl.pallas_call(
        image_kernel,
        out_shape=jax.ShapeDtypeStruct((RING_ROWS, COARSE), f32),
        in_specs=[VMEM, HBM] + [VMEM] * 4,
        out_specs=VMEM,
        scratch_shapes=[
            pltpu.VMEM((2 * own * RING_ROWS, 2 * W), jnp.bfloat16),
            pltpu.VMEM((2 * own * RING_ROWS, 2 * W), jnp.bfloat16),
            pltpu.VMEM(kernels.shape, f32),
            pltpu.SemaphoreType.DMA,
        ],
        compiler_params=pltpu.CompilerParams(
            vmem_limit_bytes=24 * 2**20
        ),
        name="image",
    )(spectrum, in_hbm(kernels), far_kernels, *tables, along_z)
    across_cores = [(i, i + 64 if (i // 64) % 2 == 0 else i - 64) for i in range(256)]
    other_image = lax.ppermute(own_image, ALL, across_cores)
    block = jax.ShapeDtypeStruct((ROWS, COLS), f32)
    high, low = dirichlet()
    return pl.pallas_call(
        bake_kernel,
        out_shape=(block, block),
        in_specs=[VMEM] * 5,
        out_specs=(HBM, HBM),
        scratch_shapes=[
            pltpu.VMEM((2 * MXU_ROWS, COARSE), jnp.bfloat16),
            pltpu.VMEM((RING_ROWS, RING_COLS), f32),
            pltpu.VMEM((ROWS, COLS), f32),
            pltpu.VMEM((ROWS, COLS), f32),
            pltpu.SemaphoreType.DMA((3,)),
        ],
        compiler_params=params,
        name="bake",
    )(own_image, other_image, jnp.asarray(high), jnp.asarray(low), bake_rates.reshape(1, 5))


def solution(mesh):
    return jax.shard_map(
        shards,
        mesh=mesh,
        in_specs=(P("slab", "kern"), P(), P(None, "kern", None, None), P("kern"), P()),
        out_specs=(P("slab", "kern"), P("slab", "kern")),
        check_vma=False,
    )
```

```python
import math

import jax
import jax.numpy as jnp
import ml_dtypes
import numpy as np
from jax import lax
from jax.experimental import pallas as pl
from jax.experimental.pallas import tpu as pltpu
from jax.sharding import PartitionSpec as P

N = 4096
W = 128
FIELDS = 48
STEPS = 2

ROWS = 64
COLS = 1024
RING_ROWS = 72
MXU_ROWS = 80
RING_COLS = 1152
SPARSE = 4
COARSE = N // SPARSE
NEAR_BLOCKS = ((0, 3), (0,), (0,), (0, 1), (0, 1, 3))
ALL = ("kern", "slab")
CHIP_Z, CORES, FAR_Z, SIDE = 2, 2, 4, 4


def device(z_lo, core, z_hi, y, x):
    return (z_lo * CORES + core) * 64 + (z_hi * SIDE + y) * SIDE + x


def place(i):
    kern, slab = divmod(i, 64)
    return kern // CORES, kern % CORES, slab // SIDE**2, slab // SIDE % SIDE, slab % SIDE


def groups_along(kept):
    groups = {}
    for i in range(256):
        groups.setdefault(tuple(place(i)[axis] for axis in kept), []).append(i)
    return list(groups.values())


def plane_groups():
    return groups_along((0, 2))


def z_groups():
    return groups_along((1, 3, 4))


def from_next_z(side):
    pairs = []
    for i in range(256):
        z_lo, core, z_hi, y, x = place(i)
        z = (z_hi * CHIP_Z + z_lo + (side if z_lo == core else -side)) % (FAR_Z * CHIP_Z)
        pairs.append((device(z % CHIP_Z, core, z // CHIP_Z, y, x), i))
    return pairs


def cos_sin(turns):
    m = jnp.bitwise_and(turns, N - 1)
    quarter = jnp.right_shift(m + N // 8, 10)
    t = (m - jnp.left_shift(quarter, 10)).astype(jnp.float32) * (2.0 * math.pi / N)
    t2 = t * t
    s = t * (1.0 + t2 * (-1.0 / 6 + t2 * (1.0 / 120 + t2 * (-1.0 / 5040 + t2 * (1.0 / 362880)))))
    c = 1.0 + t2 * (-0.5 + t2 * (1.0 / 24 + t2 * (-1.0 / 720 + t2 * (1.0 / 40320))))
    odd = jnp.bitwise_and(quarter, 1) == 1
    cos = jnp.where(odd, s, c)
    sin = jnp.where(odd, c, s)
    cos = jnp.where(jnp.bitwise_and(quarter + 1, 2) == 2, -cos, cos)
    sin = jnp.where(jnp.bitwise_and(quarter, 2) == 2, -sin, sin)
    return cos, sin


def split(values):
    high = values.astype(jnp.bfloat16)
    return high, (values - high.astype(jnp.float32)).astype(jnp.bfloat16)


def iota(shape, dim):
    return lax.broadcasted_iota(jnp.int32, shape, dim)


def image_tables(freqs, weights_ref):
    low_cos, low_sin = cos_sin(SPARSE * iota((8, W), 0) * freqs)
    high_cos, high_sin = cos_sin(SPARSE * 8 * iota((16, W), 0) * freqs)
    turn_cos, turn_sin = cos_sin(jnp.broadcast_to(SPARSE * 128 * freqs, (8, W)))
    cos_parts, sin_parts = [], []
    for a in range(16):
        ca, sa = high_cos[a : a + 1, :], high_sin[a : a + 1, :]
        cos_parts.append(ca * low_cos - sa * low_sin)
        sin_parts.append(sa * low_cos + ca * low_sin)
    cos = jnp.concatenate(cos_parts, 0).T
    sin = jnp.concatenate(sin_parts, 0).T
    turn_cos = jnp.broadcast_to(turn_cos[0:1], (W, W)).T
    turn_sin = jnp.broadcast_to(turn_sin[0:1], (W, W)).T
    for start in range(0, W, 32):
        rows = slice(start, start + 32)
        c, s, tc, ts = cos[rows], sin[rows], turn_cos[rows], turn_sin[rows]
        for tile in range(COARSE // 128):
            at = slice(tile * 128, tile * 128 + 128)
            weights_ref[rows, at] = c.astype(jnp.bfloat16)
            weights_ref[W + start : W + start + 32, at] = s.astype(jnp.bfloat16)
            c, s = c * tc - s * ts, s * tc + c * ts


def transform_kernel(
    layout_hbm, freqs_hbm, eigen_hbm, out_ref, weights_ref, row_ref, eigen_ref, table, layout_ref, freqs_ref, eigen_row,
    sems,
):
    freqs_copy = pltpu.make_async_copy(freqs_hbm, freqs_ref, sems.at[0])
    layout_copies = [
        pltpu.make_async_copy(layout_hbm.at[pl.ds(i * 16, 16), :], layout_ref.at[pl.ds(i * 16, 16), :], sems.at[2 + i])
        for i in range(ROWS // 16)
    ]
    eigen_copy = pltpu.make_async_copy(eigen_hbm, eigen_row, sems.at[1])
    freqs_copy.start()
    for copy in layout_copies:
        copy.start()
    eigen_copy.start()
    eigen_ref[...] = jnp.zeros_like(eigen_ref)
    row_first = lax.axis_index("slab") * ROWS
    col_first = lax.axis_index("kern") * COLS
    freqs_copy.wait()
    freqs = freqs_ref[...]
    step, quarter = 32, COLS // 4
    base_cos, base_sin = cos_sin((col_first + iota((step, W), 0)) * freqs)
    turn_cos, turn_sin = cos_sin((step * iota((quarter // step, W), 0)) * freqs)
    join_cos, join_sin = cos_sin((quarter * iota((8, W), 0)) * freqs)
    for a in range(quarter // step):
        ca, sa = turn_cos[a : a + 1, :], turn_sin[a : a + 1, :]
        cos = ca * base_cos - sa * base_sin
        sin = sa * base_cos + ca * base_sin
        cos_high, cos_low = split(cos)
        sin_high, sin_low = split(sin)
        at = pl.ds(a * step, step)
        table[at, 0:W] = cos_high
        table[at, W : 2 * W] = sin_high
        table[at, 2 * W : 3 * W] = cos_low
        table[at, 3 * W : 4 * W] = sin_low
    row = iota((MXU_ROWS, W), 0)
    row = jnp.where(row < ROWS + 4, row, row - RING_ROWS)
    cos_row, sin_row = cos_sin((row_first + row) * freqs)
    row_ref[...] = (jnp.concatenate([cos_row, sin_row], 1) / W).astype(jnp.bfloat16)
    left_high, left_low = split(jnp.concatenate([cos_row[0:ROWS], sin_row[0:ROWS]], 0).T)
    left = jnp.concatenate([left_high, left_high, left_low], 1)
    image_tables(freqs, weights_ref)
    for copy in layout_copies:
        copy.wait()
    transmit = (2 * layout_ref[...] - 1).astype(jnp.float32).astype(jnp.bfloat16)
    stacked = jnp.concatenate([transmit[:, h * quarter : (h + 1) * quarter] for h in range(4)], 0)
    along = jnp.dot(stacked, table[...], preferred_element_type=jnp.float32)
    along_cos = along[:, 0:W] + along[:, 2 * W : 3 * W]
    along_sin = along[:, W : 2 * W] + along[:, 3 * W : 4 * W]
    along_re, along_im = along_cos[0:ROWS], -along_sin[0:ROWS]
    for h in range(1, 4):
        c, s = along_cos[h * ROWS : (h + 1) * ROWS], along_sin[h * ROWS : (h + 1) * ROWS]
        jc, js = join_cos[h : h + 1, :], join_sin[h : h + 1, :]
        along_re = along_re + (jc * c - js * s)
        along_im = along_im - (jc * s + js * c)
    right = jnp.concatenate(
        [
            jnp.concatenate([along_re, along_im], 1),
            jnp.concatenate([along_im, -along_re], 1),
        ],
        0,
    )
    right_high, right_low = split(right)
    both = jnp.dot(
        left,
        jnp.concatenate([right_high, right_low, right_high], 0),
        preferred_element_type=jnp.float32,
    ) * (1.0 / N)
    out_ref[0:W, :] = both[:, 0:W]
    out_ref[W : 2 * W, :] = both[:, W : 2 * W]
    eigen_copy.wait()
    eigen_ref[0:1, 0 : eigen_row.shape[1]] = eigen_row[...]


def image_kernel(
    spec_ref, near_hbm, far_ref, weights_ref, row_ref, along_z_ref, image_ref,
    fields_re, fields_im, near_ref, sem,
):
    near_copy = pltpu.make_async_copy(near_hbm, near_ref, sem)
    near_copy.start()
    even_eigen = along_z_ref[8:9, :]
    odd_eigen = along_z_ref[FAR_Z * 16 + 8 : FAR_Z * 16 + 9, :]
    odd = lax.axis_index("kern") // CORES == 1
    near_eigen = jnp.where(odd, odd_eigen, even_eigen)
    far_eigen = jnp.where(odd, even_eigen, odd_eigen)
    row_table = row_ref[...]
    spec_re = spec_ref[0:W, :]
    spec_im = spec_ref[W : 2 * W, :]
    own = far_ref.shape[1]

    def row_field(kernels_ref, f):
        kern_re = kernels_ref[0, f]
        kern_im = kernels_ref[1, f]
        re16 = (spec_re * kern_re - spec_im * kern_im).astype(jnp.bfloat16)
        im16 = (spec_re * kern_im + spec_im * kern_re).astype(jnp.bfloat16)
        block = jnp.concatenate(
            [jnp.concatenate([re16, im16], 1), jnp.concatenate([-im16, re16], 1)], 0
        )
        part = jnp.dot(row_table, block, preferred_element_type=jnp.float32)
        real = part[0:RING_ROWS, 0:W]
        imag = part[0:RING_ROWS, W : 2 * W]
        return real, imag

    def pair_of_fields(kernels_ref, f, first):
        pair = [row_field(kernels_ref, f), row_field(kernels_ref, f + 1)]
        real = jnp.concatenate([pair[0][0], pair[1][0]], 0).astype(jnp.bfloat16)
        imag = jnp.concatenate([pair[0][1], pair[1][1]], 0).astype(jnp.bfloat16)
        at = slice((first + f) * RING_ROWS, (first + f + 2) * RING_ROWS)
        fields_re[at, 0:W] = real
        fields_re[at, W : 2 * W] = -imag
        fields_im[at, 0:W] = imag
        fields_im[at, W : 2 * W] = real

    def power(first, count, eigen_row, f0, p, start):
        rows = slice(first * RING_ROWS, (first + count) * RING_ROWS)
        weights = weights_ref[:, p * 256 : (p + 1) * 256]
        real = jnp.dot(fields_re[rows, :], weights, preferred_element_type=jnp.float32)
        imag = jnp.dot(fields_im[rows, :], weights, preferred_element_type=jnp.float32)
        for f in range(count):
            re = real[f * RING_ROWS : (f + 1) * RING_ROWS]
            im = imag[f * RING_ROWS : (f + 1) * RING_ROWS]
            term = eigen_row[0:1, f0 + f : f0 + f + 1] * (re * re + im * im)
            start = term if start is None else start + term
        return start

    parts = COARSE // 256
    for f in range(0, own, 2):
        pair_of_fields(far_ref, f, 0)
    near_copy.wait()
    for p in range(parts):
        for f in range(0, own, 2):
            if p == min(f * parts // own + (f > 0), parts - 1):
                pair_of_fields(near_ref, f, own)
        image_ref[:, p * 256 : (p + 1) * 256] = power(0, own, far_eigen, 0, p, None)
    for p in range(parts):
        at = slice(p * 256, (p + 1) * 256)
        image_ref[:, at] = power(own, own, near_eigen, 0, p, image_ref[:, at])


def dirichlet():
    distance = np.mod(np.arange(N)[None, :] - SPARSE * np.arange(32)[:, None], N)
    turn = np.pi * distance / N
    sine = np.where(distance == 0, 1.0, COARSE * np.sin(turn))
    kernel = np.where(distance % SPARSE == 0, distance == 0, np.sin(COARSE * turn) * np.cos(turn) / sine)
    kernel = kernel.astype(np.float32)
    tiles = kernel.reshape(32, 32, 128)
    sides = np.stack([np.concatenate([tiles[:, (8 - m) % 32, :64], tiles[:, (31 - m) % 32, 64:]], 1) for m in range(32)], 1)
    kernel = np.concatenate([kernel, sides.reshape(32, N)], 1)
    high = kernel.astype(ml_dtypes.bfloat16)
    low = (kernel - high.astype(np.float32)).astype(ml_dtypes.bfloat16)
    return high, low


def laplace(field):
    rows, cols = field.shape
    return (
        pltpu.roll(field, 1, 0)
        + pltpu.roll(field, rows - 1, 0)
        + pltpu.roll(field, 1, 1)
        + pltpu.roll(field, cols - 1, 1)
        - 4.0 * field
    )


def bake_kernel(
    own_ref, other_ref, high_ref, low_ref, rates, image_hbm, acid_hbm, parts, ring, image_ref, acid_ref, sems
):
    kern = lax.axis_index("kern")
    for p in range(COARSE // 256):
        block = jnp.bitwise_and(p - kern, COARSE // 256 - 1)
        at = pl.ds(pl.multiple_of(block * 256, 256), 256)
        value = own_ref[:, p * 256 : (p + 1) * 256] + other_ref[:, p * 256 : (p + 1) * 256]
        high = value.astype(jnp.bfloat16).astype(jnp.float32)
        parts[0 : 2 * RING_ROWS, at] = jnp.concatenate([high, value - high], 0).astype(jnp.bfloat16)

    def weights(ref, tiles, blocks):
        def tile(t, m):
            at = ((t - m) % 32 if t < 32 else t + m) * 128
            return ref[:, at : at + 128]

        rows = [
            jnp.concatenate([tile(t, m) for t in tiles], 1) for block in blocks for m in range(8 * block, 8 * block + 8)
        ]
        return jnp.concatenate(rows, 0)

    everywhere = range(COARSE // 256)
    for p in range(5):
        tiles = (2 * p, 2 * p + 1) if p < 4 else (32,)
        wide = jnp.dot(
            parts[0 : 2 * RING_ROWS, :], weights(high_ref, tiles, everywhere), preferred_element_type=jnp.float32
        )
        fine = sum(
            jnp.dot(
                parts[0:MXU_ROWS, block * 256 : (block + 1) * 256],
                weights(low_ref, tiles, (block,)),
                preferred_element_type=jnp.float32,
            )
            for block in NEAR_BLOCKS[p]
        )
        value = wide[0:RING_ROWS] + (wide[RING_ROWS : 2 * RING_ROWS] + fine[0:RING_ROWS])
        ring[:, p * 256 : p * 256 + value.shape[1]] = value

    dill_rate, acid_rate, quench_rate, react_rate, quench_start = (rates[0:1, i : i + 1] for i in range(5))
    aerial_image = ring[...] / FIELDS
    image_ref[...] = aerial_image[0:ROWS, 0:COLS]
    image_copy = pltpu.make_async_copy(image_ref, image_hbm, sems.at[0])
    image_copy.start()
    acid_field = 1.0 - jnp.exp((-4.0 * dill_rate) * aerial_image)
    acid_diffusion = acid_rate * (0.5 + 0.5 * acid_field)
    quencher = jnp.zeros_like(acid_field) + quench_start
    for bake_step in range(STEPS):
        reaction = (4.0 * react_rate) * acid_field * quencher
        new_acid = acid_field + acid_diffusion * laplace(acid_field) - reaction
        quencher = quencher + quench_rate * laplace(quencher) - reaction
        acid_field = new_acid
    acid_copies = []
    for p in range(2):
        at = slice(p * COLS // 2, (p + 1) * COLS // 2)
        acid_ref[:, at] = acid_field[0:ROWS, at]
        acid_copies.append(pltpu.make_async_copy(acid_ref.at[:, at], acid_hbm.at[:, at], sems.at[1 + p]))
        acid_copies[p].start()
    image_copy.wait()
    for copy in acid_copies:
        copy.wait()


VMEM = pl.BlockSpec(memory_space=pltpu.VMEM)
HBM = pl.BlockSpec(memory_space=pltpu.HBM)


def in_hbm(array):
    return pltpu.with_memory_space_constraint(array, pltpu.HBM)


def sum_everywhere(part, beside):
    plane, along_z = plane_groups(), z_groups()
    count, piece = len(plane[0]), part.shape[0] // len(plane[0])

    def exchange(blocks, groups):
        return lax.all_to_all(blocks, ALL, 0, 0, tiled=True, axis_index_groups=groups)

    def copies(block, many):
        return jnp.broadcast_to(block[None], (many,) + block.shape).reshape(-1, block.shape[1])

    some = jnp.sum(exchange(part, plane).reshape(count, piece, -1), 0)
    brought = exchange(copies(jnp.concatenate([some, beside], 0), len(along_z[0])), along_z)
    full = jnp.sum(brought.reshape(len(along_z[0]), 2 * piece, -1)[:, :piece], 0)
    return exchange(copies(full, count), plane), brought


def shards(layout, band_freqs, kernels, eigen_values, bake_rates):
    freqs = band_freqs.reshape(1, W)
    f32 = jnp.float32
    params = pltpu.CompilerParams(vmem_limit_bytes=24 * 2**20)
    far_kernels = lax.ppermute(kernels, ALL, from_next_z(1))
    own = kernels.shape[1]
    part, *tables, eigen_tile = pl.pallas_call(
        transform_kernel,
        out_shape=(
            jax.ShapeDtypeStruct((2 * W, W), f32),
            jax.ShapeDtypeStruct((2 * W, COARSE), jnp.bfloat16),
            jax.ShapeDtypeStruct((MXU_ROWS, 2 * W), jnp.bfloat16),
            jax.ShapeDtypeStruct((8, W), f32),
        ),
        in_specs=[HBM] * 3,
        out_specs=(VMEM,) * 4,
        scratch_shapes=[
            pltpu.VMEM((COLS // 4, 4 * W), jnp.bfloat16),
            pltpu.VMEM((ROWS, COLS), jnp.int32),
            pltpu.VMEM((1, W), jnp.int32),
            pltpu.VMEM((1, own), f32),
            pltpu.SemaphoreType.DMA((6,)),
        ],
        compiler_params=params,
        name="transform",
    )(in_hbm(layout), in_hbm(freqs), in_hbm(eigen_values.reshape(1, own)))
    spectrum, along_z = sum_everywhere(part, eigen_tile)
    own_image = pl.pallas_call(
        image_kernel,
        out_shape=jax.ShapeDtypeStruct((RING_ROWS, COARSE), f32),
        in_specs=[VMEM, HBM] + [VMEM] * 4,
        out_specs=VMEM,
        scratch_shapes=[
            pltpu.VMEM((2 * own * RING_ROWS, 2 * W), jnp.bfloat16),
            pltpu.VMEM((2 * own * RING_ROWS, 2 * W), jnp.bfloat16),
            pltpu.VMEM(kernels.shape, f32),
            pltpu.SemaphoreType.DMA,
        ],
        compiler_params=pltpu.CompilerParams(
            vmem_limit_bytes=24 * 2**20
        ),
        name="image",
    )(spectrum, in_hbm(kernels), far_kernels, *tables, along_z)
    across_cores = [(i, i + 64 if (i // 64) % 2 == 0 else i - 64) for i in range(256)]
    other_image = lax.ppermute(own_image, ALL, across_cores)
    block = jax.ShapeDtypeStruct((ROWS, COLS), f32)
    high, low = dirichlet()
    return pl.pallas_call(
        bake_kernel,
        out_shape=(block, block),
        in_specs=[VMEM] * 5,
        out_specs=(HBM, HBM),
        scratch_shapes=[
            pltpu.VMEM((2 * MXU_ROWS, COARSE), jnp.bfloat16),
            pltpu.VMEM((RING_ROWS, RING_COLS), f32),
            pltpu.VMEM((ROWS, COLS), f32),
            pltpu.VMEM((ROWS, COLS), f32),
            pltpu.SemaphoreType.DMA((3,)),
        ],
        compiler_params=params,
        name="bake",
    )(own_image, other_image, jnp.asarray(high), jnp.asarray(low), bake_rates.reshape(1, 5))


def solution(mesh):
    return jax.shard_map(
        shards,
        mesh=mesh,
        in_specs=(P("slab", "kern"), P(), P(None, "kern", None, None), P("kern"), P()),
        out_specs=(P("slab", "kern"), P("slab", "kern")),
        check_vma=False,
    )
```

```python
import math

import jax
import jax.numpy as jnp
import ml_dtypes
import numpy as np
from jax import lax
from jax.experimental import pallas as pl
from jax.experimental.pallas import tpu as pltpu
from jax.sharding import PartitionSpec as P

N = 4096
W = 128
FIELDS = 48
STEPS = 2

ROWS = 64
COLS = 1024
RING_ROWS = 72
MXU_ROWS = 80
RING_COLS = 1152
SPARSE = 4
COARSE = N // SPARSE
NEAR_BLOCKS = ((0, 3), (0,), (0,), (0, 1), (0, 1, 3))
ALL = ("kern", "slab")
CHIP_Z, CORES, FAR_Z, SIDE = 2, 2, 4, 4


def device(z_lo, core, z_hi, y, x):
    return (z_lo * CORES + core) * 64 + (z_hi * SIDE + y) * SIDE + x


def place(i):
    kern, slab = divmod(i, 64)
    return kern // CORES, kern % CORES, slab // SIDE**2, slab // SIDE % SIDE, slab % SIDE


def groups_along(kept):
    groups = {}
    for i in range(256):
        groups.setdefault(tuple(place(i)[axis] for axis in kept), []).append(i)
    return list(groups.values())


def plane_groups():
    return groups_along((0, 2))


def z_groups():
    return groups_along((1, 3, 4))


def from_next_z(side):
    pairs = []
    for i in range(256):
        z_lo, core, z_hi, y, x = place(i)
        z = (z_hi * CHIP_Z + z_lo + (side if z_lo == core else -side)) % (FAR_Z * CHIP_Z)
        pairs.append((device(z % CHIP_Z, core, z // CHIP_Z, y, x), i))
    return pairs


def cos_sin(turns):
    m = jnp.bitwise_and(turns, N - 1)
    quarter = jnp.right_shift(m + N // 8, 10)
    t = (m - jnp.left_shift(quarter, 10)).astype(jnp.float32) * (2.0 * math.pi / N)
    t2 = t * t
    s = t * (1.0 + t2 * (-1.0 / 6 + t2 * (1.0 / 120 + t2 * (-1.0 / 5040 + t2 * (1.0 / 362880)))))
    c = 1.0 + t2 * (-0.5 + t2 * (1.0 / 24 + t2 * (-1.0 / 720 + t2 * (1.0 / 40320))))
    odd = jnp.bitwise_and(quarter, 1) == 1
    cos = jnp.where(odd, s, c)
    sin = jnp.where(odd, c, s)
    cos = jnp.where(jnp.bitwise_and(quarter + 1, 2) == 2, -cos, cos)
    sin = jnp.where(jnp.bitwise_and(quarter, 2) == 2, -sin, sin)
    return cos, sin


def split(values):
    high = values.astype(jnp.bfloat16)
    return high, (values - high.astype(jnp.float32)).astype(jnp.bfloat16)


def iota(shape, dim):
    return lax.broadcasted_iota(jnp.int32, shape, dim)


def image_tables(freqs, weights_ref):
    low_cos, low_sin = cos_sin(SPARSE * iota((8, W), 0) * freqs)
    high_cos, high_sin = cos_sin(SPARSE * 8 * iota((16, W), 0) * freqs)
    turn_cos, turn_sin = cos_sin(jnp.broadcast_to(SPARSE * 128 * freqs, (8, W)))
    cos_parts, sin_parts = [], []
    for a in range(16):
        ca, sa = high_cos[a : a + 1, :], high_sin[a : a + 1, :]
        cos_parts.append(ca * low_cos - sa * low_sin)
        sin_parts.append(sa * low_cos + ca * low_sin)
    cos = jnp.concatenate(cos_parts, 0).T
    sin = jnp.concatenate(sin_parts, 0).T
    turn_cos = jnp.broadcast_to(turn_cos[0:1], (W, W)).T
    turn_sin = jnp.broadcast_to(turn_sin[0:1], (W, W)).T
    for start in range(0, W, 32):
        rows = slice(start, start + 32)
        c, s, tc, ts = cos[rows], sin[rows], turn_cos[rows], turn_sin[rows]
        for tile in range(COARSE // 128):
            at = slice(tile * 128, tile * 128 + 128)
            weights_ref[rows, at] = c.astype(jnp.bfloat16)
            weights_ref[W + start : W + start + 32, at] = s.astype(jnp.bfloat16)
            c, s = c * tc - s * ts, s * tc + c * ts


def transform_kernel(
    layout_hbm, freqs_hbm, eigen_hbm, out_ref, weights_ref, row_ref, eigen_ref, table, layout_ref, freqs_ref, eigen_row,
    sems,
):
    freqs_copy = pltpu.make_async_copy(freqs_hbm, freqs_ref, sems.at[0])
    layout_copies = [
        pltpu.make_async_copy(layout_hbm.at[pl.ds(i * 16, 16), :], layout_ref.at[pl.ds(i * 16, 16), :], sems.at[2 + i])
        for i in range(ROWS // 16)
    ]
    eigen_copy = pltpu.make_async_copy(eigen_hbm, eigen_row, sems.at[1])
    freqs_copy.start()
    for copy in layout_copies:
        copy.start()
    eigen_copy.start()
    eigen_ref[...] = jnp.zeros_like(eigen_ref)
    row_first = lax.axis_index("slab") * ROWS
    col_first = lax.axis_index("kern") * COLS
    freqs_copy.wait()
    freqs = freqs_ref[...]
    step, quarter = 32, COLS // 4
    base_cos, base_sin = cos_sin((col_first + iota((step, W), 0)) * freqs)
    turn_cos, turn_sin = cos_sin((step * iota((quarter // step, W), 0)) * freqs)
    join_cos, join_sin = cos_sin((quarter * iota((8, W), 0)) * freqs)
    for a in range(quarter // step):
        ca, sa = turn_cos[a : a + 1, :], turn_sin[a : a + 1, :]
        cos = ca * base_cos - sa * base_sin
        sin = sa * base_cos + ca * base_sin
        cos_high, cos_low = split(cos)
        sin_high, sin_low = split(sin)
        at = pl.ds(a * step, step)
        table[at, 0:W] = cos_high
        table[at, W : 2 * W] = sin_high
        table[at, 2 * W : 3 * W] = cos_low
        table[at, 3 * W : 4 * W] = sin_low
    row = iota((MXU_ROWS, W), 0)
    row = jnp.where(row < ROWS + 4, row, row - RING_ROWS)
    cos_row, sin_row = cos_sin((row_first + row) * freqs)
    row_ref[...] = (jnp.concatenate([cos_row, sin_row], 1) / W).astype(jnp.bfloat16)
    left_high, left_low = split(jnp.concatenate([cos_row[0:ROWS], sin_row[0:ROWS]], 0).T)
    left = jnp.concatenate([left_high, left_high, left_low], 1)
    image_tables(freqs, weights_ref)
    for copy in layout_copies:
        copy.wait()
    pixels = layout_ref[...].astype(jnp.float32)
    transmit = (pixels + pixels - 1.0).astype(jnp.bfloat16)
    stacked = jnp.concatenate([transmit[:, h * quarter : (h + 1) * quarter] for h in range(4)], 0)
    along = jnp.dot(stacked, table[...], preferred_element_type=jnp.float32)
    along_cos = along[:, 0:W] + along[:, 2 * W : 3 * W]
    along_sin = along[:, W : 2 * W] + along[:, 3 * W : 4 * W]
    along_re, along_im = along_cos[0:ROWS], -along_sin[0:ROWS]
    for h in range(1, 4):
        c, s = along_cos[h * ROWS : (h + 1) * ROWS], along_sin[h * ROWS : (h + 1) * ROWS]
        jc, js = join_cos[h : h + 1, :], join_sin[h : h + 1, :]
        along_re = along_re + (jc * c - js * s)
        along_im = along_im - (jc * s + js * c)
    right = jnp.concatenate(
        [
            jnp.concatenate([along_re, along_im], 1),
            jnp.concatenate([along_im, -along_re], 1),
        ],
        0,
    )
    right_high, right_low = split(right)
    both = jnp.dot(
        left,
        jnp.concatenate([right_high, right_low, right_high], 0),
        preferred_element_type=jnp.float32,
    ) * (1.0 / N)
    out_ref[0:W, :] = both[:, 0:W]
    out_ref[W : 2 * W, :] = both[:, W : 2 * W]
    eigen_copy.wait()
    eigen_ref[0:1, 0 : eigen_row.shape[1]] = eigen_row[...]


def image_kernel(
    spec_ref, near_hbm, far_ref, weights_ref, row_ref, along_z_ref, image_ref,
    fields_re, fields_im, near_ref, sem,
):
    near_copy = pltpu.make_async_copy(near_hbm, near_ref, sem)
    near_copy.start()
    even_eigen = along_z_ref[8:9, :]
    odd_eigen = along_z_ref[FAR_Z * 16 + 8 : FAR_Z * 16 + 9, :]
    odd = lax.axis_index("kern") // CORES == 1
    near_eigen = jnp.where(odd, odd_eigen, even_eigen)
    far_eigen = jnp.where(odd, even_eigen, odd_eigen)
    row_table = row_ref[...]
    spec_re = spec_ref[0:W, :]
    spec_im = spec_ref[W : 2 * W, :]
    own = far_ref.shape[1]

    def row_field(kernels_ref, f):
        kern_re = kernels_ref[0, f]
        kern_im = kernels_ref[1, f]
        re16 = (spec_re * kern_re - spec_im * kern_im).astype(jnp.bfloat16)
        im16 = (spec_re * kern_im + spec_im * kern_re).astype(jnp.bfloat16)
        block = jnp.concatenate(
            [jnp.concatenate([re16, im16], 1), jnp.concatenate([-im16, re16], 1)], 0
        )
        part = jnp.dot(row_table, block, preferred_element_type=jnp.float32)
        real = part[0:RING_ROWS, 0:W]
        imag = part[0:RING_ROWS, W : 2 * W]
        return real, imag

    def pair_of_fields(kernels_ref, f, first):
        pair = [row_field(kernels_ref, f), row_field(kernels_ref, f + 1)]
        real = jnp.concatenate([pair[0][0], pair[1][0]], 0).astype(jnp.bfloat16)
        imag = jnp.concatenate([pair[0][1], pair[1][1]], 0).astype(jnp.bfloat16)
        at = slice((first + f) * RING_ROWS, (first + f + 2) * RING_ROWS)
        fields_re[at, 0:W] = real
        fields_re[at, W : 2 * W] = -imag
        fields_im[at, 0:W] = imag
        fields_im[at, W : 2 * W] = real

    def power(first, count, eigen_row, f0, p, start):
        rows = slice(first * RING_ROWS, (first + count) * RING_ROWS)
        weights = weights_ref[:, p * 256 : (p + 1) * 256]
        real = jnp.dot(fields_re[rows, :], weights, preferred_element_type=jnp.float32)
        imag = jnp.dot(fields_im[rows, :], weights, preferred_element_type=jnp.float32)
        for f in range(count):
            re = real[f * RING_ROWS : (f + 1) * RING_ROWS]
            im = imag[f * RING_ROWS : (f + 1) * RING_ROWS]
            term = eigen_row[0:1, f0 + f : f0 + f + 1] * (re * re + im * im)
            start = term if start is None else start + term
        return start

    parts = COARSE // 256
    for f in range(0, own, 2):
        pair_of_fields(far_ref, f, 0)
    near_copy.wait()
    for p in range(parts):
        for f in range(0, own, 2):
            if p == min(f * parts // own + (f > 0), parts - 1):
                pair_of_fields(near_ref, f, own)
        image_ref[:, p * 256 : (p + 1) * 256] = power(0, own, far_eigen, 0, p, None)
    for p in range(parts):
        at = slice(p * 256, (p + 1) * 256)
        image_ref[:, at] = power(own, own, near_eigen, 0, p, image_ref[:, at])


def dirichlet():
    distance = np.mod(np.arange(N)[None, :] - SPARSE * np.arange(32)[:, None], N)
    turn = np.pi * distance / N
    sine = np.where(distance == 0, 1.0, COARSE * np.sin(turn))
    kernel = np.where(distance % SPARSE == 0, distance == 0, np.sin(COARSE * turn) * np.cos(turn) / sine)
    kernel = kernel.astype(np.float32)
    tiles = kernel.reshape(32, 32, 128)
    sides = np.stack([np.concatenate([tiles[:, (8 - m) % 32, :64], tiles[:, (31 - m) % 32, 64:]], 1) for m in range(32)], 1)
    kernel = np.concatenate([kernel, sides.reshape(32, N)], 1)
    high = kernel.astype(ml_dtypes.bfloat16)
    low = (kernel - high.astype(np.float32)).astype(ml_dtypes.bfloat16)
    return high, low


def laplace(field):
    rows, cols = field.shape
    return (
        pltpu.roll(field, 1, 0)
        + pltpu.roll(field, rows - 1, 0)
        + pltpu.roll(field, 1, 1)
        + pltpu.roll(field, cols - 1, 1)
        - 4.0 * field
    )


def bake_kernel(
    own_ref, other_ref, high_ref, low_ref, rates, image_hbm, acid_hbm, parts, ring, image_ref, acid_ref, sems
):
    kern = lax.axis_index("kern")
    for p in range(COARSE // 256):
        block = jnp.bitwise_and(p - kern, COARSE // 256 - 1)
        at = pl.ds(pl.multiple_of(block * 256, 256), 256)
        value = own_ref[:, p * 256 : (p + 1) * 256] + other_ref[:, p * 256 : (p + 1) * 256]
        high = value.astype(jnp.bfloat16).astype(jnp.float32)
        parts[0 : 2 * RING_ROWS, at] = jnp.concatenate([high, value - high], 0).astype(jnp.bfloat16)

    def weights(ref, tiles, blocks):
        def tile(t, m):
            at = ((t - m) % 32 if t < 32 else t + m) * 128
            return ref[:, at : at + 128]

        rows = [
            jnp.concatenate([tile(t, m) for t in tiles], 1) for block in blocks for m in range(8 * block, 8 * block + 8)
        ]
        return jnp.concatenate(rows, 0)

    everywhere = range(COARSE // 256)
    for p in range(5):
        tiles = (2 * p, 2 * p + 1) if p < 4 else (32,)
        wide = jnp.dot(
            parts[0 : 2 * RING_ROWS, :], weights(high_ref, tiles, everywhere), preferred_element_type=jnp.float32
        )
        fine = sum(
            jnp.dot(
                parts[0:MXU_ROWS, block * 256 : (block + 1) * 256],
                weights(low_ref, tiles, (block,)),
                preferred_element_type=jnp.float32,
            )
            for block in NEAR_BLOCKS[p]
        )
        value = wide[0:RING_ROWS] + (wide[RING_ROWS : 2 * RING_ROWS] + fine[0:RING_ROWS])
        ring[:, p * 256 : p * 256 + value.shape[1]] = value

    dill_rate, acid_rate, quench_rate, react_rate, quench_start = (rates[0:1, i : i + 1] for i in range(5))
    aerial_image = ring[...] / FIELDS
    image_ref[...] = aerial_image[0:ROWS, 0:COLS]
    image_copy = pltpu.make_async_copy(image_ref, image_hbm, sems.at[0])
    image_copy.start()
    acid_field = 1.0 - jnp.exp((-4.0 * dill_rate) * aerial_image)
    acid_diffusion = acid_rate * (0.5 + 0.5 * acid_field)
    quencher = jnp.zeros_like(acid_field) + quench_start
    for bake_step in range(STEPS):
        reaction = (4.0 * react_rate) * acid_field * quencher
        new_acid = acid_field + acid_diffusion * laplace(acid_field) - reaction
        quencher = quencher + quench_rate * laplace(quencher) - reaction
        acid_field = new_acid
    acid_copies = []
    for p in range(2):
        at = slice(p * COLS // 2, (p + 1) * COLS // 2)
        acid_ref[:, at] = acid_field[0:ROWS, at]
        acid_copies.append(pltpu.make_async_copy(acid_ref.at[:, at], acid_hbm.at[:, at], sems.at[1 + p]))
        acid_copies[p].start()
    image_copy.wait()
    for copy in acid_copies:
        copy.wait()


VMEM = pl.BlockSpec(memory_space=pltpu.VMEM)
HBM = pl.BlockSpec(memory_space=pltpu.HBM)


def in_hbm(array):
    return pltpu.with_memory_space_constraint(array, pltpu.HBM)


def sum_everywhere(part, beside):
    plane, along_z = plane_groups(), z_groups()
    count, piece = len(plane[0]), part.shape[0] // len(plane[0])

    def exchange(blocks, groups):
        return lax.all_to_all(blocks, ALL, 0, 0, tiled=True, axis_index_groups=groups)

    def copies(block, many):
        return jnp.broadcast_to(block[None], (many,) + block.shape).reshape(-1, block.shape[1])

    some = jnp.sum(exchange(part, plane).reshape(count, piece, -1), 0)
    brought = exchange(copies(jnp.concatenate([some, beside], 0), len(along_z[0])), along_z)
    full = jnp.sum(brought.reshape(len(along_z[0]), 2 * piece, -1)[:, :piece], 0)
    return exchange(copies(full, count), plane), brought


def shards(layout, band_freqs, kernels, eigen_values, bake_rates):
    freqs = band_freqs.reshape(1, W)
    f32 = jnp.float32
    params = pltpu.CompilerParams(vmem_limit_bytes=24 * 2**20)
    far_kernels = lax.ppermute(kernels, ALL, from_next_z(1))
    own = kernels.shape[1]
    part, *tables, eigen_tile = pl.pallas_call(
        transform_kernel,
        out_shape=(
            jax.ShapeDtypeStruct((2 * W, W), f32),
            jax.ShapeDtypeStruct((2 * W, COARSE), jnp.bfloat16),
            jax.ShapeDtypeStruct((MXU_ROWS, 2 * W), jnp.bfloat16),
            jax.ShapeDtypeStruct((8, W), f32),
        ),
        in_specs=[HBM] * 3,
        out_specs=(VMEM,) * 4,
        scratch_shapes=[
            pltpu.VMEM((COLS // 4, 4 * W), jnp.bfloat16),
            pltpu.VMEM((ROWS, COLS), jnp.int32),
            pltpu.VMEM((1, W), jnp.int32),
            pltpu.VMEM((1, own), f32),
            pltpu.SemaphoreType.DMA((6,)),
        ],
        compiler_params=params,
        name="transform",
    )(in_hbm(layout), in_hbm(freqs), in_hbm(eigen_values.reshape(1, own)))
    spectrum, along_z = sum_everywhere(part, eigen_tile)
    own_image = pl.pallas_call(
        image_kernel,
        out_shape=jax.ShapeDtypeStruct((RING_ROWS, COARSE), f32),
        in_specs=[VMEM, HBM] + [VMEM] * 4,
        out_specs=VMEM,
        scratch_shapes=[
            pltpu.VMEM((2 * own * RING_ROWS, 2 * W), jnp.bfloat16),
            pltpu.VMEM((2 * own * RING_ROWS, 2 * W), jnp.bfloat16),
            pltpu.VMEM(kernels.shape, f32),
            pltpu.SemaphoreType.DMA,
        ],
        compiler_params=pltpu.CompilerParams(
            vmem_limit_bytes=24 * 2**20
        ),
        name="image",
    )(spectrum, in_hbm(kernels), far_kernels, *tables, along_z)
    across_cores = [(i, i + 64 if (i // 64) % 2 == 0 else i - 64) for i in range(256)]
    other_image = lax.ppermute(own_image, ALL, across_cores)
    block = jax.ShapeDtypeStruct((ROWS, COLS), f32)
    high, low = dirichlet()
    return pl.pallas_call(
        bake_kernel,
        out_shape=(block, block),
        in_specs=[VMEM] * 5,
        out_specs=(HBM, HBM),
        scratch_shapes=[
            pltpu.VMEM((2 * MXU_ROWS, COARSE), jnp.bfloat16),
            pltpu.VMEM((RING_ROWS, RING_COLS), f32),
            pltpu.VMEM((ROWS, COLS), f32),
            pltpu.VMEM((ROWS, COLS), f32),
            pltpu.SemaphoreType.DMA((3,)),
        ],
        compiler_params=pltpu.CompilerParams(
            vmem_limit_bytes=24 * 2**20
        ),
        name="bake",
    )(own_image, other_image, jnp.asarray(high), jnp.asarray(low), bake_rates.reshape(1, 5))


def solution(mesh):
    return jax.shard_map(
        shards,
        mesh=mesh,
        in_specs=(P("slab", "kern"), P(), P(None, "kern", None, None), P("kern"), P()),
        out_specs=(P("slab", "kern"), P("slab", "kern")),
        check_vma=False,
    )
```
